32 devices in a mesh: dp: 8 (over y, x, core), seq: 4 (over z).
Axes of the slice: x: 2, y: 2, z: 4, core: 2. Of those that a mesh axis runs over, the one named last changes fastest.
Arguments:
- block_input: bfloat16 [8, 1024, 2048], P('dp', 'seq'), may hold values from -6 to 6
- norm_gain: float32 [2048], replicated, may hold values from 0.5 to 1.5
- in_proj: bfloat16 [2048, 2816], P(('dp', 'seq')), may hold values from -0.125 to 0.125
- gate_proj: bfloat16 [2048, 2816], P(('dp', 'seq')), may hold values from -0.125 to 0.125
- conv_kernel: float32 [4, 2816], replicated, may hold values from -3 to 3
- conv_bias: float32 [2816], replicated, may hold values from -3 to 3
- recur_weight: bfloat16 [16, 176, 176], replicated, may hold values from -0.4375 to 0.4375
- recur_bias: float32 [2816], replicated, may hold values from -3 to 3
- input_weight: bfloat16 [16, 176, 176], replicated, may hold values from -0.4375 to 0.4375
- input_bias: float32 [2816], replicated, may hold values from -3 to 3
- decay_param: float32 [2816], replicated, may hold values from 5 to 10
- out_proj: bfloat16 [2816, 2048], P(('dp', 'seq')), may hold values from -0.3125 to 0.3125
- mlp_gain: float32 [2048], replicated, may hold values from 0.5 to 1.5
- mlp_gate: bfloat16 [2048, 6144], P(('dp', 'seq')), may hold values from -0.125 to 0.125
- mlp_up: bfloat16 [2048, 6144], P(('dp', 'seq')), may hold values from -0.125 to 0.125
- mlp_down: bfloat16 [6144, 2048], P(('dp', 'seq')), may hold values from -0.109375 to 0.109375
- out_grad: bfloat16 [8, 1024, 2048], P('dp', 'seq'), may hold values from -6 to 6
Outputs:
- block_output: bfloat16 [8, 1024, 2048], P('dp', 'seq')
- input_grad: float32 [8, 1024, 2048], P('dp', 'seq')
- grad_norm_gain: float32 [2048], replicated
- grad_in_proj: float32 [2048, 2816], P('seq', 'dp')
- grad_gate_proj: float32 [2048, 2816], P('seq', 'dp')
- grad_conv_kernel: float32 [4, 2816], replicated
- grad_conv_bias: float32 [2816], replicated
- grad_recur_weight: float32 [16, 176, 176], replicated
- grad_recur_bias: float32 [2816], replicated
- grad_input_weight: float32 [16, 176, 176], replicated
- grad_input_bias: float32 [2816], replicated
- grad_decay_param: float32 [2816], replicated
- grad_out_proj: float32 [2816, 2048], P('seq', 'dp')
- grad_mlp_gain: float32 [2048], replicated
- grad_mlp_gate: float32 [2048, 6144], P('seq', 'dp')
- grad_mlp_up: float32 [2048, 6144], P('seq', 'dp')
- grad_mlp_down: float32 [6144, 2048], P('seq', 'dp')
The draws below stay inside these ranges and needn't reach their ends.
All inputs are finite; a program needn't handle non-finite values.
Results may differ from the reference program's by a relative error of at most 0.015.
Values may be sent and summed in bfloat16 or wider, within the bound.
No kernel may reach another device: no remote copies, remote signals or barrier semaphores. Data moves between devices by JAX's collectives and lax.ppermute only.
A program may use at most 640 MiB of HBM per device.

```python
import jax
import jax.numpy as jnp
from jax import lax

D = 2048
HEADS = 16
HEAD = 176
F = 6144
CONV = 4
R = 2816
LENGTH = 1024
SEQS = 8


def block_levels(own_key, shape, split, least, largest):
    gain, own = 1.0, jax.random.fold_in(own_key, 6)
    for dim, parts in split:
        heights = jnp.exp(jax.random.uniform(jax.random.fold_in(own, dim), (parts,), jnp.float32, least / len(split), largest / len(split)))
        gain = gain * jnp.repeat(heights, shape[dim] // parts).reshape([-1 if axis == dim else 1 for axis in range(len(shape))])
    return gain


def gaussian(own_key, extent, spread, limit, pieces=(), kind=jnp.bfloat16):
    factor_of = block_levels(own_key, extent, pieces, -0.22, 0.18) if pieces else 1.0
    array = jax.random.normal(own_key, extent, jnp.float32) * spread * factor_of
    return jnp.minimum(jnp.maximum(array, -limit), limit).astype(kind)


def setup_inputs(seed: int = 0) -> dict:
    arg_keys = jax.random.split(jax.random.key(seed), 18)
    block_input = gaussian(arg_keys[0], (SEQS, LENGTH, D), 1.0, 6.0, ((0, 8), (1, 4)))
    norm_gain = jnp.clip(1.0 + 0.1 * jax.random.normal(arg_keys[1], (D,), jnp.float32), 0.5, 1.5)
    in_proj = gaussian(arg_keys[2], (D, R), D ** -0.5, 0.125, ((0, 32),))
    gate_proj = gaussian(arg_keys[3], (D, R), D ** -0.5, 0.125, ((0, 32),))
    conv_kernel = gaussian(arg_keys[4], (CONV, R), CONV ** -0.5, 3.0, (), jnp.float32)
    conv_bias = gaussian(arg_keys[5], (R,), 0.5, 3.0, (), jnp.float32)
    recur_weight = gaussian(arg_keys[6], (HEADS, HEAD, HEAD), HEAD ** -0.5, 0.4375)
    recur_bias = gaussian(arg_keys[7], (R,), 0.5, 3.0, (), jnp.float32)
    input_weight = gaussian(arg_keys[8], (HEADS, HEAD, HEAD), HEAD ** -0.5, 0.4375)
    input_bias = gaussian(arg_keys[9], (R,), 0.5, 3.0, (), jnp.float32)
    decay_param = jnp.clip(jax.random.uniform(arg_keys[10], (R,), jnp.float32, 5.0, 10.0), 5.0, 10.0)
    out_proj = gaussian(arg_keys[11], (R, D), (R // 8) ** -0.5, 0.3125, ((0, 32),))
    mlp_gain = jnp.clip(1.0 + 0.1 * jax.random.normal(arg_keys[12], (D,), jnp.float32), 0.5, 1.5)
    mlp_gate = gaussian(arg_keys[13], (D, F), D ** -0.5, 0.125, ((0, 32),))
    mlp_up = gaussian(arg_keys[14], (D, F), D ** -0.5, 0.125, ((0, 32),))
    mlp_down = gaussian(arg_keys[15], (F, D), (F // 2) ** -0.5, 0.109375, ((0, 32),))
    out_grad = gaussian(arg_keys[16], (SEQS, LENGTH, D), 1.0, 6.0, ((0, 8), (1, 4)))
    return dict(block_input=block_input, norm_gain=norm_gain, in_proj=in_proj, gate_proj=gate_proj, conv_kernel=conv_kernel, conv_bias=conv_bias, recur_weight=recur_weight, recur_bias=recur_bias, input_weight=input_weight, input_bias=input_bias, decay_param=decay_param, out_proj=out_proj, mlp_gain=mlp_gain, mlp_gate=mlp_gate, mlp_up=mlp_up, mlp_down=mlp_down, out_grad=out_grad)


EPSILON = 1e-06
HIGH = lax.Precision.HIGHEST

@jax.custom_vjp
def low(v):
    return lax.optimization_barrier(v.astype(jnp.bfloat16)).astype(jnp.float32)

@jax.custom_vjp
def low_back(v):
    return v

def low_keep(v):
    return (low(v), None)

def low_pass(kept, grad):
    return (grad,)

def back_keep(v):
    return (v, None)

def back_low(kept, grad):
    return (low(grad),)
low.defvjp(low_keep, low_pass)
low_back.defvjp(back_keep, back_low)

def matmul(left_side, right_side):
    return jnp.dot(left_side, right_side, precision=HIGH)

def scaled_norm(values, gain_vec):
    return values * lax.rsqrt(lax.optimization_barrier(jnp.mean(values * values, axis=-1, keepdims=True)) + EPSILON) * gain_vec

def recurrence_gates(recur_pre, input_pre, conv_out, decay_param):
    recur_gate = jax.nn.sigmoid(recur_pre)
    input_gate = jax.nn.sigmoid(input_pre)
    log_rate = -8.0 * recur_gate * jax.nn.softplus(-decay_param)
    decay_rate = jnp.exp(log_rate)
    driven = jnp.sqrt(-jnp.expm1(2.0 * log_rate)) * input_gate * conv_out
    return (decay_rate, driven)

def advance(state_now, inputs):
    decay_rate, driven = inputs
    state_now = decay_rate * state_now + driven
    return (state_now, state_now)

def residual_block(sequence, params):
    norm_gain, in_proj, gate_proj, conv_kernel, conv_bias, recur_weight, recur_bias, input_weight, input_bias, decay_param, out_proj, mlp_gain, mlp_gate, mlp_up, mlp_down = params
    length = sequence.shape[0]
    head_count = recur_weight.shape[0]
    head_size = recur_weight.shape[1]
    recur_width = in_proj.shape[1]
    tap_count = conv_kernel.shape[0]
    normed = low(scaled_norm(sequence, norm_gain))
    branch = low_back(matmul(normed, in_proj))
    gate_pre = low_back(matmul(normed, gate_proj))
    gate_act = jax.nn.gelu(gate_pre)
    padded = jnp.concatenate([jnp.zeros((tap_count - 1, recur_width), jnp.float32), branch], axis=0)
    conv_out = jnp.zeros((length, recur_width), jnp.float32) + conv_bias
    for tap_index in range(tap_count):
        begin = tap_count - 1 - tap_index
        conv_out = conv_out + conv_kernel[tap_index] * padded[begin:begin + length]
    heads_in = low(conv_out).reshape(length, head_count, head_size)
    recur_pre = low_back(jnp.einsum('thi,hij->thj', heads_in, recur_weight, precision=HIGH).reshape(length, recur_width) + recur_bias)
    input_pre = low_back(jnp.einsum('thi,hij->thj', heads_in, input_weight, precision=HIGH).reshape(length, recur_width) + input_bias)
    decay_rate, driven = recurrence_gates(recur_pre, input_pre, conv_out, decay_param)
    unused, states = lax.scan(advance, jnp.zeros((recur_width,), jnp.float32), (decay_rate, driven))
    mixed_out = low(states * gate_act)
    residual = sequence + low_back(matmul(mixed_out, out_proj))
    normed_two = low(scaled_norm(residual, mlp_gain))
    ffn_gate = low_back(matmul(normed_two, mlp_gate))
    ffn_up = low_back(matmul(normed_two, mlp_up))
    hidden = low(jax.nn.gelu(ffn_gate) * ffn_up)
    return residual + low_back(matmul(hidden, mlp_down))

def reference(block_input, norm_gain, in_proj, gate_proj, conv_kernel, conv_bias, recur_weight, recur_bias, input_weight, input_bias, decay_param, out_proj, mlp_gain, mlp_gate, mlp_up, mlp_down, out_grad):
    params = tuple((argument.astype(jnp.float32) for argument in (norm_gain, in_proj, gate_proj, conv_kernel, conv_bias, recur_weight, recur_bias, input_weight, input_bias, decay_param, out_proj, mlp_gain, mlp_gate, mlp_up, mlp_down)))

    def forward(inputs, weights):

        def one_sequence(sequence):
            return residual_block(sequence, weights)
        return lax.map(jax.checkpoint(one_sequence), inputs)
    outputs, pullback = jax.vjp(forward, block_input.astype(jnp.float32), params)
    input_grad, weight_grads = pullback(out_grad.astype(jnp.float32))
    return (outputs.astype(jnp.bfloat16), input_grad, weight_grads[0], weight_grads[1], weight_grads[2], weight_grads[3], weight_grads[4], weight_grads[5], weight_grads[6], weight_grads[7], weight_grads[8], weight_grads[9], weight_grads[10], weight_grads[11], weight_grads[12], weight_grads[13], weight_grads[14])
```

```python
import jax
import jax.numpy as jnp
from jax import lax
from jax.experimental import pallas as pl
from jax.experimental.pallas import tpu as pltpu
from jax.sharding import PartitionSpec as P

EPSILON = 1e-06
F32 = jnp.float32
BF16 = jnp.bfloat16
GELU_C = 0.7978845608028654
GELU_A = 0.044715
CHUNK = 32
VMEM_LIMIT = 48 << 20


def xor_send(value, axis, offset):
    count = lax.axis_size(axis)
    return lax.ppermute(value, axis, [(i, i ^ offset) for i in range(count)])


def shift_send(value, axis, steps):
    count = lax.axis_size(axis)
    first, last = max(0, -steps), min(count, count - steps)
    return lax.ppermute(value, axis, [(i, i + steps) for i in range(first, last)])


def gather_tokens(piece):
    count = lax.axis_size("dp")
    slots = {0: piece}
    if count == 8:
        half = piece.shape[0] // 2
        slots[2] = xor_send(piece, "dp", 2)
        slots[4] = xor_send(piece, "dp", 4)
        slots[1] = xor_send(piece, "dp", 1)
        top = xor_send(slots[4][:half], "dp", 2)
        bottom = xor_send(slots[2][half:], "dp", 4)
        slots[3] = xor_send(slots[2], "dp", 1)
        slots[5] = xor_send(slots[4], "dp", 1)
        slots[6] = jnp.concatenate([top, bottom], axis=0)
        slots[7] = jnp.concatenate(
            [xor_send(top, "dp", 1), xor_send(bottom, "dp", 1)], axis=0
        )
    else:
        for offset in range(2, count, 2):
            slots[offset] = xor_send(piece, "dp", offset)
        for offset in range(0, count, 2):
            slots[offset + 1] = xor_send(slots[offset], "dp", 1)
    return jnp.stack([slots[o] for o in range(count)], axis=0)


def scatter_tokens(partial):
    count = lax.axis_size("dp")
    order = [o for o in range(count - 2, -1, -2)]
    pair = {}
    for o in order:
        other = xor_send(partial[o ^ 1], "dp", 1)
        pair[o] = partial[o].astype(F32) + other.astype(F32)
    if count == 8:
        half = partial.shape[1] // 2
        far = pair[6].astype(BF16)
        via_x = xor_send(far[:half], "dp", 2)
        via_y = xor_send(far[half:], "dp", 4)
        x_top = xor_send(pair[2][:half].astype(BF16), "dp", 2)
        y_bottom = xor_send(pair[4][half:].astype(BF16), "dp", 4)
        x_bottom = xor_send((pair[2][half:] + via_y.astype(F32)).astype(BF16), "dp", 2)
        y_top = xor_send((pair[4][:half] + via_x.astype(F32)).astype(BF16), "dp", 4)
        return jnp.concatenate(
            [
                pair[0][:half] + x_top.astype(F32) + y_top.astype(F32),
                pair[0][half:] + x_bottom.astype(F32) + y_bottom.astype(F32),
            ],
            axis=0,
        )
    total = pair[0]
    for o in order[:-1]:
        total = total + xor_send(pair[o].astype(BF16), "dp", o).astype(F32)
    return total


def sum_over(value, axis):
    offset = 1
    total = value.astype(F32)
    while offset < lax.axis_size(axis):
        total = total + xor_send(total.astype(value.dtype), axis, offset).astype(F32)
        offset *= 2
    return total


def carry_in(decay, state, steps):
    count = lax.axis_size("seq")
    both = jnp.stack([decay, state], axis=0)
    moved = [shift_send(both, "seq", steps * k) for k in range(1, count)]
    carried = moved[-1][1]
    for item in reversed(moved[:-1]):
        carried = item[1] + item[0] * carried
    return carried


def place_rows(block):
    dp_count, seq_count = lax.axis_size("dp"), lax.axis_size("seq")
    ratio = dp_count // seq_count
    rows, cols = block.shape
    width = cols // ratio
    mine = lax.axis_index("dp")
    parts = block.reshape(rows, ratio, width)
    out = jnp.zeros((ratio, rows, width), block.dtype)
    for turn in range(ratio):
        perm = []
        for d in range(dp_count):
            for s in range(seq_count):
                j = (d + turn) % ratio
                perm.append((d * seq_count + s, (ratio * s + j) * seq_count + d // ratio))
        chosen = lax.dynamic_index_in_dim(parts, (mine + turn) % ratio, 1, keepdims=False)
        got = lax.ppermute(chosen, ("dp", "seq"), perm)
        out = lax.dynamic_update_index_in_dim(out, got, (mine - turn) % ratio, 0)
    return out.reshape(ratio * rows, width)


def scaled_norm(values, gain_vec):
    return (
        values * lax.rsqrt(jnp.mean(values * values, axis=-1, keepdims=True) + EPSILON) * gain_vec
    )


def gelu_pair(v):
    square = v * v
    t = jnp.tanh(GELU_C * (v + GELU_A * v * square))
    half = 0.5 * (1.0 + t)
    slope = half + 0.5 * v * (1.0 - t * t) * (GELU_C * (1.0 + 3.0 * GELU_A * square))
    return v * half, slope


def logistic(v):
    return 1.0 / (1.0 + jnp.exp(-v))


def one_minus_exp(x, exp_x):
    poly = jnp.full_like(x, 1.0 / 362880.0)
    for coef in (1 / 40320.0, 1 / 5040.0, 1 / 720.0, 1 / 120.0, 1 / 24.0, 1 / 6.0, 0.5, 1.0):
        poly = poly * x + coef
    return jnp.where(x > -0.35, -x * poly, 1.0 - exp_x)


def fwd_gates_kernel(
    branch_ref, prior_ref, taps_ref, vec_ref, wr_ref, wi_ref,
    bt_ref, conv_ref, r_ref, i_ref, rate_ref, m_ref, loc_ref, run_ref,
    halo, state, decay,
):
    chunk, slots, width = bt_ref.shape

    @pl.when(pl.program_id(0) == 0)
    def _():
        halo[...] = prior_ref[...]
        state[...] = jnp.zeros_like(state)
        decay[...] = jnp.ones_like(decay)

    bt = jnp.swapaxes(branch_ref[...], 0, 1)
    bt_ref[...] = bt
    lag = halo.shape[0]
    padded = jnp.concatenate([halo[...], bt], axis=0)
    halo[...] = padded[chunk : chunk + lag]
    conv = jnp.zeros_like(bt) + vec_ref[0, :]
    for k in range(lag + 1):
        conv = conv + taps_ref[k, :] * padded[lag - k : lag - k + chunk]
    conv_ref[...] = conv
    rows = conv.reshape(chunk * slots, width).astype(BF16)
    r = logistic(jnp.dot(rows, wr_ref[...], preferred_element_type=F32) + vec_ref[1, :])
    g = logistic(jnp.dot(rows, wi_ref[...], preferred_element_type=F32) + vec_ref[2, :])
    r = r.reshape(chunk, slots, width)
    g = g.reshape(chunk, slots, width)
    log_rate = r * vec_ref[3, :]
    rate = jnp.exp(log_rate)
    m = jnp.sqrt(one_minus_exp(2.0 * log_rate, rate * rate))
    r_ref[...] = r
    i_ref[...] = g
    rate_ref[...] = rate
    m_ref[...] = m
    driven = m * g * conv
    st, dc = state[...], decay[...]
    for t in range(chunk):
        st = rate[t] * st + driven[t]
        dc = rate[t] * dc
        loc_ref[t] = st
        run_ref[t] = dc
    state[...] = st
    decay[...] = dc


def fwd_mix_kernel(
    loc_ref, run_ref, carry_ref, gate_ref, mixed_ref, prev_ref, across_ref, last
):
    chunk = loc_ref.shape[0]

    @pl.when(pl.program_id(0) == 0)
    def _():
        last[...] = carry_ref[...]

    states = loc_ref[...] + run_ref[...] * carry_ref[...]
    prev_ref[...] = jnp.concatenate([last[...][None], states[: chunk - 1]], axis=0)
    last[...] = states[chunk - 1]
    across = jnp.swapaxes(states, 0, 1)
    across_ref[...] = across
    act, _ = gelu_pair(gate_ref[...])
    mixed_ref[...] = (across * act).astype(BF16)


def back_mix_kernel(
    gm_ref, gate_ref, across_ref, rate_ref, ggate_ref, gl_ref, tail_ref, end_ref, held, decay
):
    chunk = rate_ref.shape[0]

    @pl.when(pl.program_id(0) == 0)
    def _():
        held[...] = jnp.zeros_like(held)
        decay[...] = jnp.ones_like(decay)

    gm = gm_ref[...]
    act, slope = gelu_pair(gate_ref[...])
    ggate_ref[...] = (gm * across_ref[...] * slope).astype(BF16)
    gs = jnp.swapaxes(gm * act, 0, 1)
    rate = rate_ref[...]
    h, dc = held[...], decay[...]
    for t in reversed(range(chunk)):
        grad = gs[t] + h
        gl_ref[t] = grad
        tail_ref[t] = dc
        h = rate[t] * grad
        dc = rate[t] * dc
    held[...] = h
    decay[...] = dc
    end_ref[0] = dc
    end_ref[1] = h


def back_gates_kernel(
    gl_ref, tail_ref, rate_ref, m_ref, r_ref, i_ref, conv_ref, prev_ref, bt_ref,
    hin_ref, prior_ref, taps_ref, vec_ref, wr_ref, wi_ref,
    gbranch_ref, last_ref, head_ref, dwr_ref, dwi_ref, sums_ref,
    later,
):
    chunk, slots, width = rate_ref.shape
    lag = later.shape[0]
    step = pl.program_id(0)

    @pl.when(step == 0)
    def _():
        later[...] = jnp.zeros_like(later)
        dwr_ref[...] = jnp.zeros_like(dwr_ref)
        dwi_ref[...] = jnp.zeros_like(dwi_ref)
        sums_ref[...] = jnp.zeros_like(sums_ref)

    s = gl_ref[...] + tail_ref[...] * hin_ref[...]
    rate, m, r, g, conv = rate_ref[...], m_ref[...], r_ref[...], i_ref[...], conv_ref[...]
    sc = s * conv
    dpi = (sc * m * (g * (1.0 - g))).astype(BF16)
    dlog = s * prev_ref[...] * rate - sc * g * (rate * rate) / m
    dpr = (dlog * vec_ref[3, :] * (r * (1.0 - r))).astype(BF16)
    sums_ref[2] += jnp.sum(dlog * r, axis=0)
    sums_ref[0] += jnp.sum(dpr.astype(F32), axis=0)
    sums_ref[1] += jnp.sum(dpi.astype(F32), axis=0)
    rows = conv.reshape(chunk * slots, width).astype(BF16)
    dpr = dpr.astype(F32).reshape(chunk * slots, width).astype(BF16)
    dpi = dpi.astype(F32).reshape(chunk * slots, width).astype(BF16)
    over_rows = (((0,), (0,)), ((), ()))
    over_cols = (((1,), (1,)), ((), ()))
    dwr_ref[...] += lax.dot_general(rows, dpr, over_rows, preferred_element_type=F32)
    dwi_ref[...] += lax.dot_general(rows, dpi, over_rows, preferred_element_type=F32)
    gconv = lax.dot_general(dpr, wr_ref[...], over_cols, preferred_element_type=F32)
    gconv = gconv + lax.dot_general(dpi, wi_ref[...], over_cols, preferred_element_type=F32)
    gconv = gconv.reshape(chunk, slots, width) + s * m * g
    padded = jnp.concatenate([gconv, later[...]], axis=0)
    later[...] = gconv[:lag]
    head_ref[...] = gconv[:lag]
    sums_ref[3] += jnp.sum(gconv, axis=0)
    bt = bt_ref[...]
    gb = jnp.zeros_like(gconv)
    for k in range(lag + 1):
        shifted = padded[k : k + chunk]
        gb = gb + taps_ref[k, :] * shifted
        sums_ref[4 + k] += jnp.sum(bt * shifted, axis=0)

    @pl.when(step == 0)
    def _():
        last_ref[...] = gb[chunk - lag :]

    gbranch_ref[...] = jnp.swapaxes(gb, 0, 1).astype(BF16)

    @pl.when(step == pl.num_programs(0) - 1)
    def _():
        for k in range(1, lag + 1):
            for j in range(1, k + 1):
                sums_ref[4 + k] += prior_ref[lag - j] * gconv[k - j]


def specs_for(slots, length, width, backwards):
    count = length // CHUNK

    def at(c):
        return count - 1 - c if backwards else c

    time_major = pl.BlockSpec((CHUNK, slots, width), lambda c: (at(c), 0, 0))
    slot_major = pl.BlockSpec((slots, CHUNK, width), lambda c: (0, at(c), 0))
    return count, time_major, slot_major


def whole(*shape):
    return pl.BlockSpec(shape, lambda c: (0,) * len(shape))


def params():
    return pltpu.CompilerParams(
        dimension_semantics=("arbitrary",), vmem_limit_bytes=VMEM_LIMIT
    )


def cost(flops, size, trans):
    return pl.CostEstimate(flops=flops, bytes_accessed=size, transcendentals=trans)


def fwd_gates(branch, prior, taps, vecs, wr, wi):
    slots, length, width = branch.shape
    count, tm, sm = specs_for(slots, length, width, False)
    full = jax.ShapeDtypeStruct((length, slots, width), F32)
    n = slots * length * width
    return pl.pallas_call(
        fwd_gates_kernel,
        out_shape=(full,) * 8,
        grid=(count,),
        in_specs=[
            sm, whole(*prior.shape), whole(*taps.shape), whole(*vecs.shape),
            whole(*wr.shape), whole(*wi.shape),
        ],
        out_specs=(tm,) * 8,
        scratch_shapes=[
            pltpu.VMEM(prior.shape, F32),
            pltpu.VMEM((slots, width), F32),
            pltpu.VMEM((slots, width), F32),
        ],
        compiler_params=params(),
        cost_estimate=cost(4 * n * width + 60 * n, 36 * n, 5 * n),
        name="gates_forward",
    )(branch, prior, taps, vecs, wr, wi)


def fwd_mix(loc, run, carry, gate_pre):
    length, slots, width = loc.shape
    count, tm, sm = specs_for(slots, length, width, False)
    n = slots * length * width
    return pl.pallas_call(
        fwd_mix_kernel,
        out_shape=(
            jax.ShapeDtypeStruct((slots, length, width), BF16),
            jax.ShapeDtypeStruct((length, slots, width), F32),
            jax.ShapeDtypeStruct((slots, length, width), F32),
        ),
        grid=(count,),
        in_specs=[tm, tm, whole(slots, width), sm],
        out_specs=(sm, tm, sm),
        scratch_shapes=[pltpu.VMEM((slots, width), F32)],
        compiler_params=params(),
        cost_estimate=cost(20 * n, 22 * n, n),
        name="mix_forward",
    )(loc, run, carry, gate_pre)


def back_mix(gm, gate_pre, across, rate):
    length, slots, width = rate.shape
    count, tm, sm = specs_for(slots, length, width, True)
    n = slots * length * width
    return pl.pallas_call(
        back_mix_kernel,
        out_shape=(
            jax.ShapeDtypeStruct((slots, length, width), BF16),
            jax.ShapeDtypeStruct((length, slots, width), F32),
            jax.ShapeDtypeStruct((length, slots, width), F32),
            jax.ShapeDtypeStruct((2, slots, width), F32),
        ),
        grid=(count,),
        in_specs=[sm, sm, sm, tm],
        out_specs=(sm, tm, tm, whole(2, slots, width)),
        scratch_shapes=[pltpu.VMEM((slots, width), F32), pltpu.VMEM((slots, width), F32)],
        compiler_params=params(),
        cost_estimate=cost(30 * n, 26 * n, n),
        name="mix_backward",
    )(gm, gate_pre, across, rate)


def back_gates(kept, hin, prior, taps, vecs, wr, wi):
    length, slots, width = kept[0].shape
    lag = prior.shape[0]
    count, tm, sm = specs_for(slots, length, width, True)
    n = slots * length * width
    return pl.pallas_call(
        back_gates_kernel,
        out_shape=(
            jax.ShapeDtypeStruct((slots, length, width), BF16),
            jax.ShapeDtypeStruct((lag, slots, width), F32),
            jax.ShapeDtypeStruct((lag, slots, width), F32),
            jax.ShapeDtypeStruct((width, width), F32),
            jax.ShapeDtypeStruct((width, width), F32),
            jax.ShapeDtypeStruct((5 + lag, slots, width), F32),
        ),
        grid=(count,),
        in_specs=[tm] * 9
        + [
            whole(slots, width), whole(*prior.shape), whole(*taps.shape), whole(*vecs.shape),
            whole(*wr.shape), whole(*wi.shape),
        ],
        out_specs=(
            sm, whole(lag, slots, width), whole(lag, slots, width),
            whole(width, width), whole(width, width), whole(5 + lag, slots, width),
        ),
        scratch_shapes=[pltpu.VMEM((lag, slots, width), F32)],
        compiler_params=params(),
        cost_estimate=cost(8 * n * width + 80 * n, 40 * n, 2 * n),
        name="gates_backward",
    )(*kept, hin, prior, taps, vecs, wr, wi)


def rows_of(value):
    return value.reshape(-1, value.shape[-1])


def mm(left, right):
    return jnp.dot(left, right, preferred_element_type=F32)


def mm_back(grad_rows, weight):
    return lax.dot_general(grad_rows, weight, (((1,), (1,)), ((), ())), preferred_element_type=F32)


def mm_weight(left, right):
    return lax.dot_general(left, right, (((0,), (0,)), ((), ())), preferred_element_type=F32)


def after(value, *others):
    return lax.optimization_barrier((value,) + others)[0]


def local(
    block_input, norm_gain, in_proj, gate_proj, conv_kernel, conv_bias,
    recur_weight, recur_bias, input_weight, input_bias, decay_param,
    out_proj, mlp_gain, mlp_gate, mlp_up, mlp_down, out_grad,
):
    dp_count, seq_count = lax.axis_size("dp"), lax.axis_size("seq")
    mine = lax.axis_index("dp")
    model = block_input.shape[2]
    tokens = block_input.reshape(-1, model).astype(F32)
    length = tokens.shape[0]
    recur_width = in_proj.shape[1]
    own = recur_width // dp_count
    width = -(-own // 128) * 128
    hidden_width = mlp_gate.shape[1] // dp_count
    head = recur_weight.shape[1]
    own_heads = own // head
    lag = conv_kernel.shape[0] - 1

    def split_cols(weight, padded):
        part = weight.reshape(weight.shape[0], dp_count, -1)
        return jnp.pad(part, ((0, 0), (0, 0), (0, padded - part.shape[2])))

    def spread(pieces):
        joined = jnp.concatenate(pieces, axis=2)
        got = lax.all_to_all(joined, "dp", split_axis=1, concat_axis=1, tiled=False)
        return got

    def gather_rows(piece):
        full = lax.all_gather(piece, "seq", axis=0)
        return full.transpose(2, 0, 1, 3).reshape(-1, piece.shape[2])

    first = spread([split_cols(in_proj, width), split_cols(gate_proj, width)])
    second = spread([split_cols(mlp_gate, hidden_width), split_cols(mlp_up, hidden_width)])
    w_first = gather_rows(first)
    w_out = lax.all_gather(out_proj, "seq", axis=0, tiled=True)
    w_out = jnp.pad(w_out, ((0, width - own), (0, 0)))
    w_second = gather_rows(second)
    w_down = lax.all_gather(mlp_down, "seq", axis=0, tiled=True)

    def own_cols(value):
        part = lax.dynamic_slice_in_dim(value, mine * own, own, axis=value.ndim - 1)
        return jnp.pad(part, [(0, 0)] * (value.ndim - 1) + [(0, width - own)])

    taps = own_cols(conv_kernel)
    own_decay = own_cols(decay_param)
    vecs = jnp.stack(
        [
            own_cols(conv_bias), own_cols(recur_bias), own_cols(input_bias),
            -8.0 * jax.nn.softplus(-own_decay),
        ],
        axis=0,
    )

    def block_diagonal(weight):
        part = lax.dynamic_slice_in_dim(weight, mine * own_heads, own_heads, axis=0)
        full = jnp.zeros((width, width), weight.dtype)
        for h in range(own_heads):
            full = lax.dynamic_update_slice(full, part[h], (h * head, h * head))
        return full

    wr, wi = block_diagonal(recur_weight), block_diagonal(input_weight)

    normed = scaled_norm(tokens, norm_gain).astype(BF16)
    normed_all = gather_tokens(normed)
    grad_low = out_grad.reshape(length, model)
    grad_all = gather_tokens(after(grad_low, normed_all))
    both = mm(rows_of(normed_all), w_first)
    branch = both[:, :width].reshape(dp_count, length, width)
    gate_pre = both[:, width:].reshape(dp_count, length, width)
    prior = shift_send(jnp.swapaxes(branch[:, length - lag :], 0, 1), "seq", 1)
    bt, conv, r, g, rate, m, loc, run = fwd_gates(branch, prior, taps, vecs, wr, wi)
    carry = carry_in(run[length - 1], loc[length - 1], 1)
    mixed, prev, across = fwd_mix(loc, run, carry, gate_pre)
    partial = mm(rows_of(mixed), w_out).astype(BF16).reshape(dp_count, length, model)
    residual = tokens + scatter_tokens(partial)

    inv_two = lax.rsqrt(jnp.mean(residual * residual, axis=-1, keepdims=True) + EPSILON)
    normed_two = (residual * inv_two * mlp_gain).astype(BF16)
    normed_two_all = rows_of(gather_tokens(normed_two))
    ffn = mm(normed_two_all, w_second)
    act, slope = gelu_pair(ffn[:, :hidden_width])
    up = ffn[:, hidden_width:]
    hidden = (act * up).astype(BF16)
    grad_all = rows_of(grad_all)
    grad_down = mm_weight(hidden, grad_all).astype(BF16)
    down_cols = lax.psum_scatter(grad_down, "seq", scatter_dimension=1, tiled=True)
    grad_hidden = mm_back(grad_all, w_down)
    grad_ffn = jnp.concatenate(
        [(grad_hidden * up * slope).astype(BF16), (grad_hidden * act).astype(BF16)], axis=1
    )
    partial = mm_back(grad_ffn, w_second).astype(BF16).reshape(dp_count, length, model)
    grad_normed_two = scatter_tokens(partial)
    grad_second = mm_weight(normed_two_all, grad_ffn).astype(BF16)
    grad_second = lax.psum_scatter(grad_second, "seq", scatter_dimension=0, tiled=True)
    grad_mgate_w = grad_second[:, :hidden_width].astype(F32)
    grad_mup_w = grad_second[:, hidden_width:].astype(F32)

    def norm_back(grad, values, inv, gain):
        unit = values * inv
        scaled = grad * gain
        mean = jnp.mean(scaled * unit, axis=-1, keepdims=True)
        return inv * (scaled - unit * mean), jnp.sum(grad * unit, axis=0)

    grad_resid, mlp_gain_term = norm_back(grad_normed_two, residual, inv_two, mlp_gain)
    grad_residual = grad_resid + grad_low.astype(F32)

    grad_rec_all = gather_tokens(grad_residual.astype(BF16))
    out_partial = mm(hidden, w_down).astype(BF16).reshape(dp_count, length, model)
    result = residual + scatter_tokens(after(out_partial, grad_rec_all))
    block_output = result.astype(BF16).reshape(block_input.shape)
    grad_rec_all = rows_of(grad_rec_all)
    gm = mm_back(grad_rec_all, w_out).reshape(dp_count, length, width)
    grad_out = mm_weight(rows_of(mixed), grad_rec_all)[:own].astype(BF16)
    out_cols = lax.psum_scatter(grad_out, "seq", scatter_dimension=1, tiled=True)
    ggate, gl, tail, end = back_mix(gm, gate_pre, across, rate)
    hin = carry_in(end[0], end[1], -1)
    gbranch, last, head_rows, dwr, dwi, sums = back_gates(
        (gl, tail, rate, m, r, g, conv, prev, bt), hin, prior, taps, vecs, wr, wi
    )
    later = shift_send(head_rows, "seq", -1)
    fixed = []
    for j in range(lag):
        row = last[j]
        for k in range(lag - j, lag + 1):
            row = row + taps[k] * later[j + k - lag]
        fixed.append(row)
    fixed = jnp.stack(fixed, axis=1).astype(BF16)
    gbranch = lax.dynamic_update_slice(gbranch, fixed, (0, length - lag, 0))
    grad_first = jnp.concatenate([rows_of(gbranch), rows_of(ggate)], axis=1)
    partial = mm_back(grad_first, w_first).astype(BF16).reshape(dp_count, length, model)
    grad_normed = scatter_tokens(partial)
    grad_first_w = mm_weight(rows_of(normed_all), grad_first).astype(BF16)
    grad_first_w = lax.psum_scatter(grad_first_w, "seq", scatter_dimension=0, tiled=True)
    grad_in_w = grad_first_w[:, :own].astype(F32)
    grad_gate_w = grad_first_w[:, width : width + own].astype(F32)
    inv_one = lax.rsqrt(jnp.mean(tokens * tokens, axis=-1, keepdims=True) + EPSILON)
    grad_tokens, norm_gain_term = norm_back(grad_normed, tokens, inv_one, norm_gain)
    input_grad = (grad_tokens + grad_residual).reshape(block_input.shape)

    grad_down_w = place_rows(down_cols).astype(F32)
    grad_out_w = place_rows(out_cols).astype(F32)

    sums = jnp.sum(sums, axis=1)[:, :own]
    decay_scale = 8.0 * jax.nn.sigmoid(-own_decay[:own])
    sums = jnp.concatenate([sums[:2], (sums[2] * decay_scale)[None], sums[3:]], axis=0)
    sums = lax.all_gather(sum_over(sums, "seq"), "dp", axis=1, tiled=True)

    def diagonal(full):
        return jnp.stack(
            [full[h * head : (h + 1) * head, h * head : (h + 1) * head] for h in range(own_heads)]
        )

    blocks = jnp.stack([diagonal(dwr), diagonal(dwi)]).astype(BF16)
    blocks = sum_over(blocks, "seq").astype(BF16)
    blocks = lax.all_gather(blocks, "dp", axis=1, tiled=True).astype(F32)
    gains = sum_over(sum_over(jnp.stack([norm_gain_term, mlp_gain_term]), "dp"), "seq")
    return (
        block_output,
        input_grad,
        gains[0],
        grad_in_w,
        grad_gate_w,
        sums[4:],
        sums[3],
        blocks[0],
        sums[0],
        blocks[1],
        sums[1],
        sums[2],
        grad_out_w,
        gains[1],
        grad_mgate_w,
        grad_mup_w,
        grad_down_w,
    )


def solution(mesh):
    rows = P(("dp", "seq"), None)
    acts = P("dp", "seq", None)
    grads = P("seq", "dp")
    return jax.shard_map(
        local,
        mesh=mesh,
        in_specs=(
            acts, P(), rows, rows, P(), P(), P(), P(), P(), P(), P(), rows, P(), rows, rows, rows,
            acts,
        ),
        out_specs=(
            acts, acts, P(), grads, grads, P(), P(), P(), P(), P(), P(), P(), grads, P(), grads,
            grads, grads,
        ),
        check_vma=False,
    )
```

```python
import jax
import jax.numpy as jnp
from jax import lax
from jax.experimental import pallas as pl
from jax.experimental.pallas import tpu as pltpu
from jax.sharding import PartitionSpec as P

EPSILON = 1e-06
F32 = jnp.float32
BF16 = jnp.bfloat16
GELU_C = 0.7978845608028654
GELU_A = 0.044715
CHUNK = 32
VMEM_LIMIT = 48 << 20


def tie(*values):
    return lax.optimization_barrier(values)


def xor_send(value, axis, offset):
    count = lax.axis_size(axis)
    return lax.ppermute(value, axis, [(i, i ^ offset) for i in range(count)])


def shift_send(value, axis, steps):
    count = lax.axis_size(axis)
    first, last = max(0, -steps), min(count, count - steps)
    return lax.ppermute(value, axis, [(i, i + steps) for i in range(first, last)])


def gather_tokens(piece, *beside):
    chips = lax.axis_size("dp") // 2
    if chips == 4:
        half = piece.shape[0] // 2
        via_x = xor_send(piece, "dp", 2)
        via_y = xor_send(piece, "dp", 4)
        via_x, via_y, *beside = tie(via_x, via_y, *beside)
        top = xor_send(via_y[:half], "dp", 2)
        bottom = xor_send(via_x[half:], "dp", 4)
        return jnp.concatenate([piece, via_x, via_y, top, bottom], axis=0), *beside
    slots = [piece] + [xor_send(piece, "dp", 2 * o) for o in range(1, chips)]
    return jnp.concatenate(slots, axis=0), *beside


def scatter_tokens(partial, *beside):
    chips = lax.axis_size("dp") // 2
    wide = [partial[o].astype(F32) for o in range(chips)]
    if chips == 4:
        half = partial.shape[1] // 2
        via_x = xor_send(partial[3, :half], "dp", 2)
        via_y = xor_send(partial[3, half:], "dp", 4)
        x_top = xor_send(partial[1, :half], "dp", 2)
        y_bottom = xor_send(partial[2, half:], "dp", 4)
        via_x, via_y, *beside = tie(via_x, via_y, *beside)
        x_bottom = xor_send((wide[1][half:] + via_y.astype(F32)).astype(BF16), "dp", 2)
        y_top = xor_send((wide[2][:half] + via_x.astype(F32)).astype(BF16), "dp", 4)
        total = jnp.concatenate(
            [
                wide[0][:half] + x_top.astype(F32) + y_top.astype(F32),
                wide[0][half:] + x_bottom.astype(F32) + y_bottom.astype(F32),
            ],
            axis=0,
        )
        return total, *beside
    total = wide[0]
    for o in range(1, chips):
        total = total + xor_send(partial[o], "dp", 2 * o).astype(F32)
    return total, *beside


def join_cores(own_half, other_half):
    moved = xor_send(other_half.astype(BF16), "dp", 1)
    return (own_half + moved.astype(F32)).astype(BF16)


def gather_small(value):
    count = lax.axis_size("dp")
    evens = [value] + [xor_send(value, "dp", o) for o in range(2, count, 2)]
    evens = jnp.stack(evens, axis=0)
    both = jnp.stack([evens, xor_send(evens, "dp", 1)], axis=1)
    return both.reshape((count,) + value.shape)


def natural_order(slots):
    count, mine = slots.shape[0], lax.axis_index("dp")
    step = 1
    while step < count:
        pairs = slots.reshape((-1, 2, step) + slots.shape[1:])
        swapped = jnp.concatenate([pairs[:, 1:], pairs[:, :1]], axis=1)
        slots = jnp.where((mine // step) % 2 == 1, swapped, pairs).reshape(slots.shape)
        step *= 2
    return slots


def widen_blocks_kernel(mine_ref, slot_ref, out_ref):
    out_ref[...] = slot_ref[0].astype(F32)


def widen_blocks(slots):
    count, kinds, heads, rows, cols = slots.shape
    mine = lax.axis_index("dp").astype(jnp.int32).reshape(1)
    return pl.pallas_call(
        widen_blocks_kernel,
        out_shape=jax.ShapeDtypeStruct((kinds, count * heads, rows, cols), F32),
        grid_spec=pltpu.PrefetchScalarGridSpec(
            num_scalar_prefetch=1,
            grid=(count,),
            in_specs=[
                pl.BlockSpec((1, kinds, heads, rows, cols), lambda d, m: (d ^ m[0], 0, 0, 0, 0))
            ],
            out_specs=pl.BlockSpec((kinds, heads, rows, cols), lambda d, m: (0, d, 0, 0)),
        ),
        compiler_params=params(),
        name="widen_blocks",
    )(mine, slots)


def sum_over(value, axis):
    offset = 1
    total = value
    while offset < lax.axis_size(axis):
        moved = xor_send(total, axis, offset)
        total = (total.astype(F32) + moved.astype(F32)).astype(value.dtype)
        offset *= 2
    return total


def carry_in(decay, state, steps):
    count = lax.axis_size("seq")
    both = jnp.stack([decay, state], axis=0)
    moved = [shift_send(both, "seq", steps * k) for k in range(1, count)]
    carried = moved[-1][1]
    for item in reversed(moved[:-1]):
        carried = item[1] + item[0] * carried
    return carried


def quarter_shift():
    dp_count, seq_count = lax.axis_size("dp"), lax.axis_size("seq")
    mine = lax.axis_index("dp")
    ratio = dp_count // seq_count
    return shift_of(mine, ratio, seq_count)


def shift_of(d, ratio, seq_count):
    group = d // ratio
    flip = (d % 2) * (seq_count - 1)
    return group ^ flip


def place_rows(block):
    dp_count, seq_count = lax.axis_size("dp"), lax.axis_size("seq")
    ratio = dp_count // seq_count
    rows, cols = block.shape
    width = cols // ratio
    mine, seat = lax.axis_index("dp"), lax.axis_index("seq")
    parts = block.reshape(rows, ratio, width)
    out = jnp.zeros((ratio, rows, width), block.dtype)
    for turn in range(ratio):
        perm = []
        for d in range(dp_count):
            for s in range(seq_count):
                quarter = s ^ shift_of(d, ratio, seq_count)
                to = ratio * quarter + (d + turn) % ratio
                perm.append((d * seq_count + s, to * seq_count + d // ratio))
        chosen = lax.dynamic_index_in_dim(parts, (mine + turn) % ratio, 1, keepdims=False)
        got = lax.ppermute(chosen, ("dp", "seq"), perm)
        out = lax.dynamic_update_index_in_dim(out, got, (mine - turn) % ratio, 0)
    return out.reshape(ratio * rows, width)


def scaled_norm(values, gain_vec):
    return (
        values * lax.rsqrt(jnp.mean(values * values, axis=-1, keepdims=True) + EPSILON) * gain_vec
    )


def gelu_pair(v):
    square = v * v
    t = jnp.tanh(GELU_C * (v + GELU_A * v * square))
    half = 0.5 * (1.0 + t)
    slope = half + 0.5 * v * (1.0 - t * t) * (GELU_C * (1.0 + 3.0 * GELU_A * square))
    return v * half, slope


def logistic(v):
    return 1.0 / (1.0 + jnp.exp(-v))


def one_minus_exp(x, exp_x):
    poly = jnp.full_like(x, 1.0 / 362880.0)
    for coef in (1 / 40320.0, 1 / 5040.0, 1 / 720.0, 1 / 120.0, 1 / 24.0, 1 / 6.0, 0.5, 1.0):
        poly = poly * x + coef
    return jnp.where(x > -0.35, -x * poly, 1.0 - exp_x)


def half_mask(chunk, slots, width):
    return lax.broadcasted_iota(jnp.int32, (chunk, slots, width), 1) < slots // 2


def join_slots(own_ref, other_ref):
    return jnp.concatenate([own_ref[...], other_ref[...]], axis=0)


def fwd_gates_kernel(
    own_ref, other_ref, prior_ref, taps_ref, vec_ref, w_ref,
    bt_ref, conv_ref, r_ref, i_ref, rate_ref, m_ref, loc_ref, run_ref,
    halo, state, decay,
):
    chunk, slots, width = bt_ref.shape

    @pl.when(pl.program_id(0) == 0)
    def _():
        halo[...] = prior_ref[...]
        state[...] = jnp.zeros_like(state)
        decay[...] = jnp.ones_like(decay)

    bt = jnp.swapaxes(join_slots(own_ref, other_ref), 0, 1)
    bt_ref[...] = bt
    lag = halo.shape[0]
    padded = jnp.concatenate([halo[...], bt], axis=0)
    halo[...] = padded[chunk : chunk + lag]
    conv = jnp.zeros_like(bt) + vec_ref[0]
    for k in range(lag + 1):
        conv = conv + taps_ref[k] * padded[lag - k : lag - k + chunk]
    conv_ref[...] = conv
    rows = conv.reshape(chunk * slots, width).astype(BF16)
    mask = half_mask(chunk, slots, width)

    def gate(which):
        own = jnp.dot(rows, w_ref[2 * which], preferred_element_type=F32)
        other = jnp.dot(rows, w_ref[2 * which + 1], preferred_element_type=F32)
        shape = (chunk, slots, width)
        pre = jnp.where(mask, own.reshape(shape), other.reshape(shape))
        return logistic(pre + vec_ref[1 + which])

    r, g = gate(0), gate(1)
    log_rate = r * vec_ref[3]
    rate = jnp.exp(log_rate)
    m = jnp.sqrt(one_minus_exp(2.0 * log_rate, rate * rate))
    r_ref[...] = r
    i_ref[...] = g
    rate_ref[...] = rate
    m_ref[...] = m
    driven = m * g * conv
    st, dc = state[...], decay[...]
    for t in range(chunk):
        st = rate[t] * st + driven[t]
        dc = rate[t] * dc
        loc_ref[t] = st
        run_ref[t] = dc
    state[...] = st
    decay[...] = dc


def fwd_mix_kernel(
    loc_ref, run_ref, carry_ref, gate_own_ref, gate_other_ref,
    mixed_ref, prev_ref, across_ref, last,
):
    chunk, slots, width = loc_ref.shape

    @pl.when(pl.program_id(0) == 0)
    def _():
        last[...] = carry_ref[...]

    states = loc_ref[...] + run_ref[...] * carry_ref[...]
    prev_ref[...] = jnp.concatenate([last[...][None], states[: chunk - 1]], axis=0)
    last[...] = states[chunk - 1]
    across = jnp.swapaxes(states, 0, 1)
    across_ref[...] = across
    half = slots // 2
    own, _ = gelu_pair(gate_own_ref[...])
    other, _ = gelu_pair(gate_other_ref[...])
    mixed_ref[:, :, :width] = (across[:half] * own).astype(BF16)
    mixed_ref[:, :, width:] = (across[half:] * other).astype(BF16)


def back_mix_kernel(
    gm_own_ref, gm_other_ref, gate_own_ref, gate_other_ref, across_ref, rate_ref,
    ggate_ref, gl_ref, tail_ref, end_ref, held, decay,
):
    chunk, slots, width = rate_ref.shape

    @pl.when(pl.program_id(0) == 0)
    def _():
        held[...] = jnp.zeros_like(held)
        decay[...] = jnp.ones_like(decay)

    half = slots // 2
    gm = join_slots(gm_own_ref, gm_other_ref)
    act, slope = gelu_pair(join_slots(gate_own_ref, gate_other_ref))
    ggate = (gm * across_ref[...] * slope).astype(BF16)
    ggate_ref[:, :, :width] = ggate[:half]
    ggate_ref[:, :, width:] = ggate[half:]
    gs = jnp.swapaxes(gm * act, 0, 1)
    rate = rate_ref[...]
    h, dc = held[...], decay[...]
    for t in reversed(range(chunk)):
        grad = gs[t] + h
        gl_ref[t] = grad
        tail_ref[t] = dc
        h = rate[t] * grad
        dc = rate[t] * dc
    held[...] = h
    decay[...] = dc
    end_ref[0] = dc
    end_ref[1] = h


def back_gates_kernel(
    gl_ref, tail_ref, rate_ref, m_ref, r_ref, i_ref, conv_ref, prev_ref, bt_ref,
    hin_ref, prior_ref, taps_ref, vec_ref, w_ref,
    gbranch_ref, last_ref, head_ref, dw_ref, total_ref,
    later, sums_ref,
):
    chunk, slots, width = rate_ref.shape
    lag = later.shape[0]
    step = pl.program_id(0)

    @pl.when(step == 0)
    def _():
        later[...] = jnp.zeros_like(later)
        dw_ref[...] = jnp.zeros_like(dw_ref)
        sums_ref[...] = jnp.zeros_like(sums_ref)

    s = gl_ref[...] + tail_ref[...] * hin_ref[...]
    rate, m, r, g, conv = rate_ref[...], m_ref[...], r_ref[...], i_ref[...], conv_ref[...]
    sc = s * conv
    dpi = (sc * m * (g * (1.0 - g))).astype(BF16).astype(F32)
    dlog = s * prev_ref[...] * rate - sc * g * (rate * rate) / m
    dpr = (dlog * vec_ref[3] * (r * (1.0 - r))).astype(BF16).astype(F32)
    sums_ref[2] += jnp.sum(dlog * r, axis=0)
    sums_ref[0] += jnp.sum(dpr, axis=0)
    sums_ref[1] += jnp.sum(dpi, axis=0)
    mask = half_mask(chunk, slots, width)
    flat = (chunk * slots, width)
    rows_own = jnp.where(mask, conv, 0.0).reshape(flat).astype(BF16)
    rows_other = jnp.where(mask, 0.0, conv).reshape(flat).astype(BF16)
    dpr = dpr.reshape(flat).astype(BF16)
    dpi = dpi.reshape(flat).astype(BF16)
    over_rows = (((0,), (0,)), ((), ()))
    over_cols = (((1,), (1,)), ((), ()))
    dw_ref[0] += lax.dot_general(rows_own, dpr, over_rows, preferred_element_type=F32)
    dw_ref[1] += lax.dot_general(rows_other, dpr, over_rows, preferred_element_type=F32)
    dw_ref[2] += lax.dot_general(rows_own, dpi, over_rows, preferred_element_type=F32)
    dw_ref[3] += lax.dot_general(rows_other, dpi, over_rows, preferred_element_type=F32)

    def through(which):
        part = lax.dot_general(dpr, w_ref[which], over_cols, preferred_element_type=F32)
        part += lax.dot_general(dpi, w_ref[2 + which], over_cols, preferred_element_type=F32)
        return part.reshape(chunk, slots, width)

    gconv = jnp.where(mask, through(0), through(1)) + s * m * g
    padded = jnp.concatenate([gconv, later[...]], axis=0)
    later[...] = gconv[:lag]
    head_ref[...] = gconv[:lag]
    sums_ref[3] += jnp.sum(gconv, axis=0)
    bt = bt_ref[...]
    gb = jnp.zeros_like(gconv)
    for k in range(lag + 1):
        shifted = padded[k : k + chunk]
        gb = gb + taps_ref[k] * shifted
        sums_ref[4 + k] += jnp.sum(bt * shifted, axis=0)

    @pl.when(step == 0)
    def _():
        last_ref[...] = gb[chunk - lag :]

    across = jnp.swapaxes(gb, 0, 1).astype(BF16)
    gbranch_ref[:, :, :width] = across[: slots // 2]
    gbranch_ref[:, :, width:] = across[slots // 2 :]

    @pl.when(step == pl.num_programs(0) - 1)
    def _():
        for k in range(1, lag + 1):
            for j in range(1, k + 1):
                sums_ref[4 + k] += prior_ref[lag - j] * gconv[k - j]
        half = slots // 2
        for kind in range(total_ref.shape[1]):
            total_ref[0, kind] = jnp.sum(sums_ref[kind, :half], axis=0)
            total_ref[1, kind] = jnp.sum(sums_ref[kind, half:], axis=0)


def specs_for(slots, length, width, backwards):
    count = length // CHUNK

    def at(c):
        return count - 1 - c if backwards else c

    time_major = pl.BlockSpec((CHUNK, slots, width), lambda c: (at(c), 0, 0))

    def columns(j, times=1, halves=2):
        return pl.BlockSpec((slots // halves, CHUNK, times * width), lambda c: (0, at(c), j))

    return count, time_major, columns


def whole(*shape):
    return pl.BlockSpec(shape, lambda c: (0,) * len(shape))


def params():
    return pltpu.CompilerParams(
        dimension_semantics=("arbitrary",), vmem_limit_bytes=VMEM_LIMIT
    )


def cost(flops, size, trans):
    return pl.CostEstimate(flops=flops, bytes_accessed=size, transcendentals=trans)


def fwd_gates(both, prior, taps, vecs, w):
    length = both.shape[1]
    lag, slots, width = prior.shape
    count, tm, cols = specs_for(slots, length, width, False)
    full = jax.ShapeDtypeStruct((length, slots, width), F32)
    n = slots * length * width
    return pl.pallas_call(
        fwd_gates_kernel,
        out_shape=(full,) * 8,
        grid=(count,),
        in_specs=[
            cols(0), cols(2), whole(*prior.shape), whole(*taps.shape), whole(*vecs.shape),
            whole(*w.shape),
        ],
        out_specs=(tm,) * 8,
        scratch_shapes=[
            pltpu.VMEM(prior.shape, F32),
            pltpu.VMEM((slots, width), F32),
            pltpu.VMEM((slots, width), F32),
        ],
        compiler_params=params(),
        cost_estimate=cost(n, 58 * n, n),
        name="gates_forward",
    )(both, both, prior, taps, vecs, w)


def fwd_mix(loc, run, carry, both):
    length, slots, width = loc.shape
    count, tm, cols = specs_for(slots, length, width, False)
    n = slots * length * width
    return pl.pallas_call(
        fwd_mix_kernel,
        out_shape=(
            jax.ShapeDtypeStruct((slots // 2, length, 2 * width), BF16),
            jax.ShapeDtypeStruct((length, slots, width), F32),
            jax.ShapeDtypeStruct((slots, length, width), F32),
        ),
        grid=(count,),
        in_specs=[tm, tm, whole(slots, width), cols(1), cols(3)],
        out_specs=(cols(0, 2), tm, cols(0, 1, 1)),
        scratch_shapes=[pltpu.VMEM((slots, width), F32)],
        compiler_params=params(),
        cost_estimate=cost(n, 36 * n, n),
        name="mix_forward",
    )(loc, run, carry, both, both)


def back_mix(gm, both, across, rate):
    length, slots, width = rate.shape
    count, tm, cols = specs_for(slots, length, width, True)
    n = slots * length * width
    return pl.pallas_call(
        back_mix_kernel,
        out_shape=(
            jax.ShapeDtypeStruct((slots // 2, length, 2 * width), BF16),
            jax.ShapeDtypeStruct((length, slots, width), F32),
            jax.ShapeDtypeStruct((length, slots, width), F32),
            jax.ShapeDtypeStruct((2, slots, width), F32),
        ),
        grid=(count,),
        in_specs=[cols(0), cols(1), cols(1), cols(3), cols(0, 1, 1), tm],
        out_specs=(cols(0, 2), tm, tm, whole(2, slots, width)),
        scratch_shapes=[pltpu.VMEM((slots, width), F32), pltpu.VMEM((slots, width), F32)],
        compiler_params=params(),
        cost_estimate=cost(n, 44 * n, n),
        name="mix_backward",
    )(gm, gm, both, both, across, rate)


def back_gates(kept, hin, prior, taps, vecs, w):
    length, slots, width = kept[0].shape
    lag = prior.shape[0]
    count, tm, cols = specs_for(slots, length, width, True)
    n = slots * length * width
    return pl.pallas_call(
        back_gates_kernel,
        out_shape=(
            jax.ShapeDtypeStruct((slots // 2, length, 2 * width), BF16),
            jax.ShapeDtypeStruct((lag, slots, width), F32),
            jax.ShapeDtypeStruct((lag, slots, width), F32),
            jax.ShapeDtypeStruct(w.shape, F32),
            jax.ShapeDtypeStruct((2, 5 + lag, width), F32),
        ),
        grid=(count,),
        in_specs=[tm] * 9
        + [
            whole(slots, width), whole(*prior.shape), whole(*taps.shape), whole(*vecs.shape),
            whole(*w.shape),
        ],
        out_specs=(
            cols(0, 2), whole(lag, slots, width), whole(lag, slots, width),
            whole(*w.shape), whole(2, 5 + lag, width),
        ),
        scratch_shapes=[
            pltpu.VMEM((lag, slots, width), F32),
            pltpu.VMEM((5 + lag, slots, width), F32),
        ],
        compiler_params=params(),
        cost_estimate=cost(n, 76 * n, n),
        name="gates_backward",
    )(*kept, hin, prior, taps, vecs, w)


def tile_of(hidden_width):
    return 256 if hidden_width % 256 == 0 else 128


def row_blocks(rows):
    step = 256 if rows % 256 == 0 else rows
    return [slice(at, at + step) for at in range(0, rows, step)]


def mlp_forward_kernel(x_ref, w_ref, hidden_ref, kept_ref):
    tile = hidden_ref.shape[1]
    weight = jnp.swapaxes(w_ref[...], 0, 1).reshape(x_ref.shape[1], 2 * tile)
    for rows in row_blocks(x_ref.shape[0]):
        ffn = jnp.dot(x_ref[rows, :], weight, preferred_element_type=F32)
        act, slope = gelu_pair(ffn[:, :tile])
        up = ffn[:, tile:]
        hidden_ref[rows, :] = (act * up).astype(BF16)
        kept_ref[rows, :tile] = (slope * up).astype(BF16)
        kept_ref[rows, tile:] = act.astype(BF16)


def mlp_forward(x, weight):
    rows, model = x.shape
    hidden_width = weight.shape[3] // 2
    tile = tile_of(hidden_width)
    return pl.pallas_call(
        mlp_forward_kernel,
        out_shape=(
            jax.ShapeDtypeStruct((rows, hidden_width), BF16),
            jax.ShapeDtypeStruct((rows, 2 * hidden_width), BF16),
        ),
        grid=(hidden_width // tile,),
        in_specs=[
            pl.BlockSpec((rows, model), lambda j: (0, 0), pipeline_mode=pl.Buffered(1)),
            pl.BlockSpec(weight.shape[:3] + (2 * tile,), lambda j: (0, 0, 0, j)),
        ],
        out_specs=(
            pl.BlockSpec((rows, tile), lambda j: (0, j)),
            pl.BlockSpec((rows, 2 * tile), lambda j: (0, j)),
        ),
        compiler_params=params(),
        cost_estimate=cost(7 * rows * hidden_width * model, rows * model, 0),
        name="mlp_forward",
    )(x, weight)


OVER_COLS = (((1,), (1,)), ((), ()))


def hidden_backward_kernel(g_ref, down0_ref, down1_ref, kept0_ref, kept1_ref, ffn0_ref, ffn1_ref):
    step = pl.program_id(0)
    tile = down0_ref.shape[0]

    def half(down_ref, kept_ref, ffn_ref):
        for rows in row_blocks(g_ref.shape[0]):
            grad = lax.dot_general(
                g_ref[rows, :], down_ref[...], OVER_COLS, preferred_element_type=F32
            )
            ffn_ref[rows, :tile] = (grad * kept_ref[rows, :tile].astype(F32)).astype(BF16)
            ffn_ref[rows, tile:] = (grad * kept_ref[rows, tile:].astype(F32)).astype(BF16)

    @pl.when(step < pl.num_programs(0) // 2)
    def _():
        half(down1_ref, kept1_ref, ffn1_ref)

    @pl.when(step >= pl.num_programs(0) // 2)
    def _():
        half(down0_ref, kept0_ref, ffn0_ref)


def hidden_backward(grad, down, kept):
    rows, model = grad.shape
    hidden_width = down[0].shape[0]
    tile = tile_of(hidden_width)
    half = hidden_width // tile

    def own(j):
        return jnp.maximum(j - half, 0)

    def other(j):
        return jnp.minimum(j, half - 1)

    full = jax.ShapeDtypeStruct((rows, 2 * hidden_width), BF16)
    return pl.pallas_call(
        hidden_backward_kernel,
        out_shape=(full, full),
        grid=(2 * half,),
        in_specs=[
            pl.BlockSpec((rows, model), lambda j: (0, 0), pipeline_mode=pl.Buffered(1)),
            pl.BlockSpec((tile, model), lambda j: (own(j), 0)),
            pl.BlockSpec((tile, model), lambda j: (other(j), 0)),
            pl.BlockSpec((rows, 2 * tile), lambda j: (0, own(j))),
            pl.BlockSpec((rows, 2 * tile), lambda j: (0, other(j))),
        ],
        out_specs=(
            pl.BlockSpec((rows, 2 * tile), lambda j: (0, own(j))),
            pl.BlockSpec((rows, 2 * tile), lambda j: (0, other(j))),
        ),
        compiler_params=params(),
        cost_estimate=cost(7 * rows * hidden_width * model, rows * model, 0),
        name="hidden_backward",
    )(grad, *down, *kept)


def normed_backward_kernel(ffn0_ref, ffn1_ref, w0_ref, w1_ref, out_ref):
    width = ffn0_ref.shape[1]
    for rows in row_blocks(ffn0_ref.shape[0]):
        total = None
        for ffn_ref, w_ref in ((ffn0_ref, w0_ref), (ffn1_ref, w1_ref)):
            part = lax.dot_general(
                ffn_ref[rows, :],
                w_ref[...].reshape(out_ref.shape[1], width),
                OVER_COLS,
                preferred_element_type=F32,
            )
            total = part if total is None else total + part
        out_ref[rows, :] = total.astype(BF16)


def normed_backward(ffn, weight):
    rows, width = ffn[0].shape
    seq_count, dp_count, shard, _ = weight[0].shape
    cols = seq_count * shard
    kept = pl.BlockSpec((rows, width), lambda j: (0, 0), pipeline_mode=pl.Buffered(1))
    block = pl.BlockSpec((seq_count, 1, shard, width), lambda j: (0, j, 0, 0))
    return pl.pallas_call(
        normed_backward_kernel,
        out_shape=jax.ShapeDtypeStruct((rows, cols * dp_count), BF16),
        grid=(dp_count,),
        in_specs=[kept, kept, block, block],
        out_specs=pl.BlockSpec((rows, cols), lambda j: (0, j)),
        compiler_params=params(),
        cost_estimate=cost(7 * rows * width * cols * dp_count, rows * width, 0),
        name="normed_backward",
    )(*ffn, *weight)


def unpack_down_kernel(packed_ref, out_ref):
    out_ref[...] = jnp.concatenate(
        [packed_ref[0, block] for block in range(packed_ref.shape[1])], axis=1
    )


def unpack_down(packed, first_column, rows):
    seq_count, dp_count, shard, _ = packed.shape
    lay = rows // (seq_count * shard)
    part = (packed.shape[3] - first_column) // lay
    begin = first_column // part
    return pl.pallas_call(
        unpack_down_kernel,
        out_shape=jax.ShapeDtypeStruct((rows, dp_count * part), packed.dtype),
        grid=(seq_count, lay),
        in_specs=[
            pl.BlockSpec((1, dp_count, shard, part), lambda s, k: (s, 0, 0, begin + k))
        ],
        out_specs=pl.BlockSpec((shard, dp_count * part), lambda s, k: (s * lay + k, 0)),
        compiler_params=pltpu.CompilerParams(
            dimension_semantics=("arbitrary", "arbitrary"), vmem_limit_bytes=VMEM_LIMIT
        ),
        cost_estimate=cost(0, 2 * rows * dp_count * part * 2, 0),
        name="unpack_down",
    )(packed)


def rows_of(value):
    return value.reshape(-1, value.shape[-1])


def mm(left, right):
    return jnp.dot(left, right, preferred_element_type=F32)


def mm_back(grad_rows, weight):
    return lax.dot_general(grad_rows, weight, (((1,), (1,)), ((), ())), preferred_element_type=F32)


def weight_kernel(left_ref, right_ref, *refs):
    out_ref = refs[-1]
    product = lax.dot_general(
        left_ref[...], right_ref[...], (((0,), (0,)), ((), ())), preferred_element_type=F32
    )
    if len(refs) == 2:
        product = product + refs[0][...].astype(F32)
    out_ref[...] = product.astype(BF16)


def mm_weight(left, right, *added):
    depth, rows = left.shape
    cols = right.shape[1]
    tile = 256 if rows % 256 == 0 else 128
    block = pl.BlockSpec((tile, cols), lambda i: (i, 0))
    return pl.pallas_call(
        weight_kernel,
        out_shape=jax.ShapeDtypeStruct((rows, cols), BF16),
        grid=(rows // tile,),
        in_specs=[
            pl.BlockSpec((depth, tile), lambda i: (0, i)),
            pl.BlockSpec((depth, cols), lambda i: (0, 0), pipeline_mode=pl.Buffered(1)),
        ]
        + [block] * len(added),
        out_specs=block,
        compiler_params=params(),
        cost_estimate=cost(3 * rows * cols * depth, rows * cols, 0),
        name="weight_gradient",
    )(left, right, *added)


def weight_rows_kernel(shift_ref, left_ref, right_ref, added_ref, *refs):
    out_ref = refs[-1]
    product = lax.dot_general(
        left_ref[...], right_ref[...], (((0,), (0,)), ((), ())), preferred_element_type=F32
    )
    product = (product + added_ref[...].astype(F32)).astype(BF16)
    count, _, cols = out_ref.shape
    for quarter in range(count):
        out_ref[quarter ^ shift_ref[0]] = product[:, quarter * cols : (quarter + 1) * cols]


def weight_rows(left, right, added, total_rows, first_row, into=None):
    depth, rows = left.shape
    cols = right.shape[1]
    count = lax.axis_size("seq")
    tile = 128
    shift = quarter_shift().astype(jnp.int32).reshape(1)
    begin = first_row // tile
    more = [] if into is None else [into]
    return pl.pallas_call(
        weight_rows_kernel,
        out_shape=jax.ShapeDtypeStruct((count, total_rows, cols // count), BF16),
        grid_spec=pltpu.PrefetchScalarGridSpec(
            num_scalar_prefetch=1,
            grid=(rows // tile,),
            in_specs=[
                pl.BlockSpec((depth, tile), lambda i, s: (0, i)),
                pl.BlockSpec((depth, cols), lambda i, s: (0, 0), pipeline_mode=pl.Buffered(1)),
                pl.BlockSpec((tile, cols), lambda i, s: (i, 0)),
            ]
            + [pl.BlockSpec(memory_space=pl.ANY)] * len(more),
            out_specs=pl.BlockSpec(
                (count, tile, cols // count), lambda i, s: (0, begin + i, 0)
            ),
        ),
        input_output_aliases={4: 0} if more else {},
        compiler_params=params(),
        cost_estimate=cost(3 * rows * cols * depth, rows * cols, 0),
        name="weight_rows",
    )(shift, left, right, added, *more)


def local(
    block_input, norm_gain, in_proj, gate_proj, conv_kernel, conv_bias,
    recur_weight, recur_bias, input_weight, input_bias, decay_param,
    out_proj, mlp_gain, mlp_gate, mlp_up, mlp_down, out_grad,
):
    dp_count, seq_count = lax.axis_size("dp"), lax.axis_size("seq")
    mine = lax.axis_index("dp")
    model = block_input.shape[2]
    tokens = block_input.reshape(-1, model).astype(F32)
    length = tokens.shape[0]
    recur_width = in_proj.shape[1]
    own = recur_width // dp_count
    width = -(-own // 128) * 128
    hidden_width = mlp_gate.shape[1] // dp_count
    head = recur_weight.shape[1]
    own_heads = own // head
    lag = conv_kernel.shape[0] - 1

    chips = dp_count // 2

    shard = in_proj.shape[0]

    def split_cols(weight, padded):
        part = jnp.swapaxes(weight.reshape(shard, dp_count, -1), 0, 1)
        return jnp.pad(part, ((0, 0), (0, 0), (0, padded - part.shape[2])))

    def spread(joined):
        return lax.all_to_all(joined, "dp", split_axis=0, concat_axis=0, tiled=True)

    def natural_rows(full):
        return full.transpose(1, 0, 2, 3).reshape(-1, full.shape[3])

    def partner(value):
        return xor_send(value, "dp", 1)

    w_out = lax.all_gather(out_proj, "seq", axis=0, tiled=True)
    first = jnp.concatenate([split_cols(in_proj, width), split_cols(gate_proj, width)], axis=2)
    first = spread(first)
    first = lax.all_gather(first, "seq", axis=0)
    def per_slot(value):
        rows = []
        for index in (mine, mine ^ 1):
            part = lax.dynamic_slice_in_dim(value, index * own, own, axis=value.ndim - 1)
            rows.append(jnp.pad(part, [(0, 0)] * (value.ndim - 1) + [(0, width - own)]))
        return jnp.repeat(jnp.stack(rows, axis=-2), chips, axis=-2)

    taps = per_slot(conv_kernel)
    vecs = per_slot(jnp.stack([conv_bias, recur_bias, input_bias, decay_param]))
    vecs = jnp.concatenate([vecs[:3], -8.0 * jax.nn.softplus(-vecs[3:])], axis=0)

    def block_diagonal(weight, index):
        part = lax.dynamic_slice_in_dim(weight, index * own_heads, own_heads, axis=0)
        rows = [
            jnp.pad(part[h], ((0, 0), (h * head, width - (h + 1) * head)))
            for h in range(own_heads)
        ]
        return jnp.pad(jnp.concatenate(rows, axis=0), ((0, width - own), (0, 0)))

    w_gates = jnp.stack(
        [block_diagonal(w, i) for w in (recur_weight, input_weight) for i in (mine, mine ^ 1)]
    )

    normed = scaled_norm(tokens, norm_gain).astype(BF16)
    normed_all, w_out = gather_tokens(normed, w_out)
    w_out = jnp.pad(w_out, ((0, width - own), (0, 0)))
    w_out = jnp.concatenate([w_out, partner(w_out)], axis=0)
    tile = tile_of(hidden_width)

    def by_tile(weight):
        return weight.reshape(shard, dp_count, hidden_width // tile, tile)

    second = jnp.concatenate([by_tile(mlp_gate), by_tile(mlp_up)], axis=3)
    second = jnp.swapaxes(second.reshape(shard, dp_count, 2 * hidden_width), 0, 1)
    lay = mlp_down.shape[0] // shard
    part = model // dp_count
    down = mlp_down.reshape(lay, shard, dp_count, part).transpose(2, 1, 0, 3)
    down = down.reshape(dp_count, shard, lay * part)
    second, down, normed_all = tie(second, down, normed_all)
    grad_low, second, first = tie(out_grad.reshape(length, model), spread(second), first)
    second = lax.all_gather(jnp.concatenate([second, down], axis=2), "seq", axis=0)

    w_first = natural_rows(first)
    w_first = jnp.concatenate([w_first, partner(w_first)], axis=1)

    both = mm(normed_all, w_first)
    grad_all, both = gather_tokens(grad_low, both)
    both = both.reshape(chips, length, 4 * width)
    ends = both[:, length - lag :]
    ends = jnp.concatenate([ends[:, :, :width], ends[:, :, 2 * width : 3 * width]], axis=0)
    prior = shift_send(jnp.swapaxes(ends, 0, 1), "seq", 1)
    bt, conv, r, g, rate, m, loc, run = fwd_gates(both, prior, taps, vecs, w_gates)
    carry = carry_in(run[length - 1], loc[length - 1], 1)
    mixed, prev, across = fwd_mix(loc, run, carry, both)
    mixed = rows_of(mixed)
    partial, grad_all = tie(mm(mixed, w_out).astype(BF16), grad_all)
    (total,) = scatter_tokens(partial.reshape(chips, length, model))
    residual = tokens + total

    inv_two = lax.rsqrt(jnp.mean(residual * residual, axis=-1, keepdims=True) + EPSILON)
    normed_two = (residual * inv_two * mlp_gain).astype(BF16)
    (normed_two_all,) = gather_tokens(normed_two)
    normed_two_all, second = tie(normed_two_all, second)
    w_second = second[:, :, :, : 2 * hidden_width]
    w_second = (w_second, partner(w_second))
    w_down = unpack_down(second, 2 * hidden_width, hidden_width)
    w_down = (w_down, partner(w_down))
    hidden, kept = zip(*[mlp_forward(normed_two_all, weight) for weight in w_second])
    hidden = list(hidden)
    grad_ffn = list(hidden_backward(grad_all, w_down, kept))
    moved = mm_weight(normed_two_all, grad_ffn[1])
    grad_ffn[0], moved = tie(grad_ffn[0], moved)
    moved = xor_send(moved, "dp", 1)
    partial = normed_backward(grad_ffn, w_second)
    partial, grad_ffn[0], normed_two_all = tie(partial, grad_ffn[0], normed_two_all)
    grad_normed_two, moved, grad_ffn[0] = scatter_tokens(
        partial.reshape(chips, length, model), moved, grad_ffn[0]
    )
    grad_second = mm_weight(normed_two_all, grad_ffn[0], moved)
    grad_normed_two, grad_second = tie(grad_normed_two, grad_second)
    grad_second_rows = lax.psum_scatter(grad_second, "seq", scatter_dimension=0, tiled=True)

    def norm_back(grad, values, inv, gain):
        unit = values * inv
        scaled = grad * gain
        mean = jnp.mean(scaled * unit, axis=-1, keepdims=True)
        return inv * (scaled - unit * mean), unit

    grad_resid, unit_two = norm_back(grad_normed_two, residual, inv_two, mlp_gain)
    mlp_gain_term = jnp.sum(grad_normed_two * unit_two, axis=0)
    grad_residual = grad_resid + grad_low.astype(F32)

    grad_rec, hidden[0], hidden[1] = tie(grad_residual.astype(BF16), *hidden)
    out_partial = mm(hidden[0], w_down[0]) + mm(hidden[1], w_down[1])
    grad_rec_all, out_partial, hidden[0], hidden[1] = gather_tokens(
        grad_rec, out_partial.astype(BF16), *hidden
    )
    moved = mm_weight(hidden[1], grad_all)
    grad_rec_all, moved = tie(grad_rec_all, moved)
    grad_rows = weight_rows(
        hidden[0], grad_all, xor_send(moved, "dp", 1), hidden_width + width, 0
    )
    gm = mm_back(grad_rec_all, w_out)
    gm = gm.reshape(chips, length, 2 * width)
    ggate, gl, tail, end = back_mix(gm, both, across, rate)
    hin = carry_in(end[0], end[1], -1)
    moved = mm_weight(mixed[:, width:], grad_rec_all)
    hin, moved, grad_rows = tie(hin, moved, grad_rows)
    moved = xor_send(moved, "dp", 1)
    grad_rows = weight_rows(
        mixed[:, :width], grad_rec_all, moved, hidden_width + width, hidden_width, grad_rows
    )
    gbranch, last, head_rows, dw, sums = back_gates(
        (gl, tail, rate, m, r, g, conv, prev, bt), hin, prior, taps, vecs, w_gates
    )
    later = shift_send(head_rows, "seq", -1)
    fixed = []
    for j in range(lag):
        row = last[j]
        for k in range(lag - j, lag + 1):
            row = row + taps[k] * later[j + k - lag]
        fixed.append(row)
    fixed = jnp.stack(fixed, axis=1).astype(BF16)
    fixed = jnp.concatenate([fixed[:chips], fixed[chips:]], axis=2)
    gbranch = lax.dynamic_update_slice(gbranch, fixed, (0, length - lag, 0))
    gbranch, ggate = rows_of(gbranch), rows_of(ggate)
    grad_first = jnp.concatenate(
        [gbranch[:, :width], ggate[:, :width], gbranch[:, width:], ggate[:, width:]], axis=1
    )
    moved = mm_weight(normed_all, grad_first[:, 2 * width :])
    grad_first, moved, grad_rows, grad_second_rows = tie(
        grad_first, moved, grad_rows, grad_second_rows
    )
    row_cols = lax.psum_scatter(grad_rows, "seq", scatter_dimension=0, tiled=False)
    moved = xor_send(moved, "dp", 1)
    partial = mm_back(grad_first, w_first).astype(BF16)
    partial, normed_all = tie(partial, normed_all)
    grad_normed, moved, grad_first, dw, sums = scatter_tokens(
        partial.reshape(chips, length, model), moved, grad_first, dw, sums
    )
    grad_first_w = mm_weight(normed_all, grad_first[:, : 2 * width], moved)
    grad_normed, grad_first_w, out_partial = tie(grad_normed, grad_first_w, out_partial)
    (total,) = scatter_tokens(out_partial.reshape(chips, length, model))
    block_output = (residual + total).astype(BF16).reshape(block_input.shape)
    grad_second_rows = grad_second_rows.reshape(-1, hidden_width // tile, 2, tile).astype(F32)
    grad_mgate_w = grad_second_rows[:, :, 0].reshape(-1, hidden_width)
    grad_mup_w = grad_second_rows[:, :, 1].reshape(-1, hidden_width)
    norm_gain_term = jnp.sum(partial.astype(F32) * normed_all.astype(F32), axis=0) / norm_gain
    grad_first_w = lax.psum_scatter(grad_first_w, "seq", scatter_dimension=0, tiled=True)
    grad_in_w = grad_first_w[:, :own].astype(F32)
    grad_gate_w = grad_first_w[:, width : width + own].astype(F32)
    inv_one = lax.rsqrt(jnp.mean(tokens * tokens, axis=-1, keepdims=True) + EPSILON)
    grad_tokens, _ = norm_back(grad_normed, tokens, inv_one, norm_gain)
    input_grad = (grad_tokens + grad_residual).reshape(block_input.shape)

    down_cols, out_cols = row_cols[:hidden_width], row_cols[hidden_width : hidden_width + own]
    grad_down_w = place_rows(down_cols).astype(F32)
    grad_out_w = place_rows(out_cols).astype(F32)

    sums = sum_over(sums[0] + xor_send(sums[1], "dp", 1), "seq")
    sums = natural_order(gather_small(sums))[:, :, :own]
    sums = jnp.swapaxes(sums, 0, 1).reshape(-1, recur_width)
    decay_term = sums[2] * (8.0 * jax.nn.sigmoid(-decay_param))

    def diagonal(full):
        return jnp.stack(
            [full[h * head : (h + 1) * head, h * head : (h + 1) * head] for h in range(own_heads)]
        )

    blocks = jnp.stack([diagonal(dw[0]), diagonal(dw[2])])
    blocks = join_cores(blocks, jnp.stack([diagonal(dw[1]), diagonal(dw[3])]))
    blocks = sum_over(blocks, "seq")
    blocks = widen_blocks(gather_small(blocks))
    gains = sum_over(sum_over(jnp.stack([norm_gain_term, mlp_gain_term]), "dp"), "seq")
    return (
        block_output,
        input_grad,
        gains[0],
        grad_in_w,
        grad_gate_w,
        sums[4:],
        sums[3],
        blocks[0],
        sums[0],
        blocks[1],
        sums[1],
        decay_term,
        grad_out_w,
        gains[1],
        grad_mgate_w,
        grad_mup_w,
        grad_down_w,
    )


def solution(mesh):
    rows = P(("dp", "seq"), None)
    acts = P("dp", "seq", None)
    grads = P("seq", "dp")
    return jax.shard_map(
        local,
        mesh=mesh,
        in_specs=(
            acts, P(), rows, rows, P(), P(), P(), P(), P(), P(), P(), rows, P(), rows, rows, rows,
            acts,
        ),
        out_specs=(
            acts, acts, P(), grads, grads, P(), P(), P(), P(), P(), P(), P(), grads, P(), grads,
            grads, grads,
        ),
        check_vma=False,
    )
```

```python
import jax
import jax.numpy as jnp
from jax import lax
from jax.experimental import pallas as pl
from jax.experimental.pallas import tpu as pltpu
from jax.sharding import PartitionSpec as P

EPSILON = 1e-06
F32 = jnp.float32
BF16 = jnp.bfloat16
GELU_C = 0.7978845608028654
GELU_A = 0.044715
CHUNK = 32
VMEM_LIMIT = 48 << 20


def tie(*values):
    return lax.optimization_barrier(values)


def xor_send(value, axis, offset):
    count = lax.axis_size(axis)
    return lax.ppermute(value, axis, [(i, i ^ offset) for i in range(count)])


def shift_send(value, axis, steps):
    count = lax.axis_size(axis)
    first, last = max(0, -steps), min(count, count - steps)
    return lax.ppermute(value, axis, [(i, i + steps) for i in range(first, last)])


def gather_tokens(piece, *beside):
    chips = lax.axis_size("dp") // 2
    if chips == 4:
        half = piece.shape[0] // 2
        via_x = xor_send(piece, "dp", 2)
        via_y = xor_send(piece, "dp", 4)
        via_x, via_y, *beside = tie(via_x, via_y, *beside)
        top = xor_send(via_y[:half], "dp", 2)
        bottom = xor_send(via_x[half:], "dp", 4)
        return jnp.concatenate([piece, via_x, via_y, top, bottom], axis=0), *beside
    slots = [piece] + [xor_send(piece, "dp", 2 * o) for o in range(1, chips)]
    return jnp.concatenate(slots, axis=0), *beside


def scatter_begin(partial):
    chips = lax.axis_size("dp") // 2
    if chips == 4:
        half = partial.shape[1] // 2
        via_x = xor_send(partial[3, :half], "dp", 2)
        via_y = xor_send(partial[3, half:], "dp", 4)
        x_top = xor_send(partial[1, :half], "dp", 2)
        y_bottom = xor_send(partial[2, half:], "dp", 4)
        return (via_x, via_y), (x_top, y_bottom, partial)
    return (), tuple(xor_send(partial[o], "dp", 2 * o) for o in range(1, chips)) + (partial,)


def scatter_middle(via, kept):
    if not via:
        return ()
    partial = kept[-1]
    half = partial.shape[1] // 2
    to_x = (partial[1, half:].astype(F32) + via[1].astype(F32)).astype(BF16)
    to_y = (partial[2, :half].astype(F32) + via[0].astype(F32)).astype(BF16)
    return to_x, to_y


def scatter_send(sums):
    return (xor_send(sums[0], "dp", 2), xor_send(sums[1], "dp", 4)) if sums else ()


def scatter_end(hops, kept):
    partial = kept[-1]
    mine = partial[0].astype(F32)
    if not hops:
        for moved in kept[:-1]:
            mine = mine + moved.astype(F32)
        return mine
    x_bottom, y_top = hops
    x_top, y_bottom, _ = kept
    half = partial.shape[1] // 2
    return jnp.concatenate(
        [
            mine[:half] + x_top.astype(F32) + y_top.astype(F32),
            mine[half:] + x_bottom.astype(F32) + y_bottom.astype(F32),
        ],
        axis=0,
    )


def scatter_tokens(partial, *beside):
    via, kept = scatter_begin(partial)
    if via:
        *via, = tie(*via, *beside)
        via, beside = via[:2], via[2:]
    hops = scatter_send(scatter_middle(via, kept))
    return scatter_end(hops, kept), *beside


def join_cores(own_half, other_half):
    moved = xor_send(other_half.astype(BF16), "dp", 1)
    return (own_half + moved.astype(F32)).astype(BF16)


def gather_small(value):
    count = lax.axis_size("dp")
    evens = [value] + [xor_send(value, "dp", o) for o in range(2, count, 2)]
    evens = jnp.stack(evens, axis=0)
    both = jnp.stack([evens, xor_send(evens, "dp", 1)], axis=1)
    return both.reshape((count,) + value.shape)


def natural_order(slots):
    count, mine = slots.shape[0], lax.axis_index("dp")
    step = 1
    while step < count:
        pairs = slots.reshape((-1, 2, step) + slots.shape[1:])
        swapped = jnp.concatenate([pairs[:, 1:], pairs[:, :1]], axis=1)
        slots = jnp.where((mine // step) % 2 == 1, swapped, pairs).reshape(slots.shape)
        step *= 2
    return slots


def widen_blocks_kernel(mine_ref, slot_ref, *out_refs):
    for kind, out_ref in enumerate(out_refs):
        out_ref[...] = slot_ref[0, kind].astype(F32)


def widen_blocks(slots):
    count, kinds, heads, rows, cols = slots.shape
    mine = lax.axis_index("dp").astype(jnp.int32).reshape(1)
    return pl.pallas_call(
        widen_blocks_kernel,
        out_shape=(jax.ShapeDtypeStruct((count * heads, rows, cols), F32),) * kinds,
        grid_spec=pltpu.PrefetchScalarGridSpec(
            num_scalar_prefetch=1,
            grid=(count,),
            in_specs=[
                pl.BlockSpec((1, kinds, heads, rows, cols), lambda d, m: (d ^ m[0], 0, 0, 0, 0))
            ],
            out_specs=(pl.BlockSpec((heads, rows, cols), lambda d, m: (d, 0, 0)),) * kinds,
        ),
        compiler_params=params(),
        name="widen_blocks",
    )(mine, slots)


def sum_over(value, axis, begin=1, end=None):
    offset = begin
    total = value
    while offset < (end or lax.axis_size(axis)):
        moved = xor_send(total, axis, offset)
        total = (total.astype(F32) + moved.astype(F32)).astype(value.dtype)
        offset *= 2
    return total


def carry_in(decay, state, steps):
    count = lax.axis_size("seq")
    both = jnp.stack([decay, state], axis=0)
    moved = [shift_send(both, "seq", steps * k) for k in range(1, count)]
    carried = moved[-1][1]
    for item in reversed(moved[:-1]):
        carried = item[1] + item[0] * carried
    return carried


def quarter_shift():
    dp_count, seq_count = lax.axis_size("dp"), lax.axis_size("seq")
    mine = lax.axis_index("dp")
    ratio = dp_count // seq_count
    return shift_of(mine, ratio, seq_count)


def shift_of(d, ratio, seq_count):
    group = d // ratio
    flip = (d % 2) * (seq_count - 1)
    return group ^ flip


def move_in_plane(block):
    dp_count, seq_count = lax.axis_size("dp"), lax.axis_size("seq")
    perm = []
    for d in range(dp_count):
        for s in range(seq_count):
            quarter = s ^ shift_of(d, dp_count // seq_count, seq_count)
            perm.append((d * seq_count + s, (2 * quarter + d % 2) * seq_count + s))
    return lax.ppermute(block, ("dp", "seq"), perm)


def move_across(block):
    dp_count, seq_count = lax.axis_size("dp"), lax.axis_size("seq")
    assert dp_count == 2 * seq_count
    perm = []
    for d in range(dp_count):
        for s in range(seq_count):
            perm.append((d * seq_count + s, d * seq_count + (s ^ shift_of(d, 2, seq_count))))
    block = lax.ppermute(block, ("dp", "seq"), perm)
    half = block.shape[1] // 2
    first_core = lax.axis_index("dp") % 2 == 0
    left, right = block[:, :half], block[:, half:]
    kept = jnp.where(first_core, left, right)
    moved = xor_send(jnp.where(first_core, right, left), "dp", 1)
    return jnp.concatenate(
        [jnp.where(first_core, kept, moved), jnp.where(first_core, moved, kept)], axis=0
    )


def scaled_norm(values, gain_vec):
    return (
        values * lax.rsqrt(jnp.mean(values * values, axis=-1, keepdims=True) + EPSILON) * gain_vec
    )


def gelu_pair(v):
    square = v * v
    t = jnp.tanh(GELU_C * (v + GELU_A * v * square))
    half = 0.5 * (1.0 + t)
    slope = half + 0.5 * v * (1.0 - t * t) * (GELU_C * (1.0 + 3.0 * GELU_A * square))
    return v * half, slope


def logistic(v):
    return 1.0 / (1.0 + jnp.exp(-v))


def one_minus_exp(x, exp_x):
    poly = jnp.full_like(x, 1.0 / 362880.0)
    for coef in (1 / 40320.0, 1 / 5040.0, 1 / 720.0, 1 / 120.0, 1 / 24.0, 1 / 6.0, 0.5, 1.0):
        poly = poly * x + coef
    return jnp.where(x > -0.35, -x * poly, 1.0 - exp_x)


def half_mask(chunk, slots, width):
    return lax.broadcasted_iota(jnp.int32, (chunk, slots, width), 1) < slots // 2


def join_slots(own_ref, other_ref):
    return jnp.concatenate([own_ref[...], other_ref[...]], axis=0)


def fwd_gates_kernel(
    own_ref, other_ref, prior_ref, taps_ref, vec_ref, w_ref,
    bt_ref, conv_ref, r_ref, i_ref, rate_ref, m_ref, loc_ref, run_ref,
    halo, state, decay,
):
    chunk, slots, width = bt_ref.shape

    @pl.when(pl.program_id(0) == 0)
    def _():
        halo[...] = prior_ref[...]
        state[...] = jnp.zeros_like(state)
        decay[...] = jnp.ones_like(decay)

    bt = jnp.swapaxes(join_slots(own_ref, other_ref), 0, 1)
    bt_ref[...] = bt
    lag = halo.shape[0]
    padded = jnp.concatenate([halo[...], bt], axis=0)
    halo[...] = padded[chunk : chunk + lag]
    conv = jnp.zeros_like(bt) + vec_ref[0]
    for k in range(lag + 1):
        conv = conv + taps_ref[k] * padded[lag - k : lag - k + chunk]
    conv_ref[...] = conv
    rows = conv.reshape(chunk * slots, width).astype(BF16)
    mask = half_mask(chunk, slots, width)

    def gate(which):
        own = jnp.dot(rows, w_ref[2 * which], preferred_element_type=F32)
        other = jnp.dot(rows, w_ref[2 * which + 1], preferred_element_type=F32)
        shape = (chunk, slots, width)
        pre = jnp.where(mask, own.reshape(shape), other.reshape(shape))
        return logistic(pre + vec_ref[1 + which])

    r, g = gate(0), gate(1)
    log_rate = r * vec_ref[3]
    rate = jnp.exp(log_rate)
    m = jnp.sqrt(one_minus_exp(2.0 * log_rate, rate * rate))
    r_ref[...] = r
    i_ref[...] = g
    rate_ref[...] = rate
    m_ref[...] = m
    driven = m * g * conv
    st, dc = state[...], decay[...]
    for t in range(chunk):
        st = rate[t] * st + driven[t]
        dc = rate[t] * dc
        loc_ref[t] = st
        run_ref[t] = dc
    state[...] = st
    decay[...] = dc


def fwd_mix_kernel(
    loc_ref, run_ref, carry_ref, gate_own_ref, gate_other_ref,
    mixed_ref, prev_ref, across_ref, last,
):
    chunk, slots, width = loc_ref.shape

    @pl.when(pl.program_id(0) == 0)
    def _():
        last[...] = carry_ref[...]

    states = loc_ref[...] + run_ref[...] * carry_ref[...]
    prev_ref[...] = jnp.concatenate([last[...][None], states[: chunk - 1]], axis=0)
    last[...] = states[chunk - 1]
    across = jnp.swapaxes(states, 0, 1)
    across_ref[...] = across
    half = slots // 2
    own, _ = gelu_pair(gate_own_ref[...])
    other, _ = gelu_pair(gate_other_ref[...])
    mixed_ref[:, :, :width] = (across[:half] * own).astype(BF16)
    mixed_ref[:, :, width:] = (across[half:] * other).astype(BF16)


def back_mix_kernel(
    gm_own_ref, gm_other_ref, gate_own_ref, gate_other_ref, across_ref, rate_ref,
    ggate_ref, gl_ref, tail_ref, end_ref, held, decay,
):
    chunk, slots, width = rate_ref.shape

    @pl.when(pl.program_id(0) == 0)
    def _():
        held[...] = jnp.zeros_like(held)
        decay[...] = jnp.ones_like(decay)

    half = slots // 2
    gm = join_slots(gm_own_ref, gm_other_ref)
    act, slope = gelu_pair(join_slots(gate_own_ref, gate_other_ref))
    ggate = (gm * across_ref[...] * slope).astype(BF16)
    ggate_ref[:, :, :width] = ggate[:half]
    ggate_ref[:, :, width:] = ggate[half:]
    gs = jnp.swapaxes(gm * act, 0, 1)
    rate = rate_ref[...]
    h, dc = held[...], decay[...]
    for t in reversed(range(chunk)):
        grad = gs[t] + h
        gl_ref[t] = grad
        tail_ref[t] = dc
        h = rate[t] * grad
        dc = rate[t] * dc
    held[...] = h
    decay[...] = dc
    end_ref[0] = dc
    end_ref[1] = h


def back_gates_kernel(
    gl_ref, tail_ref, rate_ref, m_ref, r_ref, i_ref, conv_ref, prev_ref, bt_ref,
    hin_ref, prior_ref, taps_ref, vec_ref, w_ref,
    gbranch_ref, last_ref, head_ref, dw_own_ref, dw_other_ref, total_ref,
    later, sums_ref, dw_ref,
):
    chunk, slots, width = rate_ref.shape
    lag = later.shape[0]
    step = pl.program_id(0)

    @pl.when(step == 0)
    def _():
        later[...] = jnp.zeros_like(later)
        dw_ref[...] = jnp.zeros_like(dw_ref)
        sums_ref[...] = jnp.zeros_like(sums_ref)

    s = gl_ref[...] + tail_ref[...] * hin_ref[...]
    rate, m, r, g, conv = rate_ref[...], m_ref[...], r_ref[...], i_ref[...], conv_ref[...]
    sc = s * conv
    dpi = (sc * m * (g * (1.0 - g))).astype(BF16).astype(F32)
    dlog = s * prev_ref[...] * rate - sc * g * (rate * rate) / m
    dpr = (dlog * vec_ref[3] * (r * (1.0 - r))).astype(BF16).astype(F32)
    sums_ref[2] += jnp.sum(dlog * r, axis=0)
    sums_ref[0] += jnp.sum(dpr, axis=0)
    sums_ref[1] += jnp.sum(dpi, axis=0)
    mask = half_mask(chunk, slots, width)
    flat = (chunk * slots, width)
    rows_own = jnp.where(mask, conv, 0.0).reshape(flat).astype(BF16)
    rows_other = jnp.where(mask, 0.0, conv).reshape(flat).astype(BF16)
    dpr = dpr.reshape(flat).astype(BF16)
    dpi = dpi.reshape(flat).astype(BF16)
    over_rows = (((0,), (0,)), ((), ()))
    over_cols = (((1,), (1,)), ((), ()))
    dw_ref[0] += lax.dot_general(rows_own, dpr, over_rows, preferred_element_type=F32)
    dw_ref[1] += lax.dot_general(rows_own, dpi, over_rows, preferred_element_type=F32)
    dw_ref[2] += lax.dot_general(rows_other, dpr, over_rows, preferred_element_type=F32)
    dw_ref[3] += lax.dot_general(rows_other, dpi, over_rows, preferred_element_type=F32)

    def through(which):
        part = lax.dot_general(dpr, w_ref[which], over_cols, preferred_element_type=F32)
        part += lax.dot_general(dpi, w_ref[2 + which], over_cols, preferred_element_type=F32)
        return part.reshape(chunk, slots, width)

    gconv = jnp.where(mask, through(0), through(1)) + s * m * g
    padded = jnp.concatenate([gconv, later[...]], axis=0)
    later[...] = gconv[:lag]
    head_ref[...] = gconv[:lag]
    sums_ref[3] += jnp.sum(gconv, axis=0)
    bt = bt_ref[...]
    gb = jnp.zeros_like(gconv)
    for k in range(lag + 1):
        shifted = padded[k : k + chunk]
        gb = gb + taps_ref[k] * shifted
        sums_ref[4 + k] += jnp.sum(bt * shifted, axis=0)

    @pl.when(step == 0)
    def _():
        last_ref[...] = gb[chunk - lag :]

    across = jnp.swapaxes(gb, 0, 1).astype(BF16)
    gbranch_ref[:, :, :width] = across[: slots // 2]
    gbranch_ref[:, :, width:] = across[slots // 2 :]

    @pl.when(step == pl.num_programs(0) - 1)
    def _():
        for k in range(1, lag + 1):
            for j in range(1, k + 1):
                sums_ref[4 + k] += prior_ref[lag - j] * gconv[k - j]
        half = slots // 2
        for kind in range(total_ref.shape[1]):
            total_ref[0, kind] = jnp.sum(sums_ref[kind, :half], axis=0)
            total_ref[1, kind] = jnp.sum(sums_ref[kind, half:], axis=0)
        heads, head = dw_own_ref.shape[1:3]
        for kind in range(2):
            for h in range(heads):
                for begin, ref in ((0, dw_own_ref), (2, dw_other_ref)):
                    rows = dw_ref[begin + kind, h * head : (h + 1) * head, :]
                    if h:
                        rows = pltpu.roll(rows, width - h * head, 1)
                    ref[kind, h] = rows[:, :head].astype(ref.dtype)


def specs_for(slots, length, width, backwards):
    count = length // CHUNK

    def at(c):
        return count - 1 - c if backwards else c

    time_major = pl.BlockSpec((CHUNK, slots, width), lambda c: (at(c), 0, 0))

    def columns(j, times=1, halves=2):
        return pl.BlockSpec((slots // halves, CHUNK, times * width), lambda c: (0, at(c), j))

    return count, time_major, columns


def whole(*shape):
    return pl.BlockSpec(shape, lambda c: (0,) * len(shape))


def params():
    return pltpu.CompilerParams(
        dimension_semantics=("arbitrary",), vmem_limit_bytes=VMEM_LIMIT
    )


def cost(flops, size, trans):
    return pl.CostEstimate(flops=flops, bytes_accessed=size, transcendentals=trans)


def fwd_gates(both, prior, taps, vecs, w):
    length = both.shape[1]
    lag, slots, width = prior.shape
    count, tm, cols = specs_for(slots, length, width, False)
    full = jax.ShapeDtypeStruct((length, slots, width), F32)
    n = slots * length * width
    return pl.pallas_call(
        fwd_gates_kernel,
        out_shape=(full,) * 8,
        grid=(count,),
        in_specs=[
            cols(0), cols(2), whole(*prior.shape), whole(*taps.shape), whole(*vecs.shape),
            whole(*w.shape),
        ],
        out_specs=(tm,) * 8,
        scratch_shapes=[
            pltpu.VMEM(prior.shape, F32),
            pltpu.VMEM((slots, width), F32),
            pltpu.VMEM((slots, width), F32),
        ],
        compiler_params=params(),
        cost_estimate=cost(n, 58 * n, n),
        name="gates_forward",
    )(both, both, prior, taps, vecs, w)


def fwd_mix(loc, run, carry, both):
    length, slots, width = loc.shape
    count, tm, cols = specs_for(slots, length, width, False)
    n = slots * length * width
    return pl.pallas_call(
        fwd_mix_kernel,
        out_shape=(
            jax.ShapeDtypeStruct((slots // 2, length, 2 * width), BF16),
            jax.ShapeDtypeStruct((length, slots, width), F32),
            jax.ShapeDtypeStruct((slots, length, width), F32),
        ),
        grid=(count,),
        in_specs=[tm, tm, whole(slots, width), cols(1), cols(3)],
        out_specs=(cols(0, 2), tm, cols(0, 1, 1)),
        scratch_shapes=[pltpu.VMEM((slots, width), F32)],
        compiler_params=params(),
        cost_estimate=cost(n, 36 * n, n),
        name="mix_forward",
    )(loc, run, carry, both, both)


def back_mix(gm, both, across, rate):
    length, slots, width = rate.shape
    count, tm, cols = specs_for(slots, length, width, True)
    n = slots * length * width
    return pl.pallas_call(
        back_mix_kernel,
        out_shape=(
            jax.ShapeDtypeStruct((slots // 2, length, 2 * width), BF16),
            jax.ShapeDtypeStruct((length, slots, width), F32),
            jax.ShapeDtypeStruct((length, slots, width), F32),
            jax.ShapeDtypeStruct((2, slots, width), F32),
        ),
        grid=(count,),
        in_specs=[cols(0), cols(1), cols(1), cols(3), cols(0, 1, 1), tm],
        out_specs=(cols(0, 2), tm, tm, whole(2, slots, width)),
        scratch_shapes=[pltpu.VMEM((slots, width), F32), pltpu.VMEM((slots, width), F32)],
        compiler_params=params(),
        cost_estimate=cost(n, 44 * n, n),
        name="mix_backward",
    )(gm, gm, both, both, across, rate)


def back_gates(kept, hin, prior, taps, vecs, w, heads, head):
    length, slots, width = kept[0].shape
    lag = prior.shape[0]
    count, tm, cols = specs_for(slots, length, width, True)
    n = slots * length * width
    return pl.pallas_call(
        back_gates_kernel,
        out_shape=(
            jax.ShapeDtypeStruct((slots // 2, length, 2 * width), BF16),
            jax.ShapeDtypeStruct((lag, slots, width), F32),
            jax.ShapeDtypeStruct((lag, slots, width), F32),
            jax.ShapeDtypeStruct((2, heads, head, head), F32),
            jax.ShapeDtypeStruct((2, heads, head, head), BF16),
            jax.ShapeDtypeStruct((2, 5 + lag, width), F32),
        ),
        grid=(count,),
        in_specs=[tm] * 9
        + [
            whole(slots, width), whole(*prior.shape), whole(*taps.shape), whole(*vecs.shape),
            whole(*w.shape),
        ],
        out_specs=(
            cols(0, 2), whole(lag, slots, width), whole(lag, slots, width),
            whole(2, heads, head, head), whole(2, heads, head, head), whole(2, 5 + lag, width),
        ),
        scratch_shapes=[
            pltpu.VMEM((lag, slots, width), F32),
            pltpu.VMEM((5 + lag, slots, width), F32),
            pltpu.VMEM(w.shape, F32),
        ],
        compiler_params=params(),
        cost_estimate=cost(n, 76 * n, n),
        name="gates_backward",
    )(*kept, hin, prior, taps, vecs, w)


def tile_of(hidden_width):
    return 256 if hidden_width % 256 == 0 else 128


def row_blocks(rows):
    step = 256 if rows % 256 == 0 else rows
    return [slice(at, at + step) for at in range(0, rows, step)]


def mlp_forward_kernel(x_ref, w_ref, hidden_ref, kept_ref):
    tile = hidden_ref.shape[1]
    weight = jnp.swapaxes(w_ref[...], 0, 1).reshape(x_ref.shape[1], 2 * tile)
    for rows in row_blocks(x_ref.shape[0]):
        ffn = jnp.dot(x_ref[rows, :], weight, preferred_element_type=F32)
        act, slope = gelu_pair(ffn[:, :tile])
        up = ffn[:, tile:]
        hidden_ref[rows, :] = (act * up).astype(BF16)
        kept_ref[rows, :tile] = (slope * up).astype(BF16)
        kept_ref[rows, tile:] = act.astype(BF16)


def mlp_forward(x, weight):
    rows, model = x.shape
    hidden_width = weight.shape[3] // 2
    tile = tile_of(hidden_width)
    return pl.pallas_call(
        mlp_forward_kernel,
        out_shape=(
            jax.ShapeDtypeStruct((rows, hidden_width), BF16),
            jax.ShapeDtypeStruct((rows, 2 * hidden_width), BF16),
        ),
        grid=(hidden_width // tile,),
        in_specs=[
            pl.BlockSpec((rows, model), lambda j: (0, 0), pipeline_mode=pl.Buffered(1)),
            pl.BlockSpec(weight.shape[:3] + (2 * tile,), lambda j: (0, 0, 0, j)),
        ],
        out_specs=(
            pl.BlockSpec((rows, tile), lambda j: (0, j)),
            pl.BlockSpec((rows, 2 * tile), lambda j: (0, j)),
        ),
        compiler_params=params(),
        cost_estimate=cost(7 * rows * hidden_width * model, rows * model, 0),
        name="mlp_forward",
    )(x, weight)


OVER_COLS = (((1,), (1,)), ((), ()))


def hidden_backward_kernel(g_ref, down0_ref, down1_ref, kept0_ref, kept1_ref, ffn0_ref, ffn1_ref):
    step = pl.program_id(0)
    tile = down0_ref.shape[0]

    def half(down_ref, kept_ref, ffn_ref):
        for rows in row_blocks(g_ref.shape[0]):
            grad = lax.dot_general(
                g_ref[rows, :], down_ref[...], OVER_COLS, preferred_element_type=F32
            )
            ffn_ref[rows, :tile] = (grad * kept_ref[rows, :tile].astype(F32)).astype(BF16)
            ffn_ref[rows, tile:] = (grad * kept_ref[rows, tile:].astype(F32)).astype(BF16)

    @pl.when(step < pl.num_programs(0) // 2)
    def _():
        half(down1_ref, kept1_ref, ffn1_ref)

    @pl.when(step >= pl.num_programs(0) // 2)
    def _():
        half(down0_ref, kept0_ref, ffn0_ref)


def hidden_backward(grad, down, kept):
    rows, model = grad.shape
    hidden_width = down[0].shape[0]
    tile = tile_of(hidden_width)
    half = hidden_width // tile

    def own(j):
        return jnp.maximum(j - half, 0)

    def other(j):
        return jnp.minimum(j, half - 1)

    full = jax.ShapeDtypeStruct((rows, 2 * hidden_width), BF16)
    return pl.pallas_call(
        hidden_backward_kernel,
        out_shape=(full, full),
        grid=(2 * half,),
        in_specs=[
            pl.BlockSpec((rows, model), lambda j: (0, 0), pipeline_mode=pl.Buffered(1)),
            pl.BlockSpec((tile, model), lambda j: (own(j), 0)),
            pl.BlockSpec((tile, model), lambda j: (other(j), 0)),
            pl.BlockSpec((rows, 2 * tile), lambda j: (0, own(j))),
            pl.BlockSpec((rows, 2 * tile), lambda j: (0, other(j))),
        ],
        out_specs=(
            pl.BlockSpec((rows, 2 * tile), lambda j: (0, own(j))),
            pl.BlockSpec((rows, 2 * tile), lambda j: (0, other(j))),
        ),
        compiler_params=params(),
        cost_estimate=cost(7 * rows * hidden_width * model, rows * model, 0),
        name="hidden_backward",
    )(grad, *down, *kept)


def normed_backward_kernel(ffn0_ref, ffn1_ref, w0_ref, w1_ref, out_ref):
    width = ffn0_ref.shape[1]
    for rows in row_blocks(ffn0_ref.shape[0]):
        total = None
        for ffn_ref, w_ref in ((ffn0_ref, w0_ref), (ffn1_ref, w1_ref)):
            part = lax.dot_general(
                ffn_ref[rows, :],
                w_ref[...].reshape(out_ref.shape[1], width),
                OVER_COLS,
                preferred_element_type=F32,
            )
            total = part if total is None else total + part
        out_ref[rows, :] = total.astype(BF16)


def normed_backward(ffn, weight):
    rows, width = ffn[0].shape
    seq_count, dp_count, shard, _ = weight[0].shape
    cols = seq_count * shard
    kept = pl.BlockSpec((rows, width), lambda j: (0, 0), pipeline_mode=pl.Buffered(1))
    block = pl.BlockSpec((seq_count, 1, shard, width), lambda j: (0, j, 0, 0))
    return pl.pallas_call(
        normed_backward_kernel,
        out_shape=jax.ShapeDtypeStruct((rows, cols * dp_count), BF16),
        grid=(dp_count,),
        in_specs=[kept, kept, block, block],
        out_specs=pl.BlockSpec((rows, cols), lambda j: (0, j)),
        compiler_params=params(),
        cost_estimate=cost(7 * rows * width * cols * dp_count, rows * width, 0),
        name="normed_backward",
    )(*ffn, *weight)


def unpack_down_kernel(packed_ref, out_ref):
    out_ref[...] = jnp.concatenate(
        [packed_ref[0, block] for block in range(packed_ref.shape[1])], axis=1
    )


def unpack_down(packed, first_column, rows):
    seq_count, dp_count, shard, _ = packed.shape
    lay = rows // (seq_count * shard)
    part = (packed.shape[3] - first_column) // lay
    begin = first_column // part
    return pl.pallas_call(
        unpack_down_kernel,
        out_shape=jax.ShapeDtypeStruct((rows, dp_count * part), packed.dtype),
        grid=(seq_count, lay),
        in_specs=[
            pl.BlockSpec((1, dp_count, shard, part), lambda s, k: (s, 0, 0, begin + k))
        ],
        out_specs=pl.BlockSpec((shard, dp_count * part), lambda s, k: (s * lay + k, 0)),
        compiler_params=pltpu.CompilerParams(
            dimension_semantics=("arbitrary", "arbitrary"), vmem_limit_bytes=VMEM_LIMIT
        ),
        cost_estimate=cost(0, 2 * rows * dp_count * part * 2, 0),
        name="unpack_down",
    )(packed)


def weight_kernel(left_ref, right_ref, *refs):
    out_ref = refs[-1]
    product = lax.dot_general(
        left_ref[...], right_ref[...], (((0,), (0,)), ((), ())), preferred_element_type=F32
    )
    if len(refs) == 2:
        product = product + refs[0][...].astype(F32)
    out_ref[...] = product.astype(BF16)


def mm_weight(left, right, *added):
    depth, rows = left.shape
    cols = right.shape[1]
    tile = 256 if rows % 256 == 0 else 128
    block = pl.BlockSpec((tile, cols), lambda i: (i, 0))
    return pl.pallas_call(
        weight_kernel,
        out_shape=jax.ShapeDtypeStruct((rows, cols), BF16),
        grid=(rows // tile,),
        in_specs=[
            pl.BlockSpec((depth, tile), lambda i: (0, i)),
            pl.BlockSpec((depth, cols), lambda i: (0, 0), pipeline_mode=pl.Buffered(1)),
        ]
        + [block] * len(added),
        out_specs=block,
        compiler_params=params(),
        cost_estimate=cost(3 * rows * cols * depth, rows * cols, 0),
        name="weight_gradient",
    )(left, right, *added)


def weight_rows_kernel(shift_ref, left_ref, right_ref, added_ref, out_ref):
    product = lax.dot_general(
        left_ref[...], right_ref[...], (((0,), (0,)), ((), ())), preferred_element_type=F32
    )
    product = (product + added_ref[...].astype(F32)).astype(BF16)
    count, _, cols = out_ref.shape
    for quarter in range(count):
        out_ref[quarter ^ shift_ref[0]] = product[:, quarter * cols : (quarter + 1) * cols]


def weight_rows(left, right, added):
    depth, rows = left.shape
    cols = right.shape[1]
    count = lax.axis_size("seq")
    tile = 128
    shift = quarter_shift().astype(jnp.int32).reshape(1)
    return pl.pallas_call(
        weight_rows_kernel,
        out_shape=jax.ShapeDtypeStruct((count, rows, cols // count), BF16),
        grid_spec=pltpu.PrefetchScalarGridSpec(
            num_scalar_prefetch=1,
            grid=(rows // tile,),
            in_specs=[
                pl.BlockSpec((depth, tile), lambda i, s: (0, i)),
                pl.BlockSpec((depth, cols), lambda i, s: (0, 0), pipeline_mode=pl.Buffered(1)),
                pl.BlockSpec((tile, cols), lambda i, s: (i, 0)),
            ],
            out_specs=pl.BlockSpec((count, tile, cols // count), lambda i, s: (0, i, 0)),
        ),
        compiler_params=params(),
        cost_estimate=cost(3 * rows * cols * depth, rows * cols, 0),
        name="weight_rows",
    )(shift, left, right, added)


def rows_of(value):
    return value.reshape(-1, value.shape[-1])


def mm(left, right):
    return jnp.dot(left, right, preferred_element_type=F32)


def mm_back(grad_rows, weight):
    return lax.dot_general(grad_rows, weight, (((1,), (1,)), ((), ())), preferred_element_type=F32)


def local(
    block_input, norm_gain, in_proj, gate_proj, conv_kernel, conv_bias,
    recur_weight, recur_bias, input_weight, input_bias, decay_param,
    out_proj, mlp_gain, mlp_gate, mlp_up, mlp_down, out_grad,
):
    dp_count, seq_count = lax.axis_size("dp"), lax.axis_size("seq")
    mine = lax.axis_index("dp")
    model = block_input.shape[2]
    tokens = block_input.reshape(-1, model).astype(F32)
    length = tokens.shape[0]
    recur_width = in_proj.shape[1]
    own = recur_width // dp_count
    width = -(-own // 128) * 128
    hidden_width = mlp_gate.shape[1] // dp_count
    head = recur_weight.shape[1]
    own_heads = own // head
    lag = conv_kernel.shape[0] - 1

    chips = dp_count // 2

    shard = in_proj.shape[0]

    def split_cols(weight, padded):
        part = jnp.swapaxes(weight.reshape(shard, dp_count, -1), 0, 1)
        return jnp.pad(part, ((0, 0), (0, 0), (0, padded - part.shape[2])))

    def spread(joined):
        return lax.all_to_all(joined, "dp", split_axis=0, concat_axis=0, tiled=True)

    def natural_rows(full):
        return full.transpose(1, 0, 2, 3).reshape(-1, full.shape[3])

    def partner(value):
        return xor_send(value, "dp", 1)

    w_out = lax.all_gather(out_proj, "seq", axis=0, tiled=True)
    first = jnp.concatenate([split_cols(in_proj, width), split_cols(gate_proj, width)], axis=2)
    first = spread(first)
    first = lax.all_gather(first, "seq", axis=0)
    def per_slot(value):
        rows = []
        for index in (mine, mine ^ 1):
            part = lax.dynamic_slice_in_dim(value, index * own, own, axis=value.ndim - 1)
            rows.append(jnp.pad(part, [(0, 0)] * (value.ndim - 1) + [(0, width - own)]))
        return jnp.repeat(jnp.stack(rows, axis=-2), chips, axis=-2)

    taps = per_slot(conv_kernel)
    vecs = per_slot(jnp.stack([conv_bias, recur_bias, input_bias, decay_param]))
    vecs = jnp.concatenate([vecs[:3], -8.0 * jax.nn.softplus(-vecs[3:])], axis=0)

    def block_diagonal(weight, index):
        part = lax.dynamic_slice_in_dim(weight, index * own_heads, own_heads, axis=0)
        rows = [
            jnp.pad(part[h], ((0, 0), (h * head, width - (h + 1) * head)))
            for h in range(own_heads)
        ]
        return jnp.pad(jnp.concatenate(rows, axis=0), ((0, width - own), (0, 0)))

    w_gates = jnp.stack(
        [block_diagonal(w, i) for w in (recur_weight, input_weight) for i in (mine, mine ^ 1)]
    )

    taps, vecs, w_gates = tie(taps, vecs, w_gates)

    normed = scaled_norm(tokens, norm_gain).astype(BF16)
    normed_all, w_out = gather_tokens(normed, w_out)
    w_out = jnp.pad(w_out, ((0, width - own), (0, 0)))
    w_out = jnp.concatenate([w_out, partner(w_out)], axis=0)
    tile = tile_of(hidden_width)

    def by_tile(weight):
        return weight.reshape(shard, dp_count, hidden_width // tile, tile)

    second = jnp.concatenate([by_tile(mlp_gate), by_tile(mlp_up)], axis=3)
    second = jnp.swapaxes(second.reshape(shard, dp_count, 2 * hidden_width), 0, 1)
    lay = mlp_down.shape[0] // shard
    part = model // dp_count
    down = mlp_down.reshape(lay, shard, dp_count, part).transpose(2, 1, 0, 3)
    down = down.reshape(dp_count, shard, lay * part)
    second, down, normed_all = tie(second, down, normed_all)
    grad_low, second, first = tie(out_grad.reshape(length, model), spread(second), first)
    second = lax.all_gather(jnp.concatenate([second, down], axis=2), "seq", axis=0)

    w_first = natural_rows(first)
    w_first = jnp.concatenate([w_first, partner(w_first)], axis=1)

    both = mm(normed_all, w_first)
    grad_all, both = gather_tokens(grad_low, both)
    both = both.reshape(chips, length, 4 * width)
    ends = both[:, length - lag :]
    ends = jnp.concatenate([ends[:, :, :width], ends[:, :, 2 * width : 3 * width]], axis=0)
    prior = shift_send(jnp.swapaxes(ends, 0, 1), "seq", 1)
    bt, conv, r, g, rate, m, loc, run = fwd_gates(both, prior, taps, vecs, w_gates)
    carry = carry_in(run[length - 1], loc[length - 1], 1)
    mixed, prev, across = fwd_mix(loc, run, carry, both)
    mixed = rows_of(mixed)
    partial, grad_all = tie(mm(mixed, w_out).astype(BF16), grad_all)
    (total,) = scatter_tokens(partial.reshape(chips, length, model))
    residual = tokens + total

    inv_two = lax.rsqrt(jnp.mean(residual * residual, axis=-1, keepdims=True) + EPSILON)
    normed_two = (residual * inv_two * mlp_gain).astype(BF16)
    (normed_two_all,) = gather_tokens(normed_two)
    normed_two_all, second = tie(normed_two_all, second)
    w_second = second[:, :, :, : 2 * hidden_width]
    w_second = (w_second, partner(w_second))
    w_down = unpack_down(second, 2 * hidden_width, hidden_width)
    w_down = (w_down, partner(w_down))
    hidden, kept = zip(*[mlp_forward(normed_two_all, weight) for weight in w_second])
    hidden = list(hidden)
    moved_down, grad_all = tie(mm_weight(hidden[1], grad_all), grad_all)
    moved_down = xor_send(moved_down, "dp", 1)
    grad_ffn = list(hidden_backward(grad_all, w_down, kept))
    moved = mm_weight(normed_two_all, grad_ffn[1])
    grad_down = weight_rows(hidden[0], grad_all, moved_down)
    grad_ffn[0], moved, grad_down = tie(grad_ffn[0], moved, grad_down)
    down_cols = lax.psum_scatter(grad_down, "seq", scatter_dimension=0, tiled=False)
    moved = xor_send(moved, "dp", 1)
    partial = normed_backward(grad_ffn, w_second)
    partial, grad_ffn[0], normed_two_all = tie(partial, grad_ffn[0], normed_two_all)
    grad_normed_two, moved, grad_ffn[0] = scatter_tokens(
        partial.reshape(chips, length, model), moved, grad_ffn[0]
    )
    grad_second = mm_weight(normed_two_all, grad_ffn[0], moved)
    grad_normed_two, grad_second = tie(grad_normed_two, grad_second)
    grad_second_rows = lax.psum_scatter(grad_second, "seq", scatter_dimension=0, tiled=True)

    def norm_back(grad, values, inv, gain):
        unit = values * inv
        scaled = grad * gain
        mean = jnp.mean(scaled * unit, axis=-1, keepdims=True)
        return inv * (scaled - unit * mean), unit

    grad_resid, unit_two = norm_back(grad_normed_two, residual, inv_two, mlp_gain)
    mlp_gain_term = jnp.sum(grad_normed_two * unit_two, axis=0)
    grad_residual = grad_resid + grad_low.astype(F32)

    grad_rec, hidden[0], hidden[1] = tie(grad_residual.astype(BF16), *hidden)
    out_partial = mm(hidden[0], w_down[0]) + mm(hidden[1], w_down[1])
    grad_rec_all, out_partial, down_cols = gather_tokens(
        grad_rec, out_partial.astype(BF16), down_cols
    )
    grad_rec_all, out_partial = tie(grad_rec_all, out_partial)
    via, kept_out = scatter_begin(out_partial.reshape(chips, length, model))
    gm = mm_back(grad_rec_all, w_out)
    gm = gm.reshape(chips, length, 2 * width)
    ggate, gl, tail, end = back_mix(gm, both, across, rate)
    hin = carry_in(end[0], end[1], -1)
    moved = mm_weight(mixed[:, width:], grad_rec_all)
    hin, moved, *out_sums = tie(hin, moved, *scatter_middle(via, kept_out))
    hops = scatter_send(out_sums)
    grad_out = weight_rows(mixed[:, :width], grad_rec_all, xor_send(moved, "dp", 1))
    hin, grad_out = tie(hin, grad_out)
    gbranch, last, head_rows, dw_own, dw_other, sums = back_gates(
        (gl, tail, rate, m, r, g, conv, prev, bt), hin, prior, taps, vecs, w_gates,
        own_heads, head,
    )
    later, down_cols = tie(shift_send(head_rows, "seq", -1), down_cols)
    down_cols = move_in_plane(down_cols)
    fixed = []
    for j in range(lag):
        row = last[j]
        for k in range(lag - j, lag + 1):
            row = row + taps[k] * later[j + k - lag]
        fixed.append(row)
    fixed = jnp.stack(fixed, axis=1).astype(BF16)
    fixed = jnp.concatenate([fixed[:chips], fixed[chips:]], axis=2)
    gbranch = lax.dynamic_update_slice(gbranch, fixed, (0, length - lag, 0))
    gbranch, ggate = rows_of(gbranch), rows_of(ggate)
    grad_first = jnp.concatenate(
        [gbranch[:, :width], ggate[:, :width], gbranch[:, width:], ggate[:, width:]], axis=1
    )
    moved = mm_weight(normed_all, grad_first[:, 2 * width :])
    blocks = (dw_own + xor_send(dw_other, "dp", 1).astype(F32)).astype(BF16)
    blocks = sum_over(blocks, "seq", 1, 2)
    grad_first, moved, grad_second_rows, blocks = tie(
        grad_first, moved, grad_second_rows, blocks
    )
    blocks = sum_over(blocks, "seq", 2)
    moved = xor_send(moved, "dp", 1)
    partial = mm_back(grad_first, w_first).astype(BF16)
    partial, normed_all, sums, blocks, grad_out = tie(
        partial, normed_all, sums, blocks, grad_out
    )
    out_cols = lax.psum_scatter(grad_out, "seq", scatter_dimension=0, tiled=False)
    grad_first_w = mm_weight(normed_all, grad_first[:, : 2 * width], moved)
    sums = sums[0] + xor_send(sums[1], "dp", 1)
    partial, grad_first_w = tie(partial, grad_first_w)
    grad_normed, sums, out_cols, normed_all, down_cols, *hops = scatter_tokens(
        partial.reshape(chips, length, model),
        sum_over(sums, "seq", 1, 2), out_cols, normed_all, down_cols, *hops,
    )
    out_cols = move_in_plane(out_cols[:own])
    norm_gain_term = jnp.sum(partial.astype(F32) * normed_all.astype(F32), axis=0) / norm_gain
    grad_normed, sums, blocks = tie(grad_normed, sum_over(sums, "seq", 2), blocks)
    total = scatter_end(hops, kept_out)
    block_output = (residual + total).astype(BF16).reshape(block_input.shape)
    sums, blocks = gather_small(sums), gather_small(blocks)

    def tiles_of(which):
        begins = range(which * tile, 2 * hidden_width, 2 * tile)
        return jnp.concatenate([grad_second_rows[:, at : at + tile] for at in begins], axis=1)

    grad_mgate_w, grad_mup_w = tiles_of(0).astype(F32), tiles_of(1).astype(F32)
    grad_first_w = lax.psum_scatter(grad_first_w, "seq", scatter_dimension=0, tiled=True)
    inv_one = lax.rsqrt(jnp.mean(tokens * tokens, axis=-1, keepdims=True) + EPSILON)
    grad_tokens, _ = norm_back(grad_normed, tokens, inv_one, norm_gain)
    input_grad = (grad_tokens + grad_residual).reshape(block_input.shape)
    grad_first_w, down_cols, out_cols, input_grad = tie(
        grad_first_w, down_cols, out_cols, input_grad
    )
    grad_down_w = move_across(down_cols).astype(F32)
    grad_out_w = move_across(out_cols).astype(F32)
    grad_in_w = grad_first_w[:, :own].astype(F32)
    grad_gate_w = grad_first_w[:, width : width + own].astype(F32)

    sums = jnp.swapaxes(natural_order(sums)[:, :, :own], 0, 1).reshape(-1, recur_width)
    decay_term = sums[2] * (8.0 * jax.nn.sigmoid(-decay_param))
    blocks = widen_blocks(blocks)
    gains = sum_over(sum_over(jnp.stack([norm_gain_term, mlp_gain_term]), "dp"), "seq")
    return (
        block_output,
        input_grad,
        gains[0],
        grad_in_w,
        grad_gate_w,
        sums[4:],
        sums[3],
        blocks[0],
        sums[0],
        blocks[1],
        sums[1],
        decay_term,
        grad_out_w,
        gains[1],
        grad_mgate_w,
        grad_mup_w,
        grad_down_w,
    )


def solution(mesh):
    rows = P(("dp", "seq"), None)
    acts = P("dp", "seq", None)
    grads = P("seq", "dp")
    return jax.shard_map(
        local,
        mesh=mesh,
        in_specs=(
            acts, P(), rows, rows, P(), P(), P(), P(), P(), P(), P(), rows, P(), rows, rows, rows,
            acts,
        ),
        out_specs=(
            acts, acts, P(), grads, grads, P(), P(), P(), P(), P(), P(), P(), grads, P(), grads,
            grads, grads,
        ),
        check_vma=False,
    )
```

```python
import jax
import jax.numpy as jnp
from jax import lax
from jax.experimental import pallas as pl
from jax.experimental.pallas import tpu as pltpu
from jax.sharding import PartitionSpec as P

EPSILON = 1e-06
F32 = jnp.float32
BF16 = jnp.bfloat16
GELU_C = 0.7978845608028654
GELU_A = 0.044715
CHUNK = 32
VMEM_LIMIT = 48 << 20


def tie(*values):
    return lax.optimization_barrier(values)


def xor_send(value, axis, offset):
    count = lax.axis_size(axis)
    return lax.ppermute(value, axis, [(i, i ^ offset) for i in range(count)])


def shift_send(value, axis, steps):
    count = lax.axis_size(axis)
    first, last = max(0, -steps), min(count, count - steps)
    return lax.ppermute(value, axis, [(i, i + steps) for i in range(first, last)])


def gather_tokens(piece, *beside):
    chips = lax.axis_size("dp") // 2
    if chips == 4:
        half = piece.shape[0] // 2
        via_x = xor_send(piece, "dp", 2)
        via_y = xor_send(piece, "dp", 4)
        via_x, via_y, *beside = tie(via_x, via_y, *beside)
        top = xor_send(via_y[:half], "dp", 2)
        bottom = xor_send(via_x[half:], "dp", 4)
        return jnp.concatenate([piece, via_x, via_y, top, bottom], axis=0), *beside
    slots = [piece] + [xor_send(piece, "dp", 2 * o) for o in range(1, chips)]
    return jnp.concatenate(slots, axis=0), *beside


def scatter_begin(partial):
    chips = lax.axis_size("dp") // 2
    if chips == 4:
        half = partial.shape[1] // 2
        via_x = xor_send(partial[3, :half], "dp", 2)
        via_y = xor_send(partial[3, half:], "dp", 4)
        x_top = xor_send(partial[1, :half], "dp", 2)
        y_bottom = xor_send(partial[2, half:], "dp", 4)
        return (via_x, via_y), (x_top, y_bottom, partial)
    return (), tuple(xor_send(partial[o], "dp", 2 * o) for o in range(1, chips)) + (partial,)


def scatter_middle(via, kept):
    if not via:
        return ()
    partial = kept[-1]
    half = partial.shape[1] // 2
    to_x = (partial[1, half:].astype(F32) + via[1].astype(F32)).astype(BF16)
    to_y = (partial[2, :half].astype(F32) + via[0].astype(F32)).astype(BF16)
    return to_x, to_y


def scatter_send(sums):
    return (xor_send(sums[0], "dp", 2), xor_send(sums[1], "dp", 4)) if sums else ()


def scatter_end(hops, kept):
    partial = kept[-1]
    mine = partial[0].astype(F32)
    if not hops:
        for moved in kept[:-1]:
            mine = mine + moved.astype(F32)
        return mine
    x_bottom, y_top = hops
    x_top, y_bottom, _ = kept
    half = partial.shape[1] // 2
    return jnp.concatenate(
        [
            mine[:half] + x_top.astype(F32) + y_top.astype(F32),
            mine[half:] + x_bottom.astype(F32) + y_bottom.astype(F32),
        ],
        axis=0,
    )


def scatter_tokens(partial, *beside):
    via, kept = scatter_begin(partial)
    if via:
        *via, = tie(*via, *beside)
        via, beside = via[:2], via[2:]
    hops = scatter_send(scatter_middle(via, kept))
    return scatter_end(hops, kept), *beside


def join_cores(own_half, other_half):
    moved = xor_send(other_half.astype(BF16), "dp", 1)
    return (own_half + moved.astype(F32)).astype(BF16)


def gather_small(value):
    count = lax.axis_size("dp")
    evens = [value] + [xor_send(value, "dp", o) for o in range(2, count, 2)]
    evens = jnp.stack(evens, axis=0)
    both = jnp.stack([evens, xor_send(evens, "dp", 1)], axis=1)
    return both.reshape((count,) + value.shape)


def natural_order(slots):
    count, mine = slots.shape[0], lax.axis_index("dp")
    step = 1
    while step < count:
        pairs = slots.reshape((-1, 2, step) + slots.shape[1:])
        swapped = jnp.concatenate([pairs[:, 1:], pairs[:, :1]], axis=1)
        slots = jnp.where((mine // step) % 2 == 1, swapped, pairs).reshape(slots.shape)
        step *= 2
    return slots


def widen_blocks_kernel(mine_ref, slot_ref, *out_refs):
    for kind, out_ref in enumerate(out_refs):
        out_ref[...] = slot_ref[0, kind].astype(F32)


def widen_blocks(slots):
    count, kinds, heads, rows, cols = slots.shape
    mine = lax.axis_index("dp").astype(jnp.int32).reshape(1)
    return pl.pallas_call(
        widen_blocks_kernel,
        out_shape=(jax.ShapeDtypeStruct((count * heads, rows, cols), F32),) * kinds,
        grid_spec=pltpu.PrefetchScalarGridSpec(
            num_scalar_prefetch=1,
            grid=(count,),
            in_specs=[
                pl.BlockSpec((1, kinds, heads, rows, cols), lambda d, m: (d ^ m[0], 0, 0, 0, 0))
            ],
            out_specs=(pl.BlockSpec((heads, rows, cols), lambda d, m: (d, 0, 0)),) * kinds,
        ),
        compiler_params=params(),
        name="widen_blocks",
    )(mine, slots)


def sum_over(value, axis, begin=1, end=None):
    offset = begin
    total = value
    while offset < (end or lax.axis_size(axis)):
        moved = xor_send(total, axis, offset)
        total = (total.astype(F32) + moved.astype(F32)).astype(value.dtype)
        offset *= 2
    return total


def carry_in(decay, state, steps):
    count = lax.axis_size("seq")
    both = jnp.stack([decay, state], axis=0)
    moved = [shift_send(both, "seq", steps * k) for k in range(1, count)]
    carried = moved[-1][1]
    for item in reversed(moved[:-1]):
        carried = item[1] + item[0] * carried
    return carried


def quarter_shift():
    dp_count, seq_count = lax.axis_size("dp"), lax.axis_size("seq")
    mine = lax.axis_index("dp")
    ratio = dp_count // seq_count
    return shift_of(mine, ratio, seq_count)


def shift_of(d, ratio, seq_count):
    group = d // ratio
    flip = (d % 2) * (seq_count - 1)
    return group ^ flip


def move_in_plane(block):
    dp_count, seq_count = lax.axis_size("dp"), lax.axis_size("seq")
    perm = []
    for d in range(dp_count):
        for s in range(seq_count):
            quarter = s ^ shift_of(d, dp_count // seq_count, seq_count)
            perm.append((d * seq_count + s, (2 * quarter + d % 2) * seq_count + s))
    return lax.ppermute(block, ("dp", "seq"), perm)


def move_across(block):
    dp_count, seq_count = lax.axis_size("dp"), lax.axis_size("seq")
    assert dp_count == 2 * seq_count
    perm = []
    for d in range(dp_count):
        for s in range(seq_count):
            perm.append((d * seq_count + s, d * seq_count + (s ^ shift_of(d, 2, seq_count))))
    block = lax.ppermute(block, ("dp", "seq"), perm)
    half = block.shape[1] // 2
    first_core = lax.axis_index("dp") % 2 == 0
    left, right = block[:, :half], block[:, half:]
    kept = jnp.where(first_core, left, right)
    moved = xor_send(jnp.where(first_core, right, left), "dp", 1)
    return jnp.concatenate(
        [jnp.where(first_core, kept, moved), jnp.where(first_core, moved, kept)], axis=0
    )


def scaled_norm(values, gain_vec):
    return (
        values * lax.rsqrt(jnp.mean(values * values, axis=-1, keepdims=True) + EPSILON) * gain_vec
    )


def gelu_pair(v):
    square = v * v
    t = jnp.tanh(GELU_C * (v + GELU_A * v * square))
    half = 0.5 * (1.0 + t)
    slope = half + 0.5 * v * (1.0 - t * t) * (GELU_C * (1.0 + 3.0 * GELU_A * square))
    return v * half, slope


def logistic(v):
    return 1.0 / (1.0 + jnp.exp(-v))


def one_minus_exp(x, exp_x):
    poly = jnp.full_like(x, 1.0 / 362880.0)
    for coef in (1 / 40320.0, 1 / 5040.0, 1 / 720.0, 1 / 120.0, 1 / 24.0, 1 / 6.0, 0.5, 1.0):
        poly = poly * x + coef
    return jnp.where(x > -0.35, -x * poly, 1.0 - exp_x)


def half_mask(chunk, slots, width):
    return lax.broadcasted_iota(jnp.int32, (chunk, slots, width), 1) < slots // 2


def join_slots(own_ref, other_ref):
    return jnp.concatenate([own_ref[...], other_ref[...]], axis=0)


def fwd_gates_kernel(
    own_ref, other_ref, prior_ref, taps_ref, vec_ref, w_ref,
    bt_ref, conv_ref, r_ref, i_ref, rate_ref, m_ref, loc_ref, run_ref,
    halo, state, decay,
):
    chunk, slots, width = bt_ref.shape

    @pl.when(pl.program_id(0) == 0)
    def _():
        halo[...] = prior_ref[...]
        state[...] = jnp.zeros_like(state)
        decay[...] = jnp.ones_like(decay)

    bt = jnp.swapaxes(join_slots(own_ref, other_ref), 0, 1)
    bt_ref[...] = bt
    lag = halo.shape[0]
    padded = jnp.concatenate([halo[...], bt], axis=0)
    halo[...] = padded[chunk : chunk + lag]
    conv = jnp.zeros_like(bt) + vec_ref[0]
    for k in range(lag + 1):
        conv = conv + taps_ref[k] * padded[lag - k : lag - k + chunk]
    conv_ref[...] = conv
    rows = conv.reshape(chunk * slots, width).astype(BF16)
    mask = half_mask(chunk, slots, width)

    def gate(which):
        own = jnp.dot(rows, w_ref[2 * which], preferred_element_type=F32)
        other = jnp.dot(rows, w_ref[2 * which + 1], preferred_element_type=F32)
        shape = (chunk, slots, width)
        pre = jnp.where(mask, own.reshape(shape), other.reshape(shape))
        return logistic(pre + vec_ref[1 + which])

    r, g = gate(0), gate(1)
    log_rate = r * vec_ref[3]
    rate = jnp.exp(log_rate)
    m = jnp.sqrt(one_minus_exp(2.0 * log_rate, rate * rate))
    r_ref[...] = r
    i_ref[...] = g
    rate_ref[...] = rate
    m_ref[...] = m
    driven = m * g * conv
    st, dc = state[...], decay[...]
    for t in range(chunk):
        st = rate[t] * st + driven[t]
        dc = rate[t] * dc
        loc_ref[t] = st
        run_ref[t] = dc
    state[...] = st
    decay[...] = dc


def fwd_mix_kernel(
    loc_ref, run_ref, carry_ref, gate_own_ref, gate_other_ref,
    mixed_ref, prev_ref, across_ref, last,
):
    chunk, slots, width = loc_ref.shape

    @pl.when(pl.program_id(0) == 0)
    def _():
        last[...] = carry_ref[...]

    states = loc_ref[...] + run_ref[...] * carry_ref[...]
    prev_ref[...] = jnp.concatenate([last[...][None], states[: chunk - 1]], axis=0)
    last[...] = states[chunk - 1]
    across = jnp.swapaxes(states, 0, 1)
    across_ref[...] = across
    half = slots // 2
    own, _ = gelu_pair(gate_own_ref[...])
    other, _ = gelu_pair(gate_other_ref[...])
    mixed_ref[:, :, :width] = (across[:half] * own).astype(BF16)
    mixed_ref[:, :, width:] = (across[half:] * other).astype(BF16)


def back_mix_kernel(
    gm_own_ref, gm_other_ref, gate_own_ref, gate_other_ref, across_ref, rate_ref,
    ggate_ref, gl_ref, tail_ref, end_ref, held, decay,
):
    chunk, slots, width = rate_ref.shape

    @pl.when(pl.program_id(0) == 0)
    def _():
        held[...] = jnp.zeros_like(held)
        decay[...] = jnp.ones_like(decay)

    half = slots // 2
    gm = join_slots(gm_own_ref, gm_other_ref)
    act, slope = gelu_pair(join_slots(gate_own_ref, gate_other_ref))
    ggate = (gm * across_ref[...] * slope).astype(BF16)
    ggate_ref[:, :, :width] = ggate[:half]
    ggate_ref[:, :, width:] = ggate[half:]
    gs = jnp.swapaxes(gm * act, 0, 1)
    rate = rate_ref[...]
    h, dc = held[...], decay[...]
    for t in reversed(range(chunk)):
        grad = gs[t] + h
        gl_ref[t] = grad
        tail_ref[t] = dc
        h = rate[t] * grad
        dc = rate[t] * dc
    held[...] = h
    decay[...] = dc
    end_ref[0] = dc
    end_ref[1] = h


def back_gates_kernel(
    gl_ref, tail_ref, rate_ref, m_ref, r_ref, i_ref, conv_ref, prev_ref, bt_ref,
    hin_ref, prior_ref, taps_ref, vec_ref, w_ref,
    gbranch_ref, last_ref, head_ref, dw_own_ref, dw_other_ref, total_ref,
    later, sums_ref, dw_ref,
):
    chunk, slots, width = rate_ref.shape
    lag = later.shape[0]
    step = pl.program_id(0)

    @pl.when(step == 0)
    def _():
        later[...] = jnp.zeros_like(later)
        dw_ref[...] = jnp.zeros_like(dw_ref)
        sums_ref[...] = jnp.zeros_like(sums_ref)

    s = gl_ref[...] + tail_ref[...] * hin_ref[...]
    rate, m, r, g, conv = rate_ref[...], m_ref[...], r_ref[...], i_ref[...], conv_ref[...]
    sc = s * conv
    dpi = (sc * m * (g * (1.0 - g))).astype(BF16).astype(F32)
    dlog = s * prev_ref[...] * rate - sc * g * (rate * rate) / m
    dpr = (dlog * vec_ref[3] * (r * (1.0 - r))).astype(BF16).astype(F32)
    sums_ref[2] += jnp.sum(dlog * r, axis=0)
    sums_ref[0] += jnp.sum(dpr, axis=0)
    sums_ref[1] += jnp.sum(dpi, axis=0)
    mask = half_mask(chunk, slots, width)
    flat = (chunk * slots, width)
    rows_own = jnp.where(mask, conv, 0.0).reshape(flat).astype(BF16)
    rows_other = jnp.where(mask, 0.0, conv).reshape(flat).astype(BF16)
    dpr = dpr.reshape(flat).astype(BF16)
    dpi = dpi.reshape(flat).astype(BF16)
    over_rows = (((0,), (0,)), ((), ()))
    over_cols = (((1,), (1,)), ((), ()))
    dw_ref[0] += lax.dot_general(rows_own, dpr, over_rows, preferred_element_type=F32)
    dw_ref[1] += lax.dot_general(rows_own, dpi, over_rows, preferred_element_type=F32)
    dw_ref[2] += lax.dot_general(rows_other, dpr, over_rows, preferred_element_type=F32)
    dw_ref[3] += lax.dot_general(rows_other, dpi, over_rows, preferred_element_type=F32)

    def through(which):
        part = lax.dot_general(dpr, w_ref[which], over_cols, preferred_element_type=F32)
        part += lax.dot_general(dpi, w_ref[2 + which], over_cols, preferred_element_type=F32)
        return part.reshape(chunk, slots, width)

    gconv = jnp.where(mask, through(0), through(1)) + s * m * g
    padded = jnp.concatenate([gconv, later[...]], axis=0)
    later[...] = gconv[:lag]
    head_ref[...] = gconv[:lag]
    sums_ref[3] += jnp.sum(gconv, axis=0)
    bt = bt_ref[...]
    gb = jnp.zeros_like(gconv)
    for k in range(lag + 1):
        shifted = padded[k : k + chunk]
        gb = gb + taps_ref[k] * shifted
        sums_ref[4 + k] += jnp.sum(bt * shifted, axis=0)

    @pl.when(step == 0)
    def _():
        last_ref[...] = gb[chunk - lag :]

    across = jnp.swapaxes(gb, 0, 1).astype(BF16)
    gbranch_ref[:, :, :width] = across[: slots // 2]
    gbranch_ref[:, :, width:] = across[slots // 2 :]

    @pl.when(step == pl.num_programs(0) - 1)
    def _():
        for k in range(1, lag + 1):
            for j in range(1, k + 1):
                sums_ref[4 + k] += prior_ref[lag - j] * gconv[k - j]
        half = slots // 2
        for kind in range(total_ref.shape[1]):
            total_ref[0, kind] = jnp.sum(sums_ref[kind, :half], axis=0)
            total_ref[1, kind] = jnp.sum(sums_ref[kind, half:], axis=0)
        heads, head = dw_own_ref.shape[1:3]
        for kind in range(2):
            for h in range(heads):
                for begin, ref in ((0, dw_own_ref), (2, dw_other_ref)):
                    rows = dw_ref[begin + kind, h * head : (h + 1) * head, :]
                    if h:
                        rows = pltpu.roll(rows, width - h * head, 1)
                    ref[kind, h] = rows[:, :head].astype(ref.dtype)


def specs_for(slots, length, width, backwards):
    count = length // CHUNK

    def at(c):
        return count - 1 - c if backwards else c

    time_major = pl.BlockSpec((CHUNK, slots, width), lambda c: (at(c), 0, 0))

    def columns(j, times=1, halves=2):
        return pl.BlockSpec((slots // halves, CHUNK, times * width), lambda c: (0, at(c), j))

    return count, time_major, columns


def whole(*shape):
    return pl.BlockSpec(shape, lambda c: (0,) * len(shape))


def params():
    return pltpu.CompilerParams(
        dimension_semantics=("arbitrary",), vmem_limit_bytes=VMEM_LIMIT
    )


def cost(flops, size, trans):
    return pl.CostEstimate(flops=flops, bytes_accessed=size, transcendentals=trans)


def fwd_gates(both, prior, taps, vecs, w):
    length = both.shape[1]
    lag, slots, width = prior.shape
    count, tm, cols = specs_for(slots, length, width, False)
    full = jax.ShapeDtypeStruct((length, slots, width), F32)
    n = slots * length * width
    return pl.pallas_call(
        fwd_gates_kernel,
        out_shape=(full,) * 8,
        grid=(count,),
        in_specs=[
            cols(0), cols(2), whole(*prior.shape), whole(*taps.shape), whole(*vecs.shape),
            whole(*w.shape),
        ],
        out_specs=(tm,) * 8,
        scratch_shapes=[
            pltpu.VMEM(prior.shape, F32),
            pltpu.VMEM((slots, width), F32),
            pltpu.VMEM((slots, width), F32),
        ],
        compiler_params=params(),
        cost_estimate=cost(n, 58 * n, n),
        name="gates_forward",
    )(both, both, prior, taps, vecs, w)


def fwd_mix(loc, run, carry, both):
    length, slots, width = loc.shape
    count, tm, cols = specs_for(slots, length, width, False)
    n = slots * length * width
    return pl.pallas_call(
        fwd_mix_kernel,
        out_shape=(
            jax.ShapeDtypeStruct((slots // 2, length, 2 * width), BF16),
            jax.ShapeDtypeStruct((length, slots, width), F32),
            jax.ShapeDtypeStruct((slots, length, width), F32),
        ),
        grid=(count,),
        in_specs=[tm, tm, whole(slots, width), cols(1), cols(3)],
        out_specs=(cols(0, 2), tm, cols(0, 1, 1)),
        scratch_shapes=[pltpu.VMEM((slots, width), F32)],
        compiler_params=params(),
        cost_estimate=cost(n, 36 * n, n),
        name="mix_forward",
    )(loc, run, carry, both, both)


def back_mix(gm, both, across, rate):
    length, slots, width = rate.shape
    count, tm, cols = specs_for(slots, length, width, True)
    n = slots * length * width
    return pl.pallas_call(
        back_mix_kernel,
        out_shape=(
            jax.ShapeDtypeStruct((slots // 2, length, 2 * width), BF16),
            jax.ShapeDtypeStruct((length, slots, width), F32),
            jax.ShapeDtypeStruct((length, slots, width), F32),
            jax.ShapeDtypeStruct((2, slots, width), F32),
        ),
        grid=(count,),
        in_specs=[cols(0), cols(1), cols(1), cols(3), cols(0, 1, 1), tm],
        out_specs=(cols(0, 2), tm, tm, whole(2, slots, width)),
        scratch_shapes=[pltpu.VMEM((slots, width), F32), pltpu.VMEM((slots, width), F32)],
        compiler_params=params(),
        cost_estimate=cost(n, 44 * n, n),
        name="mix_backward",
    )(gm, gm, both, both, across, rate)


def back_gates(kept, hin, prior, taps, vecs, w, heads, head):
    length, slots, width = kept[0].shape
    lag = prior.shape[0]
    count, tm, cols = specs_for(slots, length, width, True)
    n = slots * length * width
    return pl.pallas_call(
        back_gates_kernel,
        out_shape=(
            jax.ShapeDtypeStruct((slots // 2, length, 2 * width), BF16),
            jax.ShapeDtypeStruct((lag, slots, width), F32),
            jax.ShapeDtypeStruct((lag, slots, width), F32),
            jax.ShapeDtypeStruct((2, heads, head, head), F32),
            jax.ShapeDtypeStruct((2, heads, head, head), BF16),
            jax.ShapeDtypeStruct((2, 5 + lag, width), F32),
        ),
        grid=(count,),
        in_specs=[tm] * 9
        + [
            whole(slots, width), whole(*prior.shape), whole(*taps.shape), whole(*vecs.shape),
            whole(*w.shape),
        ],
        out_specs=(
            cols(0, 2), whole(lag, slots, width), whole(lag, slots, width),
            whole(2, heads, head, head), whole(2, heads, head, head), whole(2, 5 + lag, width),
        ),
        scratch_shapes=[
            pltpu.VMEM((lag, slots, width), F32),
            pltpu.VMEM((5 + lag, slots, width), F32),
            pltpu.VMEM(w.shape, F32),
        ],
        compiler_params=params(),
        cost_estimate=cost(n, 76 * n, n),
        name="gates_backward",
    )(*kept, hin, prior, taps, vecs, w)


def tile_of(hidden_width):
    return 256 if hidden_width % 256 == 0 else 128


def row_blocks(rows):
    step = 256 if rows % 256 == 0 else rows
    return [slice(at, at + step) for at in range(0, rows, step)]


def mlp_forward_kernel(x_ref, w_ref, hidden_ref, kept_ref):
    tile = hidden_ref.shape[1]
    weight = jnp.swapaxes(w_ref[...], 0, 1).reshape(x_ref.shape[1], 2 * tile)
    for rows in row_blocks(x_ref.shape[0]):
        ffn = jnp.dot(x_ref[rows, :], weight, preferred_element_type=F32)
        act, slope = gelu_pair(ffn[:, :tile])
        up = ffn[:, tile:]
        hidden_ref[rows, :] = (act * up).astype(BF16)
        kept_ref[rows, :tile] = (slope * up).astype(BF16)
        kept_ref[rows, tile:] = act.astype(BF16)


def mlp_forward(x, weight):
    rows, model = x.shape
    hidden_width = weight.shape[3] // 2
    tile = tile_of(hidden_width)
    return pl.pallas_call(
        mlp_forward_kernel,
        out_shape=(
            jax.ShapeDtypeStruct((rows, hidden_width), BF16),
            jax.ShapeDtypeStruct((rows, 2 * hidden_width), BF16),
        ),
        grid=(hidden_width // tile,),
        in_specs=[
            pl.BlockSpec((rows, model), lambda j: (0, 0), pipeline_mode=pl.Buffered(1)),
            pl.BlockSpec(weight.shape[:3] + (2 * tile,), lambda j: (0, 0, 0, j)),
        ],
        out_specs=(
            pl.BlockSpec((rows, tile), lambda j: (0, j)),
            pl.BlockSpec((rows, 2 * tile), lambda j: (0, j)),
        ),
        compiler_params=params(),
        cost_estimate=cost(7 * rows * hidden_width * model, rows * model, 0),
        name="mlp_forward",
    )(x, weight)


OVER_COLS = (((1,), (1,)), ((), ()))


def hidden_backward_kernel(g_ref, down0_ref, down1_ref, kept0_ref, kept1_ref, ffn0_ref, ffn1_ref):
    step = pl.program_id(0)
    tile = down0_ref.shape[0]

    def half(down_ref, kept_ref, ffn_ref):
        for rows in row_blocks(g_ref.shape[0]):
            grad = lax.dot_general(
                g_ref[rows, :], down_ref[...], OVER_COLS, preferred_element_type=F32
            )
            ffn_ref[rows, :tile] = (grad * kept_ref[rows, :tile].astype(F32)).astype(BF16)
            ffn_ref[rows, tile:] = (grad * kept_ref[rows, tile:].astype(F32)).astype(BF16)

    @pl.when(step < pl.num_programs(0) // 2)
    def _():
        half(down1_ref, kept1_ref, ffn1_ref)

    @pl.when(step >= pl.num_programs(0) // 2)
    def _():
        half(down0_ref, kept0_ref, ffn0_ref)


def hidden_backward(grad, down, kept):
    rows, model = grad.shape
    hidden_width = down[0].shape[0]
    tile = tile_of(hidden_width)
    half = hidden_width // tile

    def own(j):
        return jnp.maximum(j - half, 0)

    def other(j):
        return jnp.minimum(j, half - 1)

    full = jax.ShapeDtypeStruct((rows, 2 * hidden_width), BF16)
    return pl.pallas_call(
        hidden_backward_kernel,
        out_shape=(full, full),
        grid=(2 * half,),
        in_specs=[
            pl.BlockSpec((rows, model), lambda j: (0, 0), pipeline_mode=pl.Buffered(1)),
            pl.BlockSpec((tile, model), lambda j: (own(j), 0)),
            pl.BlockSpec((tile, model), lambda j: (other(j), 0)),
            pl.BlockSpec((rows, 2 * tile), lambda j: (0, own(j))),
            pl.BlockSpec((rows, 2 * tile), lambda j: (0, other(j))),
        ],
        out_specs=(
            pl.BlockSpec((rows, 2 * tile), lambda j: (0, own(j))),
            pl.BlockSpec((rows, 2 * tile), lambda j: (0, other(j))),
        ),
        compiler_params=params(),
        cost_estimate=cost(7 * rows * hidden_width * model, rows * model, 0),
        name="hidden_backward",
    )(grad, *down, *kept)


def normed_backward_kernel(ffn0_ref, ffn1_ref, w0_ref, w1_ref, out_ref):
    width = ffn0_ref.shape[1]
    for rows in row_blocks(ffn0_ref.shape[0]):
        total = None
        for ffn_ref, w_ref in ((ffn0_ref, w0_ref), (ffn1_ref, w1_ref)):
            part = lax.dot_general(
                ffn_ref[rows, :],
                w_ref[...].reshape(out_ref.shape[1], width),
                OVER_COLS,
                preferred_element_type=F32,
            )
            total = part if total is None else total + part
        out_ref[rows, :] = total.astype(BF16)


def normed_backward(ffn, weight):
    rows, width = ffn[0].shape
    seq_count, dp_count, shard, _ = weight[0].shape
    cols = seq_count * shard
    kept = pl.BlockSpec((rows, width), lambda j: (0, 0), pipeline_mode=pl.Buffered(1))
    block = pl.BlockSpec((seq_count, 1, shard, width), lambda j: (0, j, 0, 0))
    return pl.pallas_call(
        normed_backward_kernel,
        out_shape=jax.ShapeDtypeStruct((rows, cols * dp_count), BF16),
        grid=(dp_count,),
        in_specs=[kept, kept, block, block],
        out_specs=pl.BlockSpec((rows, cols), lambda j: (0, j)),
        compiler_params=params(),
        cost_estimate=cost(7 * rows * width * cols * dp_count, rows * width, 0),
        name="normed_backward",
    )(*ffn, *weight)


def unpack_down_kernel(packed_ref, out_ref):
    _, blocks, shard, lanes = packed_ref.shape
    part = out_ref.shape[1] // blocks
    for k in range(lanes // part):
        cols = slice(k * part, (k + 1) * part)
        for block in range(blocks):
            out_ref[k * shard : (k + 1) * shard, block * part : (block + 1) * part] = packed_ref[
                0, block, :, cols
            ]


def unpack_down(packed, first_column, rows):
    seq_count, dp_count, shard, _ = packed.shape
    lay = rows // (seq_count * shard)
    lanes = packed.shape[3] - first_column
    begin = first_column // lanes
    cols = dp_count * lanes // lay
    return pl.pallas_call(
        unpack_down_kernel,
        out_shape=jax.ShapeDtypeStruct((rows, cols), packed.dtype),
        grid=(seq_count,),
        in_specs=[pl.BlockSpec((1, dp_count, shard, lanes), lambda s: (s, 0, 0, begin))],
        out_specs=pl.BlockSpec((lay * shard, cols), lambda s: (s, 0)),
        compiler_params=params(),
        cost_estimate=cost(0, 4 * rows * cols, 0),
        name="unpack_down",
    )(packed)


def weight_kernel(left_ref, right_ref, *refs):
    out_ref = refs[-1]
    product = lax.dot_general(
        left_ref[...], right_ref[...], (((0,), (0,)), ((), ())), preferred_element_type=F32
    )
    if len(refs) == 2:
        product = product + refs[0][...].astype(F32)
    out_ref[...] = product.astype(BF16)


def mm_weight(left, right, *added):
    depth, rows = left.shape
    cols = right.shape[1]
    tile = 256 if rows % 256 == 0 else 128
    block = pl.BlockSpec((tile, cols), lambda i: (i, 0))
    return pl.pallas_call(
        weight_kernel,
        out_shape=jax.ShapeDtypeStruct((rows, cols), BF16),
        grid=(rows // tile,),
        in_specs=[
            pl.BlockSpec((depth, tile), lambda i: (0, i)),
            pl.BlockSpec((depth, cols), lambda i: (0, 0), pipeline_mode=pl.Buffered(1)),
        ]
        + [block] * len(added),
        out_specs=block,
        compiler_params=params(),
        cost_estimate=cost(3 * rows * cols * depth, rows * cols, 0),
        name="weight_gradient",
    )(left, right, *added)


def weight_rows_kernel(shift_ref, left_ref, right_ref, added_ref, out_ref):
    product = lax.dot_general(
        left_ref[...], right_ref[...], (((0,), (0,)), ((), ())), preferred_element_type=F32
    )
    product = (product + added_ref[...].astype(F32)).astype(BF16)
    count, _, cols = out_ref.shape
    for quarter in range(count):
        out_ref[quarter ^ shift_ref[0]] = product[:, quarter * cols : (quarter + 1) * cols]


def weight_rows(left, right, added):
    depth, rows = left.shape
    cols = right.shape[1]
    count = lax.axis_size("seq")
    tile = 128
    shift = quarter_shift().astype(jnp.int32).reshape(1)
    return pl.pallas_call(
        weight_rows_kernel,
        out_shape=jax.ShapeDtypeStruct((count, rows, cols // count), BF16),
        grid_spec=pltpu.PrefetchScalarGridSpec(
            num_scalar_prefetch=1,
            grid=(rows // tile,),
            in_specs=[
                pl.BlockSpec((depth, tile), lambda i, s: (0, i)),
                pl.BlockSpec((depth, cols), lambda i, s: (0, 0), pipeline_mode=pl.Buffered(1)),
                pl.BlockSpec((tile, cols), lambda i, s: (i, 0)),
            ],
            out_specs=pl.BlockSpec((count, tile, cols // count), lambda i, s: (0, i, 0)),
        ),
        compiler_params=params(),
        cost_estimate=cost(3 * rows * cols * depth, rows * cols, 0),
        name="weight_rows",
    )(shift, left, right, added)


def rows_of(value):
    return value.reshape(-1, value.shape[-1])


def mm(left, right):
    return jnp.dot(left, right, preferred_element_type=F32)


def mm_back(grad_rows, weight):
    return lax.dot_general(grad_rows, weight, (((1,), (1,)), ((), ())), preferred_element_type=F32)


def local(
    block_input, norm_gain, in_proj, gate_proj, conv_kernel, conv_bias,
    recur_weight, recur_bias, input_weight, input_bias, decay_param,
    out_proj, mlp_gain, mlp_gate, mlp_up, mlp_down, out_grad,
):
    dp_count, seq_count = lax.axis_size("dp"), lax.axis_size("seq")
    mine = lax.axis_index("dp")
    model = block_input.shape[2]
    tokens = block_input.reshape(-1, model).astype(F32)
    length = tokens.shape[0]
    recur_width = in_proj.shape[1]
    own = recur_width // dp_count
    width = -(-own // 128) * 128
    hidden_width = mlp_gate.shape[1] // dp_count
    head = recur_weight.shape[1]
    own_heads = own // head
    lag = conv_kernel.shape[0] - 1

    chips = dp_count // 2

    shard = in_proj.shape[0]

    def split_cols(weight, padded):
        part = jnp.swapaxes(weight.reshape(shard, dp_count, -1), 0, 1)
        return jnp.pad(part, ((0, 0), (0, 0), (0, padded - part.shape[2])))

    def spread(joined):
        return lax.all_to_all(joined, "dp", split_axis=0, concat_axis=0, tiled=True)

    def natural_rows(full):
        return full.transpose(1, 0, 2, 3).reshape(-1, full.shape[3])

    def partner(value):
        return xor_send(value, "dp", 1)

    w_out = lax.all_gather(out_proj, "seq", axis=0, tiled=True)
    first = jnp.concatenate([split_cols(in_proj, width), split_cols(gate_proj, width)], axis=2)
    first = spread(first)
    first = lax.all_gather(first, "seq", axis=0)
    def per_slot(value):
        rows = []
        for index in (mine, mine ^ 1):
            part = lax.dynamic_slice_in_dim(value, index * own, own, axis=value.ndim - 1)
            rows.append(jnp.pad(part, [(0, 0)] * (value.ndim - 1) + [(0, width - own)]))
        return jnp.repeat(jnp.stack(rows, axis=-2), chips, axis=-2)

    taps = per_slot(conv_kernel)
    vecs = per_slot(jnp.stack([conv_bias, recur_bias, input_bias, decay_param]))
    vecs = jnp.concatenate([vecs[:3], -8.0 * jax.nn.softplus(-vecs[3:])], axis=0)

    def block_diagonal(weight, index):
        part = lax.dynamic_slice_in_dim(weight, index * own_heads, own_heads, axis=0)
        rows = [
            jnp.pad(part[h], ((0, 0), (h * head, width - (h + 1) * head)))
            for h in range(own_heads)
        ]
        return jnp.pad(jnp.concatenate(rows, axis=0), ((0, width - own), (0, 0)))

    w_gates = jnp.stack(
        [block_diagonal(w, i) for w in (recur_weight, input_weight) for i in (mine, mine ^ 1)]
    )

    taps, vecs, w_gates = tie(taps, vecs, w_gates)

    normed = scaled_norm(tokens, norm_gain).astype(BF16)
    normed_all, w_out = gather_tokens(normed, w_out)
    w_out = jnp.pad(w_out, ((0, width - own), (0, 0)))
    w_out = jnp.concatenate([w_out, partner(w_out)], axis=0)
    tile = tile_of(hidden_width)

    def by_tile(weight):
        return weight.reshape(shard, dp_count, hidden_width // tile, tile)

    second = jnp.concatenate([by_tile(mlp_gate), by_tile(mlp_up)], axis=3)
    second = jnp.swapaxes(second.reshape(shard, dp_count, 2 * hidden_width), 0, 1)
    lay = mlp_down.shape[0] // shard
    part = model // dp_count
    down = mlp_down.reshape(lay, shard, dp_count, part).transpose(2, 1, 0, 3)
    down = down.reshape(dp_count, shard, lay * part)
    second, down, normed_all = tie(second, down, normed_all)
    grad_low, second, first = tie(out_grad.reshape(length, model), spread(second), first)
    second = lax.all_gather(jnp.concatenate([second, down], axis=2), "seq", axis=0)

    w_first = natural_rows(first)
    w_first = jnp.concatenate([w_first, partner(w_first)], axis=1)

    both = mm(normed_all, w_first)
    grad_all, both = gather_tokens(grad_low, both)
    both = both.reshape(chips, length, 4 * width)
    ends = both[:, length - lag :]
    ends = jnp.concatenate([ends[:, :, :width], ends[:, :, 2 * width : 3 * width]], axis=0)
    prior = shift_send(jnp.swapaxes(ends, 0, 1), "seq", 1)
    bt, conv, r, g, rate, m, loc, run = fwd_gates(both, prior, taps, vecs, w_gates)
    carry = carry_in(run[length - 1], loc[length - 1], 1)
    mixed, prev, across = fwd_mix(loc, run, carry, both)
    mixed = rows_of(mixed)
    partial, grad_all = tie(mm(mixed, w_out).astype(BF16), grad_all)
    (total,) = scatter_tokens(partial.reshape(chips, length, model))
    residual = tokens + total

    inv_two = lax.rsqrt(jnp.mean(residual * residual, axis=-1, keepdims=True) + EPSILON)
    normed_two = (residual * inv_two * mlp_gain).astype(BF16)
    (normed_two_all,) = gather_tokens(normed_two)
    normed_two_all, second = tie(normed_two_all, second)
    w_second = second[:, :, :, : 2 * hidden_width]
    w_second = (w_second, partner(w_second))
    w_down = unpack_down(second, 2 * hidden_width, hidden_width)
    w_down = (w_down, partner(w_down))
    hidden, kept = zip(*[mlp_forward(normed_two_all, weight) for weight in w_second])
    hidden = list(hidden)
    moved_down, grad_all = tie(mm_weight(hidden[1], grad_all), grad_all)
    moved_down = xor_send(moved_down, "dp", 1)
    grad_ffn = list(hidden_backward(grad_all, w_down, kept))
    moved = mm_weight(normed_two_all, grad_ffn[1])
    grad_down = weight_rows(hidden[0], grad_all, moved_down)
    grad_ffn[0], moved, grad_down = tie(grad_ffn[0], moved, grad_down)
    down_cols = lax.psum_scatter(grad_down, "seq", scatter_dimension=0, tiled=False)
    moved = xor_send(moved, "dp", 1)
    partial = normed_backward(grad_ffn, w_second)
    partial, grad_ffn[0], normed_two_all = tie(partial, grad_ffn[0], normed_two_all)
    grad_normed_two, moved, grad_ffn[0] = scatter_tokens(
        partial.reshape(chips, length, model), moved, grad_ffn[0]
    )
    grad_second = mm_weight(normed_two_all, grad_ffn[0], moved)
    grad_normed_two, grad_second = tie(grad_normed_two, grad_second)
    grad_second_rows = lax.psum_scatter(grad_second, "seq", scatter_dimension=0, tiled=True)

    def norm_back(grad, values, inv, gain):
        unit = values * inv
        scaled = grad * gain
        mean = jnp.mean(scaled * unit, axis=-1, keepdims=True)
        return inv * (scaled - unit * mean), unit

    grad_resid, unit_two = norm_back(grad_normed_two, residual, inv_two, mlp_gain)
    mlp_gain_term = jnp.sum(grad_normed_two * unit_two, axis=0)
    grad_residual = grad_resid + grad_low.astype(F32)

    grad_rec, hidden[0], hidden[1] = tie(grad_residual.astype(BF16), *hidden)
    out_partial = mm(hidden[0], w_down[0]) + mm(hidden[1], w_down[1])
    grad_rec_all, out_partial, down_cols = gather_tokens(
        grad_rec, out_partial.astype(BF16), down_cols
    )
    grad_rec_all, out_partial = tie(grad_rec_all, out_partial)
    via, kept_out = scatter_begin(out_partial.reshape(chips, length, model))
    gm = mm_back(grad_rec_all, w_out)
    gm = gm.reshape(chips, length, 2 * width)
    ggate, gl, tail, end = back_mix(gm, both, across, rate)
    hin = carry_in(end[0], end[1], -1)
    moved = mm_weight(mixed[:, width:], grad_rec_all)
    hin, moved, *out_sums = tie(hin, moved, *scatter_middle(via, kept_out))
    hops = scatter_send(out_sums)
    grad_out = weight_rows(mixed[:, :width], grad_rec_all, xor_send(moved, "dp", 1))
    hin, grad_out = tie(hin, grad_out)
    gbranch, last, head_rows, dw_own, dw_other, sums = back_gates(
        (gl, tail, rate, m, r, g, conv, prev, bt), hin, prior, taps, vecs, w_gates,
        own_heads, head,
    )
    later, down_cols = tie(shift_send(head_rows, "seq", -1), down_cols)
    down_cols = move_in_plane(down_cols)
    fixed = []
    for j in range(lag):
        row = last[j]
        for k in range(lag - j, lag + 1):
            row = row + taps[k] * later[j + k - lag]
        fixed.append(row)
    fixed = jnp.stack(fixed, axis=1).astype(BF16)
    fixed = jnp.concatenate([fixed[:chips], fixed[chips:]], axis=2)
    gbranch = lax.dynamic_update_slice(gbranch, fixed, (0, length - lag, 0))
    gbranch, ggate = rows_of(gbranch), rows_of(ggate)
    grad_first = jnp.concatenate(
        [gbranch[:, :width], ggate[:, :width], gbranch[:, width:], ggate[:, width:]], axis=1
    )
    moved = mm_weight(normed_all, grad_first[:, 2 * width :])
    blocks = (dw_own + xor_send(dw_other, "dp", 1).astype(F32)).astype(BF16)
    blocks = sum_over(blocks, "seq", 1, 2)
    grad_first, moved, grad_second_rows, blocks = tie(
        grad_first, moved, grad_second_rows, blocks
    )
    blocks = sum_over(blocks, "seq", 2)
    moved = xor_send(moved, "dp", 1)
    partial = mm_back(grad_first, w_first).astype(BF16)
    partial, normed_all, sums, blocks, grad_out = tie(
        partial, normed_all, sums, blocks, grad_out
    )
    out_cols = lax.psum_scatter(grad_out, "seq", scatter_dimension=0, tiled=False)
    grad_first_w = mm_weight(normed_all, grad_first[:, : 2 * width], moved)
    sums = sums[0] + xor_send(sums[1], "dp", 1)
    partial, grad_first_w = tie(partial, grad_first_w)
    grad_normed, sums, normed_all, down_cols, *hops = scatter_tokens(
        partial.reshape(chips, length, model),
        sum_over(sums, "seq", 1, 2), normed_all, down_cols, *hops,
    )
    grad_first_w, out_cols = tie(grad_first_w, out_cols)
    out_cols = move_in_plane(out_cols[:own])
    norm_gain_term = jnp.sum(partial.astype(F32) * normed_all.astype(F32), axis=0) / norm_gain
    grad_normed, sums, blocks = tie(grad_normed, sum_over(sums, "seq", 2), blocks)
    total = scatter_end(hops, kept_out)
    block_output = (residual + total).astype(BF16).reshape(block_input.shape)
    sums, blocks = gather_small(sums), gather_small(blocks)

    def tiles_of(which):
        begins = range(which * tile, 2 * hidden_width, 2 * tile)
        return jnp.concatenate([grad_second_rows[:, at : at + tile] for at in begins], axis=1)

    grad_mgate_w, grad_mup_w = tiles_of(0).astype(F32), tiles_of(1).astype(F32)
    grad_first_w = lax.psum_scatter(grad_first_w, "seq", scatter_dimension=0, tiled=True)
    inv_one = lax.rsqrt(jnp.mean(tokens * tokens, axis=-1, keepdims=True) + EPSILON)
    grad_tokens, _ = norm_back(grad_normed, tokens, inv_one, norm_gain)
    input_grad = (grad_tokens + grad_residual).reshape(block_input.shape)
    grad_first_w, down_cols, out_cols, input_grad = tie(
        grad_first_w, down_cols, out_cols, input_grad
    )
    grad_down_w = move_across(down_cols).astype(F32)
    grad_out_w = move_across(out_cols).astype(F32)
    grad_in_w = grad_first_w[:, :own].astype(F32)
    grad_gate_w = grad_first_w[:, width : width + own].astype(F32)

    sums = jnp.swapaxes(natural_order(sums)[:, :, :own], 0, 1).reshape(-1, recur_width)
    decay_term = sums[2] * (8.0 * jax.nn.sigmoid(-decay_param))
    blocks = widen_blocks(blocks)
    gains = sum_over(sum_over(jnp.stack([norm_gain_term, mlp_gain_term]), "dp"), "seq")
    return (
        block_output,
        input_grad,
        gains[0],
        grad_in_w,
        grad_gate_w,
        sums[4:],
        sums[3],
        blocks[0],
        sums[0],
        blocks[1],
        sums[1],
        decay_term,
        grad_out_w,
        gains[1],
        grad_mgate_w,
        grad_mup_w,
        grad_down_w,
    )


def solution(mesh):
    rows = P(("dp", "seq"), None)
    acts = P("dp", "seq", None)
    grads = P("seq", "dp")
    return jax.shard_map(
        local,
        mesh=mesh,
        in_specs=(
            acts, P(), rows, rows, P(), P(), P(), P(), P(), P(), P(), rows, P(), rows, rows, rows,
            acts,
        ),
        out_specs=(
            acts, acts, P(), grads, grads, P(), P(), P(), P(), P(), P(), P(), grads, P(), grads,
            grads, grads,
        ),
        check_vma=False,
    )
```

```python
import jax
import jax.numpy as jnp
from jax import lax
from jax.experimental import pallas as pl
from jax.experimental.pallas import tpu as pltpu
from jax.sharding import PartitionSpec as P

EPSILON = 1e-06
F32 = jnp.float32
BF16 = jnp.bfloat16
GELU_C = 0.7978845608028654
GELU_A = 0.044715
CHUNK = 32
VMEM_LIMIT = 48 << 20


def tie(*values):
    return lax.optimization_barrier(values)


def xor_send(value, axis, offset):
    count = lax.axis_size(axis)
    return lax.ppermute(value, axis, [(i, i ^ offset) for i in range(count)])


def shift_send(value, axis, steps):
    count = lax.axis_size(axis)
    first, last = max(0, -steps), min(count, count - steps)
    return lax.ppermute(value, axis, [(i, i + steps) for i in range(first, last)])


def gather_tokens(piece, *beside):
    chips = lax.axis_size("dp") // 2
    if chips == 4:
        half = piece.shape[0] // 2
        via_x = xor_send(piece, "dp", 2)
        via_y = xor_send(piece, "dp", 4)
        via_x, via_y, *beside = tie(via_x, via_y, *beside)
        top = xor_send(via_y[:half], "dp", 2)
        bottom = xor_send(via_x[half:], "dp", 4)
        return jnp.concatenate([piece, via_x, via_y, top, bottom], axis=0), *beside
    slots = [piece] + [xor_send(piece, "dp", 2 * o) for o in range(1, chips)]
    return jnp.concatenate(slots, axis=0), *beside


def scatter_begin(partial):
    chips = lax.axis_size("dp") // 2
    if chips == 4:
        half = partial.shape[1] // 2
        via_x = xor_send(partial[3, :half], "dp", 2)
        via_y = xor_send(partial[3, half:], "dp", 4)
        x_top = xor_send(partial[1, :half], "dp", 2)
        y_bottom = xor_send(partial[2, half:], "dp", 4)
        return (via_x, via_y), (x_top, y_bottom, partial)
    return (), tuple(xor_send(partial[o], "dp", 2 * o) for o in range(1, chips)) + (partial,)


def scatter_middle(via, kept):
    if not via:
        return ()
    partial = kept[-1]
    half = partial.shape[1] // 2
    to_x = (partial[1, half:].astype(F32) + via[1].astype(F32)).astype(BF16)
    to_y = (partial[2, :half].astype(F32) + via[0].astype(F32)).astype(BF16)
    return to_x, to_y


def scatter_send(sums):
    return (xor_send(sums[0], "dp", 2), xor_send(sums[1], "dp", 4)) if sums else ()


def scatter_end(hops, kept):
    partial = kept[-1]
    mine = partial[0].astype(F32)
    if not hops:
        for moved in kept[:-1]:
            mine = mine + moved.astype(F32)
        return mine
    x_bottom, y_top = hops
    x_top, y_bottom, _ = kept
    half = partial.shape[1] // 2
    return jnp.concatenate(
        [
            mine[:half] + x_top.astype(F32) + y_top.astype(F32),
            mine[half:] + x_bottom.astype(F32) + y_bottom.astype(F32),
        ],
        axis=0,
    )


def scatter_tokens(partial, *beside):
    via, kept = scatter_begin(partial)
    if via:
        *via, = tie(*via, *beside)
        via, beside = via[:2], via[2:]
    hops = scatter_send(scatter_middle(via, kept))
    return scatter_end(hops, kept), *beside


def join_cores(own_half, other_half):
    moved = xor_send(other_half.astype(BF16), "dp", 1)
    return (own_half + moved.astype(F32)).astype(BF16)


def gather_small(value):
    count = lax.axis_size("dp")
    evens = [value] + [xor_send(value, "dp", o) for o in range(2, count, 2)]
    evens = jnp.stack(evens, axis=0)
    both = jnp.stack([evens, xor_send(evens, "dp", 1)], axis=1)
    return both.reshape((count,) + value.shape)


def natural_order(slots):
    count, mine = slots.shape[0], lax.axis_index("dp")
    step = 1
    while step < count:
        pairs = slots.reshape((-1, 2, step) + slots.shape[1:])
        swapped = jnp.concatenate([pairs[:, 1:], pairs[:, :1]], axis=1)
        slots = jnp.where((mine // step) % 2 == 1, swapped, pairs).reshape(slots.shape)
        step *= 2
    return slots


def widen_blocks_kernel(mine_ref, slot_ref, *out_refs):
    for kind, out_ref in enumerate(out_refs):
        out_ref[...] = slot_ref[0, kind].astype(F32)


def widen_blocks(slots):
    count, kinds, heads, rows, cols = slots.shape
    mine = lax.axis_index("dp").astype(jnp.int32).reshape(1)
    return pl.pallas_call(
        widen_blocks_kernel,
        out_shape=(jax.ShapeDtypeStruct((count * heads, rows, cols), F32),) * kinds,
        grid_spec=pltpu.PrefetchScalarGridSpec(
            num_scalar_prefetch=1,
            grid=(count,),
            in_specs=[
                pl.BlockSpec((1, kinds, heads, rows, cols), lambda d, m: (d ^ m[0], 0, 0, 0, 0))
            ],
            out_specs=(pl.BlockSpec((heads, rows, cols), lambda d, m: (d, 0, 0)),) * kinds,
        ),
        compiler_params=params(),
        name="widen_blocks",
    )(mine, slots)


def sum_over(value, axis, begin=1, end=None):
    offset = begin
    total = value
    while offset < (end or lax.axis_size(axis)):
        moved = xor_send(total, axis, offset)
        total = (total.astype(F32) + moved.astype(F32)).astype(value.dtype)
        offset *= 2
    return total


def carry_in(decay, state, steps):
    count = lax.axis_size("seq")
    both = jnp.stack([decay, state], axis=0)
    moved = [shift_send(both, "seq", steps * k) for k in range(1, count)]
    carried = moved[-1][1]
    for item in reversed(moved[:-1]):
        carried = item[1] + item[0] * carried
    return carried


def quarter_shift():
    dp_count, seq_count = lax.axis_size("dp"), lax.axis_size("seq")
    mine = lax.axis_index("dp")
    ratio = dp_count // seq_count
    return shift_of(mine, ratio, seq_count)


def shift_of(d, ratio, seq_count):
    group = d // ratio
    flip = (d % 2) * (seq_count - 1)
    return group ^ flip


def move_in_plane(block):
    dp_count, seq_count = lax.axis_size("dp"), lax.axis_size("seq")
    perm = []
    for d in range(dp_count):
        for s in range(seq_count):
            quarter = s ^ shift_of(d, dp_count // seq_count, seq_count)
            perm.append((d * seq_count + s, (2 * quarter + d % 2) * seq_count + s))
    return lax.ppermute(block, ("dp", "seq"), perm)


def move_across(block, *beside):
    dp_count, seq_count = lax.axis_size("dp"), lax.axis_size("seq")
    assert dp_count == 2 * seq_count
    perm = []
    for d in range(dp_count):
        for s in range(seq_count):
            perm.append((d * seq_count + s, d * seq_count + (s ^ shift_of(d, 2, seq_count))))
    block, *beside = tie(lax.ppermute(block, ("dp", "seq"), perm), *beside)
    half = block.shape[1] // 2
    first_core = lax.axis_index("dp") % 2 == 0
    left, right = block[:, :half], block[:, half:]
    kept = jnp.where(first_core, left, right)
    moved = xor_send(jnp.where(first_core, right, left), "dp", 1)
    rows = jnp.where(first_core, kept, moved), jnp.where(first_core, moved, kept)
    return rows, *beside


def scaled_norm(values, gain_vec):
    return (
        values * lax.rsqrt(jnp.mean(values * values, axis=-1, keepdims=True) + EPSILON) * gain_vec
    )


def gelu_pair(v):
    square = v * v
    t = jnp.tanh(GELU_C * (v + GELU_A * v * square))
    half = 0.5 * (1.0 + t)
    slope = half + 0.5 * v * (1.0 - t * t) * (GELU_C * (1.0 + 3.0 * GELU_A * square))
    return v * half, slope


def logistic(v):
    return 1.0 / (1.0 + jnp.exp(-v))


def one_minus_exp(x, exp_x):
    poly = jnp.full_like(x, 1.0 / 362880.0)
    for coef in (1 / 40320.0, 1 / 5040.0, 1 / 720.0, 1 / 120.0, 1 / 24.0, 1 / 6.0, 0.5, 1.0):
        poly = poly * x + coef
    return jnp.where(x > -0.35, -x * poly, 1.0 - exp_x)


def half_mask(chunk, slots, width):
    return lax.broadcasted_iota(jnp.int32, (chunk, slots, width), 1) < slots // 2


def join_slots(own_ref, other_ref):
    return jnp.concatenate([own_ref[...], other_ref[...]], axis=0)


def fwd_gates_kernel(
    own_ref, other_ref, prior_ref, taps_ref, vec_ref, w_ref,
    bt_ref, conv_ref, r_ref, i_ref, rate_ref, m_ref, loc_ref, run_ref,
    halo, state, decay,
):
    chunk, slots, width = bt_ref.shape

    @pl.when(pl.program_id(0) == 0)
    def _():
        halo[...] = prior_ref[...]
        state[...] = jnp.zeros_like(state)
        decay[...] = jnp.ones_like(decay)

    bt = jnp.swapaxes(join_slots(own_ref, other_ref), 0, 1)
    bt_ref[...] = bt
    lag = halo.shape[0]
    padded = jnp.concatenate([halo[...], bt], axis=0)
    halo[...] = padded[chunk : chunk + lag]
    conv = jnp.zeros_like(bt) + vec_ref[0]
    for k in range(lag + 1):
        conv = conv + taps_ref[k] * padded[lag - k : lag - k + chunk]
    conv_ref[...] = conv
    rows = conv.reshape(chunk * slots, width).astype(BF16)
    mask = half_mask(chunk, slots, width)

    def gate(which):
        own = jnp.dot(rows, w_ref[2 * which], preferred_element_type=F32)
        other = jnp.dot(rows, w_ref[2 * which + 1], preferred_element_type=F32)
        shape = (chunk, slots, width)
        pre = jnp.where(mask, own.reshape(shape), other.reshape(shape))
        return logistic(pre + vec_ref[1 + which])

    r, g = gate(0), gate(1)
    log_rate = r * vec_ref[3]
    rate = jnp.exp(log_rate)
    m = jnp.sqrt(one_minus_exp(2.0 * log_rate, rate * rate))
    r_ref[...] = r
    i_ref[...] = g
    rate_ref[...] = rate
    m_ref[...] = m
    driven = m * g * conv
    st, dc = state[...], decay[...]
    for t in range(chunk):
        st = rate[t] * st + driven[t]
        dc = rate[t] * dc
        loc_ref[t] = st
        run_ref[t] = dc
    state[...] = st
    decay[...] = dc


def fwd_mix_kernel(
    loc_ref, run_ref, carry_ref, gate_own_ref, gate_other_ref,
    mixed_ref, prev_ref, across_ref, last,
):
    chunk, slots, width = loc_ref.shape

    @pl.when(pl.program_id(0) == 0)
    def _():
        last[...] = carry_ref[...]

    states = loc_ref[...] + run_ref[...] * carry_ref[...]
    prev_ref[...] = jnp.concatenate([last[...][None], states[: chunk - 1]], axis=0)
    last[...] = states[chunk - 1]
    across = jnp.swapaxes(states, 0, 1)
    across_ref[...] = across
    half = slots // 2
    own, _ = gelu_pair(gate_own_ref[...])
    other, _ = gelu_pair(gate_other_ref[...])
    mixed_ref[:, :, :width] = (across[:half] * own).astype(BF16)
    mixed_ref[:, :, width:] = (across[half:] * other).astype(BF16)


def back_mix_kernel(
    gm_own_ref, gm_other_ref, gate_own_ref, gate_other_ref, across_ref, rate_ref,
    ggate_ref, gl_ref, tail_ref, end_ref, held, decay,
):
    chunk, slots, width = rate_ref.shape

    @pl.when(pl.program_id(0) == 0)
    def _():
        held[...] = jnp.zeros_like(held)
        decay[...] = jnp.ones_like(decay)

    half = slots // 2
    gm = join_slots(gm_own_ref, gm_other_ref)
    act, slope = gelu_pair(join_slots(gate_own_ref, gate_other_ref))
    ggate = (gm * across_ref[...] * slope).astype(BF16)
    ggate_ref[:, :, :width] = ggate[:half]
    ggate_ref[:, :, width:] = ggate[half:]
    gs = jnp.swapaxes(gm * act, 0, 1)
    rate = rate_ref[...]
    h, dc = held[...], decay[...]
    for t in reversed(range(chunk)):
        grad = gs[t] + h
        gl_ref[t] = grad
        tail_ref[t] = dc
        h = rate[t] * grad
        dc = rate[t] * dc
    held[...] = h
    decay[...] = dc
    end_ref[0] = dc
    end_ref[1] = h


def back_gates_kernel(
    gl_ref, tail_ref, rate_ref, m_ref, r_ref, i_ref, conv_ref, prev_ref, bt_ref,
    hin_ref, prior_ref, taps_ref, vec_ref, w_ref,
    gbranch_ref, last_ref, head_ref, dw_own_ref, dw_other_ref, total_ref,
    later, sums_ref, dw_ref,
):
    chunk, slots, width = rate_ref.shape
    lag = later.shape[0]
    step = pl.program_id(0)

    @pl.when(step == 0)
    def _():
        later[...] = jnp.zeros_like(later)
        dw_ref[...] = jnp.zeros_like(dw_ref)
        sums_ref[...] = jnp.zeros_like(sums_ref)

    s = gl_ref[...] + tail_ref[...] * hin_ref[...]
    rate, m, r, g, conv = rate_ref[...], m_ref[...], r_ref[...], i_ref[...], conv_ref[...]
    sc = s * conv
    dpi = (sc * m * (g * (1.0 - g))).astype(BF16).astype(F32)
    dlog = s * prev_ref[...] * rate - sc * g * (rate * rate) / m
    dpr = (dlog * vec_ref[3] * (r * (1.0 - r))).astype(BF16).astype(F32)
    sums_ref[2] += jnp.sum(dlog * r, axis=0)
    sums_ref[0] += jnp.sum(dpr, axis=0)
    sums_ref[1] += jnp.sum(dpi, axis=0)
    mask = half_mask(chunk, slots, width)
    flat = (chunk * slots, width)
    rows_own = jnp.where(mask, conv, 0.0).reshape(flat).astype(BF16)
    rows_other = jnp.where(mask, 0.0, conv).reshape(flat).astype(BF16)
    dpr = dpr.reshape(flat).astype(BF16)
    dpi = dpi.reshape(flat).astype(BF16)
    over_rows = (((0,), (0,)), ((), ()))
    over_cols = (((1,), (1,)), ((), ()))
    dw_ref[0] += lax.dot_general(rows_own, dpr, over_rows, preferred_element_type=F32)
    dw_ref[1] += lax.dot_general(rows_own, dpi, over_rows, preferred_element_type=F32)
    dw_ref[2] += lax.dot_general(rows_other, dpr, over_rows, preferred_element_type=F32)
    dw_ref[3] += lax.dot_general(rows_other, dpi, over_rows, preferred_element_type=F32)

    def through(which):
        part = lax.dot_general(dpr, w_ref[which], over_cols, preferred_element_type=F32)
        part += lax.dot_general(dpi, w_ref[2 + which], over_cols, preferred_element_type=F32)
        return part.reshape(chunk, slots, width)

    gconv = jnp.where(mask, through(0), through(1)) + s * m * g
    padded = jnp.concatenate([gconv, later[...]], axis=0)
    later[...] = gconv[:lag]
    head_ref[...] = gconv[:lag]
    sums_ref[3] += jnp.sum(gconv, axis=0)
    bt = bt_ref[...]
    gb = jnp.zeros_like(gconv)
    for k in range(lag + 1):
        shifted = padded[k : k + chunk]
        gb = gb + taps_ref[k] * shifted
        sums_ref[4 + k] += jnp.sum(bt * shifted, axis=0)

    @pl.when(step == 0)
    def _():
        last_ref[...] = gb[chunk - lag :]

    across = jnp.swapaxes(gb, 0, 1).astype(BF16)
    gbranch_ref[:, :, :width] = across[: slots // 2]
    gbranch_ref[:, :, width:] = across[slots // 2 :]

    @pl.when(step == pl.num_programs(0) - 1)
    def _():
        for k in range(1, lag + 1):
            for j in range(1, k + 1):
                sums_ref[4 + k] += prior_ref[lag - j] * gconv[k - j]
        half = slots // 2
        for kind in range(total_ref.shape[1]):
            total_ref[0, kind] = jnp.sum(sums_ref[kind, :half], axis=0)
            total_ref[1, kind] = jnp.sum(sums_ref[kind, half:], axis=0)
        heads, head = dw_own_ref.shape[1:3]
        for kind in range(2):
            for h in range(heads):
                for begin, ref in ((0, dw_own_ref), (2, dw_other_ref)):
                    rows = dw_ref[begin + kind, h * head : (h + 1) * head, :]
                    if h:
                        rows = pltpu.roll(rows, width - h * head, 1)
                    ref[kind, h] = rows[:, :head].astype(ref.dtype)


def specs_for(slots, length, width, backwards):
    count = length // CHUNK

    def at(c):
        return count - 1 - c if backwards else c

    time_major = pl.BlockSpec((CHUNK, slots, width), lambda c: (at(c), 0, 0))

    def columns(j, times=1, halves=2):
        return pl.BlockSpec((slots // halves, CHUNK, times * width), lambda c: (0, at(c), j))

    return count, time_major, columns


def whole(*shape):
    return pl.BlockSpec(shape, lambda c: (0,) * len(shape))


def params():
    return pltpu.CompilerParams(
        dimension_semantics=("arbitrary",), vmem_limit_bytes=VMEM_LIMIT
    )


def cost(flops, size, trans):
    return pl.CostEstimate(flops=flops, bytes_accessed=size, transcendentals=trans)


def fwd_gates(both, prior, taps, vecs, w):
    length = both.shape[1]
    lag, slots, width = prior.shape
    count, tm, cols = specs_for(slots, length, width, False)
    full = jax.ShapeDtypeStruct((length, slots, width), F32)
    n = slots * length * width
    return pl.pallas_call(
        fwd_gates_kernel,
        out_shape=(full,) * 8,
        grid=(count,),
        in_specs=[
            cols(0), cols(2), whole(*prior.shape), whole(*taps.shape), whole(*vecs.shape),
            whole(*w.shape),
        ],
        out_specs=(tm,) * 8,
        scratch_shapes=[
            pltpu.VMEM(prior.shape, F32),
            pltpu.VMEM((slots, width), F32),
            pltpu.VMEM((slots, width), F32),
        ],
        compiler_params=params(),
        cost_estimate=cost(n, 58 * n, n),
        name="gates_forward",
    )(both, both, prior, taps, vecs, w)


def fwd_mix(loc, run, carry, both):
    length, slots, width = loc.shape
    count, tm, cols = specs_for(slots, length, width, False)
    n = slots * length * width
    return pl.pallas_call(
        fwd_mix_kernel,
        out_shape=(
            jax.ShapeDtypeStruct((slots // 2, length, 2 * width), BF16),
            jax.ShapeDtypeStruct((length, slots, width), F32),
            jax.ShapeDtypeStruct((slots, length, width), F32),
        ),
        grid=(count,),
        in_specs=[tm, tm, whole(slots, width), cols(1), cols(3)],
        out_specs=(cols(0, 2), tm, cols(0, 1, 1)),
        scratch_shapes=[pltpu.VMEM((slots, width), F32)],
        compiler_params=params(),
        cost_estimate=cost(n, 36 * n, n),
        name="mix_forward",
    )(loc, run, carry, both, both)


def back_mix(gm, both, across, rate):
    length, slots, width = rate.shape
    count, tm, cols = specs_for(slots, length, width, True)
    n = slots * length * width
    return pl.pallas_call(
        back_mix_kernel,
        out_shape=(
            jax.ShapeDtypeStruct((slots // 2, length, 2 * width), BF16),
            jax.ShapeDtypeStruct((length, slots, width), F32),
            jax.ShapeDtypeStruct((length, slots, width), F32),
            jax.ShapeDtypeStruct((2, slots, width), F32),
        ),
        grid=(count,),
        in_specs=[cols(0), cols(1), cols(1), cols(3), cols(0, 1, 1), tm],
        out_specs=(cols(0, 2), tm, tm, whole(2, slots, width)),
        scratch_shapes=[pltpu.VMEM((slots, width), F32), pltpu.VMEM((slots, width), F32)],
        compiler_params=params(),
        cost_estimate=cost(n, 44 * n, n),
        name="mix_backward",
    )(gm, gm, both, both, across, rate)


def back_gates(kept, hin, prior, taps, vecs, w, heads, head):
    length, slots, width = kept[0].shape
    lag = prior.shape[0]
    count, tm, cols = specs_for(slots, length, width, True)
    n = slots * length * width
    return pl.pallas_call(
        back_gates_kernel,
        out_shape=(
            jax.ShapeDtypeStruct((slots // 2, length, 2 * width), BF16),
            jax.ShapeDtypeStruct((lag, slots, width), F32),
            jax.ShapeDtypeStruct((lag, slots, width), F32),
            jax.ShapeDtypeStruct((2, heads, head, head), F32),
            jax.ShapeDtypeStruct((2, heads, head, head), BF16),
            jax.ShapeDtypeStruct((2, 5 + lag, width), F32),
        ),
        grid=(count,),
        in_specs=[tm] * 9
        + [
            whole(slots, width), whole(*prior.shape), whole(*taps.shape), whole(*vecs.shape),
            whole(*w.shape),
        ],
        out_specs=(
            cols(0, 2), whole(lag, slots, width), whole(lag, slots, width),
            whole(2, heads, head, head), whole(2, heads, head, head), whole(2, 5 + lag, width),
        ),
        scratch_shapes=[
            pltpu.VMEM((lag, slots, width), F32),
            pltpu.VMEM((5 + lag, slots, width), F32),
            pltpu.VMEM(w.shape, F32),
        ],
        compiler_params=params(),
        cost_estimate=cost(n, 76 * n, n),
        name="gates_backward",
    )(*kept, hin, prior, taps, vecs, w)


def tile_of(hidden_width):
    return 256 if hidden_width % 256 == 0 else 128


def row_blocks(rows):
    step = 256 if rows % 256 == 0 else rows
    return [slice(at, at + step) for at in range(0, rows, step)]


def mlp_forward_kernel(x_ref, w_ref, hidden_ref, kept_ref):
    tile = hidden_ref.shape[1]
    weight = jnp.swapaxes(w_ref[...], 0, 1).reshape(x_ref.shape[1], 2 * tile)
    for rows in row_blocks(x_ref.shape[0]):
        ffn = jnp.dot(x_ref[rows, :], weight, preferred_element_type=F32)
        act, slope = gelu_pair(ffn[:, :tile])
        up = ffn[:, tile:]
        hidden_ref[rows, :] = (act * up).astype(BF16)
        kept_ref[rows, :tile] = (slope * up).astype(BF16)
        kept_ref[rows, tile:] = act.astype(BF16)


def mlp_forward(x, weight):
    rows, model = x.shape
    hidden_width = weight.shape[3] // 2
    tile = tile_of(hidden_width)
    return pl.pallas_call(
        mlp_forward_kernel,
        out_shape=(
            jax.ShapeDtypeStruct((rows, hidden_width), BF16),
            jax.ShapeDtypeStruct((rows, 2 * hidden_width), BF16),
        ),
        grid=(hidden_width // tile,),
        in_specs=[
            pl.BlockSpec((rows, model), lambda j: (0, 0), pipeline_mode=pl.Buffered(1)),
            pl.BlockSpec(weight.shape[:3] + (2 * tile,), lambda j: (0, 0, 0, j)),
        ],
        out_specs=(
            pl.BlockSpec((rows, tile), lambda j: (0, j)),
            pl.BlockSpec((rows, 2 * tile), lambda j: (0, j)),
        ),
        compiler_params=params(),
        cost_estimate=cost(7 * rows * hidden_width * model, rows * model, 0),
        name="mlp_forward",
    )(x, weight)


OVER_COLS = (((1,), (1,)), ((), ()))


def hidden_backward_kernel(g_ref, down0_ref, down1_ref, kept0_ref, kept1_ref, ffn0_ref, ffn1_ref):
    step = pl.program_id(0)
    tile = down0_ref.shape[0]

    def half(down_ref, kept_ref, ffn_ref):
        for rows in row_blocks(g_ref.shape[0]):
            grad = lax.dot_general(
                g_ref[rows, :], down_ref[...], OVER_COLS, preferred_element_type=F32
            )
            ffn_ref[rows, :tile] = (grad * kept_ref[rows, :tile].astype(F32)).astype(BF16)
            ffn_ref[rows, tile:] = (grad * kept_ref[rows, tile:].astype(F32)).astype(BF16)

    @pl.when(step < pl.num_programs(0) // 2)
    def _():
        half(down1_ref, kept1_ref, ffn1_ref)

    @pl.when(step >= pl.num_programs(0) // 2)
    def _():
        half(down0_ref, kept0_ref, ffn0_ref)


def hidden_backward(grad, down, kept):
    rows, model = grad.shape
    hidden_width = down[0].shape[0]
    tile = tile_of(hidden_width)
    half = hidden_width // tile

    def own(j):
        return jnp.maximum(j - half, 0)

    def other(j):
        return jnp.minimum(j, half - 1)

    full = jax.ShapeDtypeStruct((rows, 2 * hidden_width), BF16)
    return pl.pallas_call(
        hidden_backward_kernel,
        out_shape=(full, full),
        grid=(2 * half,),
        in_specs=[
            pl.BlockSpec((rows, model), lambda j: (0, 0), pipeline_mode=pl.Buffered(1)),
            pl.BlockSpec((tile, model), lambda j: (own(j), 0)),
            pl.BlockSpec((tile, model), lambda j: (other(j), 0)),
            pl.BlockSpec((rows, 2 * tile), lambda j: (0, own(j))),
            pl.BlockSpec((rows, 2 * tile), lambda j: (0, other(j))),
        ],
        out_specs=(
            pl.BlockSpec((rows, 2 * tile), lambda j: (0, own(j))),
            pl.BlockSpec((rows, 2 * tile), lambda j: (0, other(j))),
        ),
        compiler_params=params(),
        cost_estimate=cost(7 * rows * hidden_width * model, rows * model, 0),
        name="hidden_backward",
    )(grad, *down, *kept)


def normed_backward_kernel(ffn0_ref, ffn1_ref, w0_ref, w1_ref, out_ref):
    width = ffn0_ref.shape[1]
    for rows in row_blocks(ffn0_ref.shape[0]):
        total = None
        for ffn_ref, w_ref in ((ffn0_ref, w0_ref), (ffn1_ref, w1_ref)):
            part = lax.dot_general(
                ffn_ref[rows, :],
                w_ref[...].reshape(out_ref.shape[1], width),
                OVER_COLS,
                preferred_element_type=F32,
            )
            total = part if total is None else total + part
        out_ref[rows, :] = total.astype(BF16)


def normed_backward(ffn, weight):
    rows, width = ffn[0].shape
    seq_count, dp_count, shard, _ = weight[0].shape
    cols = seq_count * shard
    kept = pl.BlockSpec((rows, width), lambda j: (0, 0), pipeline_mode=pl.Buffered(1))
    block = pl.BlockSpec((seq_count, 1, shard, width), lambda j: (0, j, 0, 0))
    return pl.pallas_call(
        normed_backward_kernel,
        out_shape=jax.ShapeDtypeStruct((rows, cols * dp_count), BF16),
        grid=(dp_count,),
        in_specs=[kept, kept, block, block],
        out_specs=pl.BlockSpec((rows, cols), lambda j: (0, j)),
        compiler_params=params(),
        cost_estimate=cost(7 * rows * width * cols * dp_count, rows * width, 0),
        name="normed_backward",
    )(*ffn, *weight)


def unpack_down_kernel(packed_ref, out_ref):
    _, blocks, shard, lanes = packed_ref.shape
    part = out_ref.shape[1] // blocks
    for k in range(lanes // part):
        cols = slice(k * part, (k + 1) * part)
        for block in range(blocks):
            out_ref[k * shard : (k + 1) * shard, block * part : (block + 1) * part] = packed_ref[
                0, block, :, cols
            ]


def unpack_down(packed, first_column, rows):
    seq_count, dp_count, shard, _ = packed.shape
    lay = rows // (seq_count * shard)
    lanes = packed.shape[3] - first_column
    begin = first_column // lanes
    cols = dp_count * lanes // lay
    return pl.pallas_call(
        unpack_down_kernel,
        out_shape=jax.ShapeDtypeStruct((rows, cols), packed.dtype),
        grid=(seq_count,),
        in_specs=[pl.BlockSpec((1, dp_count, shard, lanes), lambda s: (s, 0, 0, begin))],
        out_specs=pl.BlockSpec((lay * shard, cols), lambda s: (s, 0)),
        compiler_params=params(),
        cost_estimate=cost(0, 4 * rows * cols, 0),
        name="unpack_down",
    )(packed)


def weight_kernel(left_ref, right_ref, *refs):
    out_ref = refs[-1]
    product = lax.dot_general(
        left_ref[...], right_ref[...], (((0,), (0,)), ((), ())), preferred_element_type=F32
    )
    if len(refs) == 2:
        product = product + refs[0][...].astype(F32)
    out_ref[...] = product.astype(BF16)


def mm_weight(left, right, *added):
    depth, rows = left.shape
    cols = right.shape[1]
    tile = 256 if rows % 256 == 0 else 128
    block = pl.BlockSpec((tile, cols), lambda i: (i, 0))
    return pl.pallas_call(
        weight_kernel,
        out_shape=jax.ShapeDtypeStruct((rows, cols), BF16),
        grid=(rows // tile,),
        in_specs=[
            pl.BlockSpec((depth, tile), lambda i: (0, i)),
            pl.BlockSpec((depth, cols), lambda i: (0, 0), pipeline_mode=pl.Buffered(1)),
        ]
        + [block] * len(added),
        out_specs=block,
        compiler_params=params(),
        cost_estimate=cost(3 * rows * cols * depth, rows * cols, 0),
        name="weight_gradient",
    )(left, right, *added)


def weight_rows_kernel(shift_ref, left_ref, right_ref, added_ref, out_ref):
    product = lax.dot_general(
        left_ref[...], right_ref[...], (((0,), (0,)), ((), ())), preferred_element_type=F32
    )
    product = (product + added_ref[...].astype(F32)).astype(BF16)
    count, _, cols = out_ref.shape
    for quarter in range(count):
        out_ref[quarter ^ shift_ref[0]] = product[:, quarter * cols : (quarter + 1) * cols]


def weight_rows(left, right, added):
    depth, rows = left.shape
    cols = right.shape[1]
    count = lax.axis_size("seq")
    tile = 128
    shift = quarter_shift().astype(jnp.int32).reshape(1)
    return pl.pallas_call(
        weight_rows_kernel,
        out_shape=jax.ShapeDtypeStruct((count, rows, cols // count), BF16),
        grid_spec=pltpu.PrefetchScalarGridSpec(
            num_scalar_prefetch=1,
            grid=(rows // tile,),
            in_specs=[
                pl.BlockSpec((depth, tile), lambda i, s: (0, i)),
                pl.BlockSpec((depth, cols), lambda i, s: (0, 0), pipeline_mode=pl.Buffered(1)),
                pl.BlockSpec((tile, cols), lambda i, s: (i, 0)),
            ],
            out_specs=pl.BlockSpec((count, tile, cols // count), lambda i, s: (0, i, 0)),
        ),
        compiler_params=params(),
        cost_estimate=cost(3 * rows * cols * depth, rows * cols, 0),
        name="weight_rows",
    )(shift, left, right, added)


def rows_of(value):
    return value.reshape(-1, value.shape[-1])


def mm(left, right):
    return jnp.dot(left, right, preferred_element_type=F32)


def mm_back(grad_rows, weight):
    return lax.dot_general(grad_rows, weight, (((1,), (1,)), ((), ())), preferred_element_type=F32)


def local(
    block_input, norm_gain, in_proj, gate_proj, conv_kernel, conv_bias,
    recur_weight, recur_bias, input_weight, input_bias, decay_param,
    out_proj, mlp_gain, mlp_gate, mlp_up, mlp_down, out_grad,
):
    dp_count, seq_count = lax.axis_size("dp"), lax.axis_size("seq")
    mine = lax.axis_index("dp")
    model = block_input.shape[2]
    tokens = block_input.reshape(-1, model).astype(F32)
    length = tokens.shape[0]
    recur_width = in_proj.shape[1]
    own = recur_width // dp_count
    width = -(-own // 128) * 128
    hidden_width = mlp_gate.shape[1] // dp_count
    head = recur_weight.shape[1]
    own_heads = own // head
    lag = conv_kernel.shape[0] - 1

    chips = dp_count // 2

    shard = in_proj.shape[0]

    def split_cols(weight, padded):
        part = jnp.swapaxes(weight.reshape(shard, dp_count, -1), 0, 1)
        return jnp.pad(part, ((0, 0), (0, 0), (0, padded - part.shape[2])))

    def spread(joined):
        return lax.all_to_all(joined, "dp", split_axis=0, concat_axis=0, tiled=True)

    def natural_rows(full):
        return full.transpose(1, 0, 2, 3).reshape(-1, full.shape[3])

    def partner(value):
        return xor_send(value, "dp", 1)

    w_out = lax.all_gather(out_proj, "seq", axis=0, tiled=True)
    first = jnp.concatenate([split_cols(in_proj, width), split_cols(gate_proj, width)], axis=2)
    first = spread(first)
    first = lax.all_gather(first, "seq", axis=0)
    def per_slot(value):
        rows = []
        for index in (mine, mine ^ 1):
            part = lax.dynamic_slice_in_dim(value, index * own, own, axis=value.ndim - 1)
            rows.append(jnp.pad(part, [(0, 0)] * (value.ndim - 1) + [(0, width - own)]))
        return jnp.repeat(jnp.stack(rows, axis=-2), chips, axis=-2)

    taps = per_slot(conv_kernel)
    vecs = per_slot(jnp.stack([conv_bias, recur_bias, input_bias, decay_param]))
    vecs = jnp.concatenate([vecs[:3], -8.0 * jax.nn.softplus(-vecs[3:])], axis=0)

    def block_diagonal(weight, index):
        part = lax.dynamic_slice_in_dim(weight, index * own_heads, own_heads, axis=0)
        rows = [
            jnp.pad(part[h], ((0, 0), (h * head, width - (h + 1) * head)))
            for h in range(own_heads)
        ]
        return jnp.pad(jnp.concatenate(rows, axis=0), ((0, width - own), (0, 0)))

    w_gates = jnp.stack(
        [block_diagonal(w, i) for w in (recur_weight, input_weight) for i in (mine, mine ^ 1)]
    )

    taps, vecs, w_gates = tie(taps, vecs, w_gates)

    normed = scaled_norm(tokens, norm_gain).astype(BF16)
    normed_all, w_out = gather_tokens(normed, w_out)
    w_out = jnp.pad(w_out, ((0, width - own), (0, 0)))
    w_out = jnp.concatenate([w_out, partner(w_out)], axis=0)
    tile = tile_of(hidden_width)

    def by_tile(weight):
        return weight.reshape(shard, dp_count, hidden_width // tile, tile)

    second = jnp.concatenate([by_tile(mlp_gate), by_tile(mlp_up)], axis=3)
    second = jnp.swapaxes(second.reshape(shard, dp_count, 2 * hidden_width), 0, 1)
    lay = mlp_down.shape[0] // shard
    part = model // dp_count
    down = mlp_down.reshape(lay, shard, dp_count, part).transpose(2, 1, 0, 3)
    down = down.reshape(dp_count, shard, lay * part)
    second, down, normed_all = tie(second, down, normed_all)
    grad_low, second, first = tie(out_grad.reshape(length, model), spread(second), first)
    second = lax.all_gather(jnp.concatenate([second, down], axis=2), "seq", axis=0)

    w_first = natural_rows(first)
    w_first = jnp.concatenate([w_first, partner(w_first)], axis=1)

    both = mm(normed_all, w_first)
    grad_all, both = gather_tokens(grad_low, both)
    both = both.reshape(chips, length, 4 * width)
    ends = both[:, length - lag :]
    ends = jnp.concatenate([ends[:, :, :width], ends[:, :, 2 * width : 3 * width]], axis=0)
    prior = shift_send(jnp.swapaxes(ends, 0, 1), "seq", 1)
    bt, conv, r, g, rate, m, loc, run = fwd_gates(both, prior, taps, vecs, w_gates)
    carry = carry_in(run[length - 1], loc[length - 1], 1)
    mixed, prev, across = fwd_mix(loc, run, carry, both)
    mixed = rows_of(mixed)
    partial, grad_all = tie(mm(mixed, w_out).astype(BF16), grad_all)
    (total,) = scatter_tokens(partial.reshape(chips, length, model))
    residual = tokens + total

    inv_two = lax.rsqrt(jnp.mean(residual * residual, axis=-1, keepdims=True) + EPSILON)
    normed_two = (residual * inv_two * mlp_gain).astype(BF16)
    (normed_two_all,) = gather_tokens(normed_two)
    normed_two_all, second = tie(normed_two_all, second)
    w_second = second[:, :, :, : 2 * hidden_width]
    w_second = (w_second, partner(w_second))
    w_down = unpack_down(second, 2 * hidden_width, hidden_width)
    w_down = (w_down, partner(w_down))
    hidden, kept = zip(*[mlp_forward(normed_two_all, weight) for weight in w_second])
    hidden = list(hidden)
    moved_down, grad_all = tie(mm_weight(hidden[1], grad_all), grad_all)
    moved_down = xor_send(moved_down, "dp", 1)
    grad_ffn = list(hidden_backward(grad_all, w_down, kept))
    moved = mm_weight(normed_two_all, grad_ffn[1])
    grad_down = weight_rows(hidden[0], grad_all, moved_down)
    grad_ffn[0], moved, grad_down = tie(grad_ffn[0], moved, grad_down)
    down_cols = lax.psum_scatter(grad_down, "seq", scatter_dimension=0, tiled=False)
    moved = xor_send(moved, "dp", 1)
    partial = normed_backward(grad_ffn, w_second)
    partial, grad_ffn[0], normed_two_all = tie(partial, grad_ffn[0], normed_two_all)
    grad_normed_two, moved, grad_ffn[0] = scatter_tokens(
        partial.reshape(chips, length, model), moved, grad_ffn[0]
    )
    grad_second = mm_weight(normed_two_all, grad_ffn[0], moved)
    grad_normed_two, grad_second = tie(grad_normed_two, grad_second)
    grad_second_rows = lax.psum_scatter(grad_second, "seq", scatter_dimension=0, tiled=True)

    def norm_back(grad, values, inv, gain):
        unit = values * inv
        scaled = grad * gain
        mean = jnp.mean(scaled * unit, axis=-1, keepdims=True)
        return inv * (scaled - unit * mean), unit

    grad_resid, unit_two = norm_back(grad_normed_two, residual, inv_two, mlp_gain)
    mlp_gain_term = jnp.sum(grad_normed_two * unit_two, axis=0)
    grad_residual = grad_resid + grad_low.astype(F32)

    grad_rec, hidden[0], hidden[1] = tie(grad_residual.astype(BF16), *hidden)
    out_partial = mm(hidden[0], w_down[0]) + mm(hidden[1], w_down[1])
    grad_rec_all, out_partial, down_cols = gather_tokens(
        grad_rec, out_partial.astype(BF16), down_cols
    )
    grad_rec_all, out_partial = tie(grad_rec_all, out_partial)
    via, kept_out = scatter_begin(out_partial.reshape(chips, length, model))
    gm = mm_back(grad_rec_all, w_out)
    gm = gm.reshape(chips, length, 2 * width)
    ggate, gl, tail, end = back_mix(gm, both, across, rate)
    hin = carry_in(end[0], end[1], -1)
    moved = mm_weight(mixed[:, width:], grad_rec_all)
    hin, moved, *out_sums = tie(hin, moved, *scatter_middle(via, kept_out))
    hops = scatter_send(out_sums)
    grad_out = weight_rows(mixed[:, :width], grad_rec_all, xor_send(moved, "dp", 1))
    hin, grad_out = tie(hin, grad_out)
    gbranch, last, head_rows, dw_own, dw_other, sums = back_gates(
        (gl, tail, rate, m, r, g, conv, prev, bt), hin, prior, taps, vecs, w_gates,
        own_heads, head,
    )
    later, down_cols = tie(shift_send(head_rows, "seq", -1), down_cols)
    down_cols = move_in_plane(down_cols)
    fixed = []
    for j in range(lag):
        row = last[j]
        for k in range(lag - j, lag + 1):
            row = row + taps[k] * later[j + k - lag]
        fixed.append(row)
    fixed = jnp.stack(fixed, axis=1).astype(BF16)
    fixed = jnp.concatenate([fixed[:chips], fixed[chips:]], axis=2)
    gbranch = lax.dynamic_update_slice(gbranch, fixed, (0, length - lag, 0))
    gbranch, ggate = rows_of(gbranch), rows_of(ggate)
    grad_first = jnp.concatenate(
        [gbranch[:, :width], ggate[:, :width], gbranch[:, width:], ggate[:, width:]], axis=1
    )
    moved = mm_weight(normed_all, grad_first[:, 2 * width :])
    blocks = (dw_own + xor_send(dw_other, "dp", 1).astype(F32)).astype(BF16)
    blocks = sum_over(blocks, "seq", 1, 2)
    grad_first, moved, grad_second_rows, blocks = tie(
        grad_first, moved, grad_second_rows, blocks
    )
    blocks = sum_over(blocks, "seq", 2)
    moved = xor_send(moved, "dp", 1)
    partial = mm_back(grad_first, w_first).astype(BF16)
    partial, normed_all, sums, blocks, grad_out = tie(
        partial, normed_all, sums, blocks, grad_out
    )
    out_cols = lax.psum_scatter(grad_out, "seq", scatter_dimension=0, tiled=False)
    grad_first_w = mm_weight(normed_all, grad_first[:, : 2 * width], moved)
    sums = sums[0] + xor_send(sums[1], "dp", 1)
    partial, grad_first_w = tie(partial, grad_first_w)
    grad_normed, sums, normed_all, down_cols, *hops = scatter_tokens(
        partial.reshape(chips, length, model),
        sum_over(sums, "seq", 1, 2), normed_all, down_cols, *hops,
    )
    grad_first_w, out_cols = tie(grad_first_w, out_cols)
    out_cols = move_in_plane(out_cols[:own])
    norm_gain_term = jnp.sum(partial.astype(F32) * normed_all.astype(F32), axis=0) / norm_gain
    grad_normed, sums, blocks = tie(grad_normed, sum_over(sums, "seq", 2), blocks)
    total = scatter_end(hops, kept_out)
    block_output = (residual + total).astype(BF16).reshape(block_input.shape)
    sums, blocks = gather_small(sums), gather_small(blocks)

    def tiles_of(which):
        begins = range(which * tile, 2 * hidden_width, 2 * tile)
        return jnp.concatenate([grad_second_rows[:, at : at + tile] for at in begins], axis=1)

    grad_mgate_w, grad_mup_w = tiles_of(0).astype(F32), tiles_of(1).astype(F32)
    grad_first_w = lax.psum_scatter(grad_first_w, "seq", scatter_dimension=0, tiled=True)
    inv_one = lax.rsqrt(jnp.mean(tokens * tokens, axis=-1, keepdims=True) + EPSILON)
    grad_tokens, _ = norm_back(grad_normed, tokens, inv_one, norm_gain)
    input_grad = (grad_tokens + grad_residual).reshape(block_input.shape)
    grad_first_w, placed_rows, input_grad = tie(
        grad_first_w, jnp.concatenate([down_cols, out_cols], axis=0), input_grad
    )
    grad_in_w = grad_first_w[:, :own].astype(F32)
    grad_gate_w = grad_first_w[:, width : width + own].astype(F32)

    sums = jnp.swapaxes(natural_order(sums)[:, :, :own], 0, 1).reshape(-1, recur_width)
    decay_term = sums[2] * (8.0 * jax.nn.sigmoid(-decay_param))
    blocks = widen_blocks(blocks)
    gains = sum_over(sum_over(jnp.stack([norm_gain_term, mlp_gain_term]), "dp"), "seq")
    blocks_of_rows, gains, sums, grad_in_w, grad_gate_w, *blocks = move_across(
        placed_rows, gains, sums, grad_in_w, grad_gate_w, *blocks
    )
    grad_down_w = jnp.concatenate([part[:hidden_width] for part in blocks_of_rows]).astype(F32)
    grad_out_w = jnp.concatenate([part[hidden_width:] for part in blocks_of_rows]).astype(F32)
    return (
        block_output,
        input_grad,
        gains[0],
        grad_in_w,
        grad_gate_w,
        sums[4:],
        sums[3],
        blocks[0],
        sums[0],
        blocks[1],
        sums[1],
        decay_term,
        grad_out_w,
        gains[1],
        grad_mgate_w,
        grad_mup_w,
        grad_down_w,
    )


def solution(mesh):
    rows = P(("dp", "seq"), None)
    acts = P("dp", "seq", None)
    grads = P("seq", "dp")
    return jax.shard_map(
        local,
        mesh=mesh,
        in_specs=(
            acts, P(), rows, rows, P(), P(), P(), P(), P(), P(), P(), rows, P(), rows, rows, rows,
            acts,
        ),
        out_specs=(
            acts, acts, P(), grads, grads, P(), P(), P(), P(), P(), P(), P(), grads, P(), grads,
            grads, grads,
        ),
        check_vma=False,
    )
```
